256 devices in a mesh: rows: 32 (over z, y), samp: 8 (over x, core).
Axes of the slice: x: 4, y: 4, z: 8, core: 2. Of those that a mesh axis runs over, the one named last changes fastest.
Arguments:
- coupling_tiles: bfloat16 [512, 32, 128, 128], P('rows', 'samp'), may hold values from -0.09375 to 0.09375
- tile_columns: int32 [512, 32], P('rows', 'samp'), may hold values from 0 to 511, as said below
- sample_matrix: bfloat16 [65536, 512], P('rows'), may hold values from -6 to 6
- phi_leaf: float32 [512, 256], replicated, may hold values from -0.25 to 0.25
- phi_pair: float32 [512, 256], replicated, may hold values from -0.25 to 0.25
- phi_quad: float32 [512, 256], replicated, may hold values from -0.25 to 0.25
Outputs:
- leaf_basis: float32 [65536, 256], P('rows')
- nested_transfer: float32 [8192, 256], P('rows')
- sample_approx: float32 [65536, 512], P('rows', 'samp')
The draws below stay inside these ranges and needn't reach their ends.
Inputs may be any that keep to these rules, and one draw needn't show every extreme that they name: `tile_columns`: the 32 tile columns of a tile row are distinct and lie in the leaf block of that row or in one of the two leaf blocks beside it (16 tile rows to a leaf block).
All inputs are finite; a program needn't handle non-finite values.
Results may differ from the reference program's by a relative error of at most 0.0003.
Values may be sent and summed in bfloat16 or wider, within the bound.
A program may use at most 128 MiB of HBM per device.

```python
import jax
import jax.numpy as jnp
from jax import lax

LEAF = 2048
S = 512
R0 = 256
R1 = 256
R2 = 256
NS_ITERS = 5
TB = 128
NZ = 32
TROWS = 512
ORDER = 65536
N_ROWS = 32


def draw_tile_columns(key, part):
    tile_rows = jnp.arange(TROWS, dtype=jnp.int32)
    leaf_index = tile_rows // 16
    offsets = jnp.arange(48, dtype=jnp.int32)
    candidates = (leaf_index[:, None] - 1) * 16 + offsets[None, :]
    valid = (candidates >= 0) & (candidates < TROWS)
    scores = jax.random.randint(key, (TROWS, 48), 0, 1 << 20, dtype=jnp.int32) * 64 + offsets[None, :]
    scores = jnp.where(valid, scores, (1 << 27) + offsets[None, :])
    order = jnp.argsort(scores, axis=1, stable=True)[:, :NZ]
    return jnp.take_along_axis(candidates, order, axis=1).astype(jnp.int32)


def levels(stream_key, shape, cuts, least, top_value):
    gain = 1.0
    for dim, shards_of in cuts:
        draws = jax.random.uniform(jax.random.fold_in(jax.random.fold_in(stream_key, 6), dim), (shards_of,), jnp.float32, least / len(cuts), top_value / len(cuts))
        gain = gain * jnp.repeat(jnp.exp(draws), shape[dim] // shards_of).reshape((-1,) + (1,) * (len(shape) - 1 - dim))
    return gain


def bell_draw(rng, shape, deviation, bound, pieces=(), held_as=jnp.bfloat16):
    drawn = deviation * jax.random.normal(rng, shape, jnp.float32)
    if pieces:
        drawn = drawn * levels(rng, shape, pieces, -0.22, 0.18)
    return jnp.clip(drawn, -bound, bound).astype(held_as)


def setup_inputs(seed: int = 0) -> dict:
    keys = jax.random.split(jax.random.key(seed), 7)
    coupling_tiles = bell_draw(keys[0], (TROWS, NZ, TB, TB), (NZ * TB) ** -0.5, 0.09375, ((0, 32), (1, 8)))
    tile_columns = draw_tile_columns(jax.random.fold_in(keys[6], 71), 0)
    sample_matrix = bell_draw(keys[2], (ORDER, S), 1.0, 6.0, ((0, 32),))
    phi_leaf = bell_draw(keys[3], (S, R0), S ** -0.5, 0.25, (), jnp.float32)
    phi_pair = bell_draw(keys[4], (S, R1), S ** -0.5, 0.25, (), jnp.float32)
    phi_quad = bell_draw(keys[5], (S, R2), S ** -0.5, 0.25, (), jnp.float32)
    return dict(coupling_tiles=coupling_tiles, tile_columns=tile_columns, sample_matrix=sample_matrix, phi_leaf=phi_leaf, phi_pair=phi_pair, phi_quad=phi_quad)


HIGH = lax.Precision.HIGHEST

def orthogonal(matrix):
    gram_matrix = jnp.einsum('bmi,bmj->bij', matrix, matrix, precision=HIGH)
    norm_scale = jnp.sqrt(lax.optimization_barrier(jnp.sum(gram_matrix * gram_matrix, axis=(1, 2)))) + 1e-06
    norm_scale = norm_scale[:, None, None]
    identity = jnp.eye(gram_matrix.shape[1], dtype=jnp.float32)[None]
    iterate = gram_matrix / norm_scale
    inverse_root = jnp.broadcast_to(identity, gram_matrix.shape)
    for step in range(NS_ITERS):
        factor = 1.5 * identity - 0.5 * jnp.einsum('bij,bjk->bik', inverse_root, iterate, precision=HIGH)
        iterate = jnp.einsum('bij,bjk->bik', iterate, factor, precision=HIGH)
        inverse_root = jnp.einsum('bij,bjk->bik', factor, inverse_root, precision=HIGH)
    return jnp.einsum('bmi,bij->bmj', matrix, inverse_root, precision=HIGH) / jnp.sqrt(norm_scale)

def merge_level(stacked, sketch):
    sketched = jnp.einsum('bms,sr->bmr', stacked, sketch, precision=HIGH)
    basis_now = orthogonal(sketched)
    return (basis_now, jnp.einsum('bmr,bms->brs', basis_now, stacked, precision=HIGH))

def reference(coupling_tiles, tile_columns, sample_matrix, phi_leaf, phi_pair, phi_quad):
    blocks = sample_matrix.reshape(TROWS, TB, S)

    def row_product(operands):
        row_tiles, columns = operands
        picked = jnp.take(blocks, columns, axis=0)
        return jnp.einsum('kab,kbs->as', row_tiles.astype(jnp.float32), picked.astype(jnp.float32), precision=HIGH)
    sample = lax.map(row_product, (coupling_tiles, tile_columns)).reshape(N_ROWS, LEAF, S)
    basis, coarse = merge_level(sample, phi_leaf)
    upper, middle = merge_level(coarse.reshape(N_ROWS // 2, 2 * R0, S), phi_pair)
    top, summary = merge_level(middle.reshape(N_ROWS // 4, 2 * R1, S), phi_quad)
    own_upper = upper.reshape(N_ROWS, R0, R1)
    own_top = jnp.repeat(top.reshape(N_ROWS // 2, R1, R2), 2, axis=0)
    nested = jnp.einsum('nij,njk->nik', own_upper, own_top, precision=HIGH)
    leaf_summary = jnp.repeat(summary, 4, axis=0)
    inner = jnp.einsum('nrk,nks->nrs', nested, leaf_summary, precision=HIGH)
    approx = jnp.einsum('nlr,nrs->nls', basis, inner, precision=HIGH)
    return (basis.reshape(ORDER, R0), nested.reshape(N_ROWS * R0, R2), approx.reshape(ORDER, S))
```

```python
import functools

import jax
import jax.numpy as jnp
from jax import lax
from jax.experimental import pallas as pl
from jax.experimental.pallas import tpu as pltpu
from jax.sharding import PartitionSpec as P

NS_ITERS = 5
MESH = pl.DeviceIdType.MESH
F32 = jnp.float32
BF16 = jnp.bfloat16
NT, NN = ((1,), (1,)), ((1,), (0,))

N_COPIES = 80
SAMP = 8
CHIPS = 4
RANK = 256
PIECE = RANK // SAMP

SCRATCH = dict(
    ext=pltpu.VMEM((48, 128, 256), BF16),
    tiles=pltpu.VMEM((2, 16, 4, 128, 128), BF16),
    cols_in=pltpu.VMEM((16, 4), jnp.int32),
    cols=pltpu.SMEM((2, 16, 4), jnp.int32),
    phi=pltpu.VMEM((3, 512, 256), F32),
    phi_h=pltpu.VMEM((3, 512, 256), BF16),
    phi_l=pltpu.VMEM((3, 512, 256), BF16),
    part=pltpu.VMEM((4, 4, 128, 256), F32),
    part_in=pltpu.VMEM((3, 4, 128, 256), F32),
    swap=pltpu.VMEM((2, 128, 256), F32),
    samp=pltpu.VMEM((2, 2, 128, 256), F32),
    mine=pltpu.VMEM((3, 256, 256), F32),
    rs_in=pltpu.VMEM((3, 7, PIECE, 256), F32),
    full=pltpu.VMEM((3, 256, 256), F32),
    wpart=pltpu.VMEM((4, 2, 128, 128), F32),
    wrs_in=pltpu.VMEM((7, 128, 128), F32),
    wcol=pltpu.VMEM((2, 128, 128), F32),
    z_all=pltpu.VMEM((SAMP, 2, 256, 256), BF16),
    yx_h=pltpu.VMEM((512, 256), BF16),
    yx_l=pltpu.VMEM((512, 256), BF16),
    f_h=pltpu.VMEM((256, 256), BF16),
    f_l=pltpu.VMEM((256, 256), BF16),
    x_h=pltpu.VMEM((3, 256, 256), BF16),
    x_l=pltpu.VMEM((3, 256, 256), BF16),
    a_h=pltpu.VMEM((6, 256, 256), BF16),
    a_l=pltpu.VMEM((6, 256, 256), BF16),
    t_h=pltpu.VMEM((256, 256), BF16),
    t_l=pltpu.VMEM((256, 256), BF16),
    gram=pltpu.VMEM((2, 256, 256), F32),
    gram_in=pltpu.VMEM((2, 256, 256), F32),
    cross=pltpu.VMEM((256, 256), F32),
    cross_in=pltpu.VMEM((256, 256), F32),
    wc=pltpu.VMEM((2, 256, 128), F32),
    wc_in=pltpu.VMEM((2, 256, 128), F32),
    basis_v=pltpu.VMEM((2048, 256), F32),
    nested_v=pltpu.VMEM((256, 256), F32),
    approx_v=pltpu.VMEM((2048, 64), F32),
    local=pltpu.SemaphoreType.DMA((10,)),
    send=pltpu.SemaphoreType.DMA((N_COPIES,)),
    recv=pltpu.SemaphoreType.DMA((N_COPIES,)),
)


def split(value):
    high = value.astype(BF16)
    return high, (value - high.astype(F32)).astype(BF16)


def dot3(a, b):
    left = jnp.concatenate([a[0], a[0], a[1]], axis=1)
    right = jnp.concatenate([b[0], b[1], b[0]], axis=0)
    return lax.dot_general(left, right, ((NN[0], NN[1]), ((), ())), preferred_element_type=F32)


def kernel(n_rows, *refs):
    tiles_hbm, cols_hbm, b_hbm, phi0_hbm, phi1_hbm, phi2_hbm = refs[:6]
    basis_hbm, nested_hbm, approx_hbm = refs[6:9]
    v = dict(zip(SCRATCH, refs[9:]))

    r = lax.axis_index("rows")
    s = lax.axis_index("samp")
    x = lax.div(s, 2)
    c = lax.rem(s, 2)
    partner = (r, s + 1 - 2 * c)
    left = (lax.rem(r + n_rows - 1, n_rows), s)
    right = (lax.rem(r + 1, n_rows), s)
    sibling = (r + 1 - 2 * lax.rem(r, 2), s)
    cousin = (r + 2 - 4 * lax.rem(lax.div(r, 2), 2), s)

    def samp_peer(offset):
        return lax.rem(s + offset, SAMP)

    def chip_peer(offset):
        return (r, 2 * lax.rem(x + offset, CHIPS) + c)

    barrier = pltpu.get_barrier_semaphore()
    peers = [(r, samp_peer(o)) for o in range(1, SAMP)] + [left, right, cousin]
    for peer in peers:
        pl.semaphore_signal(barrier, inc=1, device_id=peer, device_id_type=MESH)

    locals_ = []

    def local(src, dst):
        copy = pltpu.make_async_copy(src, dst, v["local"].at[len(locals_)])
        locals_.append(copy)
        copy.start()
        return copy

    mine_half = pl.ds(pl.multiple_of(c * 256, 256), 256)
    own_cols = local(cols_hbm, v["cols"].at[0])
    own_tiles = local(tiles_hbm, v["tiles"].at[0])
    own_b = local(b_hbm.at[:, :, mine_half], v["ext"].at[pl.ds(16, 16)])
    phis = [local(p, v["phi"].at[i]) for i, p in enumerate((phi0_hbm, phi1_hbm, phi2_hbm))]
    pl.semaphore_wait(barrier, len(peers))

    sent = []

    def remote(src, dst, device):
        i = len(sent)
        copy = pltpu.make_async_remote_copy(
            src_ref=src,
            dst_ref=dst,
            send_sem=v["send"].at[i],
            recv_sem=v["recv"].at[i],
            device_id=device,
            device_id_type=MESH,
        )
        sent.append(copy)
        copy.start()
        return copy

    with jax.named_scope("halo"):
        halo = [
            remote(b_hbm.at[:, :, mine_half], v["ext"].at[pl.ds(32, 16)], left),
            remote(b_hbm.at[:, :, mine_half], v["ext"].at[pl.ds(0, 16)], right),
        ]
        cols_copy = remote(cols_hbm, v["cols_in"], partner)
        tiles_copy = remote(tiles_hbm, v["tiles"].at[1], partner)
        for i, copy in enumerate(phis):
            copy.wait()
            high, low = split(v["phi"][i])
            v["phi_h"][i] = high
            v["phi_l"][i] = low
        cols_copy.wait_recv()
        other_cols = local(v["cols_in"], v["cols"].at[1])
        for copy in (own_cols, own_tiles, own_b, other_cols):
            copy.wait()
        tiles_copy.wait_recv()
        for copy in halo:
            copy.wait_recv()

    first = (r - 1) * 16

    with jax.named_scope("product"):
        parts = []
        for j, offset in enumerate((2, 1, 3, 0)):
            base = 4 * lax.rem(x + offset, CHIPS)

            def tile_row(t, _, j=j, base=base):
                row = base + t
                lhs = jnp.concatenate(
                    [v["tiles"][h, row, k] for h in range(2) for k in range(4)], axis=1
                )
                rhs = jnp.concatenate(
                    [
                        v["ext"][jnp.clip(v["cols"][h, row, k] - first, 0, 47)]
                        for h in range(2)
                        for k in range(4)
                    ],
                    axis=0,
                )
                v["part"][j, t] = jnp.dot(lhs, rhs, preferred_element_type=F32)
                return 0

            lax.fori_loop(0, 4, tile_row, 0)
            if offset:
                parts.append(
                    remote(v["part"].at[j], v["part_in"].at[offset - 1], chip_peer(offset))
                )
        for copy in parts:
            copy.wait_recv()

        def summed(half):
            at = pl.ds(2 * half, 2)
            total = v["part"][3, at]
            for i in range(3):
                total = total + v["part_in"][i, at]
            return total

        v["swap"][...] = summed(1 - c)
        swapped = remote(v["swap"], v["samp"].at[c], partner)
        v["samp"][c] = summed(c)
        swapped.wait_recv()

    def put(slot, value):
        high, low = split(value)
        v["a_h"][slot] = high
        v["a_l"][slot] = low

    def get(slot):
        return v["a_h"][slot], v["a_l"][slot]

    def phi_of(i):
        return v["phi_h"][i], v["phi_l"][i]

    with jax.named_scope("sums"):
        for half in range(2):
            put(half, v["samp"][half].reshape(256, 256))
        sample = (
            jnp.concatenate([v["a_h"][0], v["a_h"][1]], axis=1),
            jnp.concatenate([v["a_l"][0], v["a_l"][1]], axis=1),
        )
        z = dot3(sample, phi_of(0))
        put(2, z)
        z_high, z_low = split(z)
        v["z_all"][s, 0] = z_high
        v["z_all"][s, 1] = z_low
        t_high, t_low = split(z.T)
        v["t_h"][...] = t_high
        v["t_l"][...] = t_low
        z_t = lambda: (v["t_h"][...], v["t_l"][...])
        v["mine"][0] = dot3(z_t(), get(2))

        def scatter(m):
            return [
                remote(
                    v["mine"].at[m, pl.ds(pl.multiple_of(samp_peer(o) * PIECE, PIECE), PIECE)],
                    v["rs_in"].at[m, o - 1],
                    (r, samp_peer(o)),
                )
                for o in range(1, SAMP)
            ]

        own = pl.ds(pl.multiple_of(s * PIECE, PIECE), PIECE)

        def gather(m, copies):
            for copy in copies:
                copy.wait_recv()
            total = v["mine"][m, own]
            for o in range(SAMP - 1):
                total = total + v["rs_in"][m, o]
            v["full"][m, own] = total
            return [
                remote(v["full"].at[m, own], v["full"].at[m, own], (r, samp_peer(o)))
                for o in range(1, SAMP)
            ]

        scatter_g = scatter(0)
        for half in range(2):
            w = dot3(z_t(), get(half))
            put(3 + half, w)
            for q in range(4):
                v["wpart"][2 * half + q // 2, q % 2] = w[
                    128 * (q % 2) : 128 * (q % 2) + 128, 128 * (q // 2) : 128 * (q // 2) + 128
                ]
        w_all = (
            jnp.concatenate([v["a_h"][3], v["a_h"][4]], axis=1),
            jnp.concatenate([v["a_l"][3], v["a_l"][4]], axis=1),
        )
        v["mine"][1] = dot3(w_all, phi_of(1))
        gather_g = gather(0, scatter_g)
        scatter_n = scatter(1)
        v["mine"][2] = dot3(w_all, phi_of(2))
        gather_n = gather(1, scatter_n)
        scatter_o = scatter(2)
        for copy in gather_g:
            copy.wait_recv()

    eye = jnp.where(
        lax.broadcasted_iota(jnp.int32, (RANK, RANK), 0)
        == lax.broadcasted_iota(jnp.int32, (RANK, RANK), 1),
        F32(1.5),
        F32(0),
    )

    def inverse_root(level, gram):
        norm = jnp.sqrt(jnp.sum(jnp.sum(gram * gram, axis=1, keepdims=True), axis=0, keepdims=True)) + 1e-06
        y = gram / norm
        high, low = split(y)
        factor = split(eye - 0.5 * y)
        new_high, new_low = split(dot3((high, low), factor))
        v["yx_h"][0:256] = new_high
        v["yx_l"][0:256] = new_low
        v["yx_h"][256:512] = factor[0]
        v["yx_l"][256:512] = factor[1]

        def make_factor():
            product = dot3(
                (v["yx_h"][256:512], v["yx_l"][256:512]), (v["yx_h"][0:256], v["yx_l"][0:256])
            )
            high, low = split(eye - 0.5 * product)
            v["f_h"][...] = high
            v["f_l"][...] = low

        def step(_, carry):
            make_factor()
            high, low = split(
                dot3((v["yx_h"][...], v["yx_l"][...]), (v["f_h"][...], v["f_l"][...]))
            )
            v["yx_h"][...] = high
            v["yx_l"][...] = low
            return carry

        lax.fori_loop(0, NS_ITERS - 2, step, 0)
        make_factor()
        high, low = split(
            dot3(
                (v["yx_h"][256:512], v["yx_l"][256:512]), (v["f_h"][...], v["f_l"][...])
            )
        )
        v["x_h"][level] = high
        v["x_l"][level] = low
        return 1.0 / jnp.sqrt(norm)

    def root(level):
        return v["x_h"][level], v["x_l"][level]

    with jax.named_scope("leaf"):
        scale_leaf = inverse_root(0, v["full"][0])
        for copy in gather_n:
            copy.wait_recv()
        put(0, dot3(root(0), split(v["full"][1])) * scale_leaf)
        zp = v["a_h"][0].astype(F32) + v["a_l"][0].astype(F32)
        t_high, t_low = split(zp.T)
        v["t_h"][...] = t_high
        v["t_l"][...] = t_low
        v["gram"][0] = dot3(z_t(), get(0))
        gram_copy = remote(v["gram"].at[0], v["gram_in"].at[0], sibling)

        gather_o = gather(2, scatter_o)
        scatter_w = []
        for o in range(1, SAMP):
            d = samp_peer(o)
            scatter_w.append(
                remote(v["wpart"].at[lax.div(d, 2), lax.rem(d, 2)], v["wrs_in"].at[o - 1], (r, d))
            )
        spread = [
            remote(v["z_all"].at[s], v["z_all"].at[s], chip_peer(o)) for o in range(1, CHIPS)
        ]
        spread_partner = remote(v["z_all"].at[s], v["z_all"].at[s], partner)
        for copy in gather_o:
            copy.wait_recv()
        put(5, dot3(root(0), split(v["full"][2])) * scale_leaf)
        v["cross"][...] = dot3(z_t(), get(5))
        cross_copy = remote(v["cross"], v["cross_in"], sibling)
        gram_copy.wait_recv()

    with jax.named_scope("pair"):
        scale_pair = inverse_root(1, v["gram"][0] + v["gram_in"][0])
        cross_copy.wait_recv()
        zq = dot3(root(1), split(v["cross"][...] + v["cross_in"][...])) * scale_pair
        put(1, zq)
        tq_high, tq_low = split(zq.T)
        v["a_h"][3] = tq_high
        v["a_l"][3] = tq_low
        v["gram"][1] = dot3(get(3), get(1))
        gram_copy = remote(v["gram"].at[1], v["gram_in"].at[1], cousin)

        for copy in scatter_w:
            copy.wait_recv()
        total = v["wpart"][x, c]
        for o in range(SAMP - 1):
            total = total + v["wrs_in"][o]
        v["wcol"][c] = total
        wcol_copy = remote(v["wcol"].at[c], v["wcol"].at[c], partner)
        wcol_copy.wait_recv()
        coarse = dot3(root(0), split(v["wcol"][...].reshape(256, 128))) * scale_leaf
        v["wc"][0] = dot3(z_t(), split(coarse))
        wc_copy = remote(v["wc"].at[0], v["wc_in"].at[0], sibling)
        put(2, dot3(get(0), root(1)) * scale_pair)
        put(4, dot3(get(2), get(1)))
        forwarded = []
        for o in range(1, CHIPS):
            spread[o - 1].wait_recv()
            origin = 2 * lax.rem(x + CHIPS - o, CHIPS) + c
            forwarded.append(remote(v["z_all"].at[origin], v["z_all"].at[origin], partner))
        wc_copy.wait_recv()
        middle = dot3(root(1), split(v["wc"][0] + v["wc_in"][0])) * scale_pair
        v["wc"][1] = dot3(get(3), split(middle))
        wc_copy = remote(v["wc"].at[1], v["wc_in"].at[1], cousin)
        spread_partner.wait_recv()
        for copy in forwarded:
            copy.wait_recv()

        def basis_rows(i, carry):
            rows = pl.ds(pl.multiple_of(i * 256, 256), 256)
            v["basis_v"][rows] = (
                dot3((v["z_all"][i, 0], v["z_all"][i, 1]), root(0)) * scale_leaf
            )
            return carry

        lax.fori_loop(0, SAMP, basis_rows, 0)
        basis_copy = local(v["basis_v"], basis_hbm)
        gram_copy.wait_recv()

    with jax.named_scope("quad"):
        scale_quad = inverse_root(2, v["gram"][1] + v["gram_in"][1])
        nested = dot3(get(4), root(2)) * scale_quad
        v["nested_v"][...] = nested
        nested_copy = local(v["nested_v"], nested_hbm)
        wc_copy.wait_recv()
        summary = dot3(root(2), split(v["wc"][1] + v["wc_in"][1])) * scale_quad
        inner = dot3(split(nested), split(summary))
        inner = jnp.where(c == 0, inner[:, 0:64], inner[:, 64:128])
        put_high, put_low = split(inner)

        def approx_rows(i, carry):
            rows = pl.ds(pl.multiple_of(i * 256, 256), 256)
            v["approx_v"][rows] = dot3(split(v["basis_v"][rows]), (put_high, put_low))
            return carry

        lax.fori_loop(0, SAMP, approx_rows, 0)
        approx_copy = local(v["approx_v"], approx_hbm)
        for copy in (basis_copy, nested_copy, approx_copy):
            copy.wait()
        assert len(sent) <= N_COPIES and len(locals_) <= 10
        for copy in sent:
            copy.wait_send()


def on_device(n_rows, coupling_tiles, tile_columns, sample_matrix, phi_leaf, phi_pair, phi_quad):
    rows = sample_matrix.shape[0]
    any_ = pl.BlockSpec(memory_space=pl.ANY)
    return pl.pallas_call(
        functools.partial(kernel, n_rows),
        out_shape=(
            jax.ShapeDtypeStruct((rows, RANK), F32),
            jax.ShapeDtypeStruct((RANK, RANK), F32),
            jax.ShapeDtypeStruct((rows, sample_matrix.shape[1] // SAMP), F32),
        ),
        in_specs=[any_] * 6,
        out_specs=(any_, any_, any_),
        scratch_shapes=list(SCRATCH.values()),
        compiler_params=pltpu.CompilerParams(
            collective_id=0, has_side_effects=True, vmem_limit_bytes=56 * 2**20
        ),
        name="hss",
    )(coupling_tiles, tile_columns, sample_matrix.reshape(16, 128, 512), phi_leaf, phi_pair, phi_quad)


def solution(mesh):
    return jax.shard_map(
        functools.partial(on_device, mesh.shape["rows"]),
        mesh=mesh,
        in_specs=(P("rows", "samp", None, None), P("rows", "samp"), P("rows", None), P(), P(), P()),
        out_specs=(P("rows", None), P("rows", None), P("rows", "samp")),
        check_vma=False,
    )
```

```python
import functools

import jax
import jax.numpy as jnp
from jax import lax
from jax.experimental import pallas as pl
from jax.experimental.pallas import tpu as pltpu
from jax.sharding import PartitionSpec as P

NS_ITERS = 5
MESH = pl.DeviceIdType.MESH
F32 = jnp.float32
BF16 = jnp.bfloat16
NT, NN = ((1,), (1,)), ((1,), (0,))

N_COPIES = 96
SAMP = 8
CHIPS = 4
RANK = 256

I16 = jnp.int16

SCRATCH = dict(
    ext=pltpu.VMEM((48, 128, 256), BF16),
    tiles=pltpu.VMEM((2, 16, 4, 128, 128), BF16),
    cols_in=pltpu.VMEM((4, 16), jnp.int32),
    cols=pltpu.SMEM((2, 4, 16), jnp.int32),
    phi=pltpu.VMEM((3, 512, 256), F32),
    phi_h=pltpu.VMEM((3, 512, 256), BF16),
    phi_l=pltpu.VMEM((3, 512, 256), BF16),
    part=pltpu.VMEM((2, 2, 128, 256), F32),
    code=pltpu.VMEM((6, 256, 256), I16),
    code_in=pltpu.VMEM((6, 256, 256), I16),
    unit=pltpu.VMEM((6, 8, 256), F32),
    unit_in=pltpu.VMEM((6, 8, 256), F32),
    swap=pltpu.VMEM((256, 256), F32),
    samp=pltpu.VMEM((2, 256, 256), F32),
    mine=pltpu.VMEM((3, 256, 256), F32),
    in_core=pltpu.VMEM((3, 128, 256), F32),
    chip=pltpu.VMEM((3, 128, 256), F32),
    in_chip=pltpu.VMEM((3, 128, 256), F32),
    two=pltpu.VMEM((3, 128, 256), F32),
    in_two=pltpu.VMEM((3, 128, 256), F32),
    full=pltpu.VMEM((3, 256, 256), F32),
    wpart=pltpu.VMEM((2, 4, 128, 128), F32),
    w_core=pltpu.VMEM((4, 128, 128), F32),
    w_chip=pltpu.VMEM((4, 128, 128), F32),
    w_in=pltpu.VMEM((3, 128, 128), F32),
    wcol=pltpu.VMEM((2, 128, 128), F32),
    z_own=pltpu.VMEM((2, 256, 256), BF16),
    yx_h=pltpu.VMEM((512, 256), BF16),
    yx_l=pltpu.VMEM((512, 256), BF16),
    f_h=pltpu.VMEM((256, 256), BF16),
    f_l=pltpu.VMEM((256, 256), BF16),
    x_h=pltpu.VMEM((3, 256, 256), BF16),
    x_l=pltpu.VMEM((3, 256, 256), BF16),
    a_h=pltpu.VMEM((6, 256, 256), BF16),
    a_l=pltpu.VMEM((6, 256, 256), BF16),
    t_h=pltpu.VMEM((256, 256), BF16),
    t_l=pltpu.VMEM((256, 256), BF16),
    swapped_pair=pltpu.VMEM((3, 256, 256), F32),
    swapped_in=pltpu.VMEM((3, 128, 256), F32),
    swapped_sum=pltpu.VMEM((3, 256, 256), F32),
    wc=pltpu.VMEM((2, 256, 128), F32),
    wc_in=pltpu.VMEM((2, 256, 128), F32),
    root_v=pltpu.VMEM((2, 256, 256), BF16),
    nested_v=pltpu.VMEM((256, 256), F32),
    inner_t=pltpu.VMEM((128, 256), F32),
    inner_v=pltpu.VMEM((64, 256), F32),
    local=pltpu.SemaphoreType.DMA((12,)),
    send=pltpu.SemaphoreType.DMA((N_COPIES,)),
    recv=pltpu.SemaphoreType.DMA((N_COPIES,)),
)


def split(value):
    high = value.astype(BF16)
    return high, (value - high.astype(F32)).astype(BF16)


def dot3(a, b):
    left = jnp.concatenate([a[0], a[0], a[1]], axis=1)
    right = jnp.concatenate([b[0], b[1], b[0]], axis=0)
    return lax.dot_general(left, right, (NN, ((), ())), preferred_element_type=F32)


def dot3_nt(a, b):
    left = jnp.concatenate([a[0], a[0], a[1]], axis=1)
    right = jnp.concatenate([b[0], b[1], b[0]], axis=1)
    return lax.dot_general(left, right, (NT, ((), ())), preferred_element_type=F32)


def kernel(n_rows, *refs):
    tiles_hbm, cols_hbm, b_hbm, phi0_hbm, phi1_hbm, phi2_hbm = refs[:6]
    z_hbm, root_hbm, nested_hbm, inner_hbm = refs[6:10]
    v = dict(zip(SCRATCH, refs[10:]))

    r = lax.axis_index("rows")
    s = lax.axis_index("samp")
    x = lax.div(s, 2)
    c = lax.rem(s, 2)
    y = lax.rem(r, 4)
    xr, opposite, xl = (lax.rem(x + o, CHIPS) for o in (1, 2, 3))

    def chip(index):
        return (r, 2 * index + c)

    partner = (r, s + 1 - 2 * c)
    left = (lax.rem(r + n_rows - 1, n_rows), s)
    right = (lax.rem(r + 1, n_rows), s)
    sibling = (r + 1 - 2 * lax.rem(r, 2), s)
    cousin = (r + 3 - 2 * y, s)
    first_dim = x + 1 - 2 * lax.rem(x, 2)
    second_dim = 3 - x

    barrier = pltpu.get_barrier_semaphore()
    peers = [partner, chip(xr), chip(opposite), chip(xl), left, right, cousin]
    for peer in peers:
        pl.semaphore_signal(barrier, inc=1, device_id=peer, device_id_type=MESH)

    locals_ = []

    def local(src, dst):
        copy = pltpu.make_async_copy(src, dst, v["local"].at[len(locals_)])
        locals_.append(copy)
        copy.start()
        return copy

    sent = []

    def remote(src, dst, device):
        i = len(sent)
        copy = pltpu.make_async_remote_copy(
            src_ref=src,
            dst_ref=dst,
            send_sem=v["send"].at[i],
            recv_sem=v["recv"].at[i],
            device_id=device,
            device_id_type=MESH,
        )
        sent.append(copy)
        copy.start()
        return copy

    mine_half = pl.ds(pl.multiple_of(c * 256, 256), 256)
    own_cols = local(cols_hbm, v["cols"].at[0])
    pl.semaphore_wait(barrier, len(peers))

    with jax.named_scope("halo"):
        direct = []
        for i in range(4):
            at = 4 * x + i
            piece = b_hbm.at[at, :, mine_half]
            direct.append(
                (
                    remote(piece, v["ext"].at[at], right),
                    remote(piece, v["ext"].at[32 + at], left),
                )
            )
        cols_copy = remote(cols_hbm, v["cols_in"], partner)
        far = pl.ds(4 * opposite, 4)
        far_copies = [
            remote(b_hbm.at[far, :, mine_half], v["ext"].at[far], right),
            remote(b_hbm.at[far, :, mine_half], v["ext"].at[pl.ds(32 + 4 * opposite, 4)], left),
        ]
        tiles_copy = remote(tiles_hbm, v["tiles"].at[1], partner)
        own_tiles = local(tiles_hbm, v["tiles"].at[0])
        own_b = local(b_hbm.at[:, :, mine_half], v["ext"].at[pl.ds(16, 16)])
        phis = [local(p, v["phi"].at[i]) for i, p in enumerate((phi0_hbm, phi1_hbm, phi2_hbm))]
        handed = []
        for i in range(4):
            for side in range(2):
                direct[i][side].wait_recv()
                piece = v["ext"].at[32 * side + 4 * x + i]
                handed.append(remote(piece, piece, chip(xr)))
                handed.append(remote(piece, piece, chip(xl)))
        for i, copy in enumerate(phis):
            copy.wait()
            high, low = split(v["phi"][i])
            v["phi_h"][i] = high
            v["phi_l"][i] = low
        cols_copy.wait_recv()
        other_cols = local(v["cols_in"], v["cols"].at[1])
        for copy in (own_cols, own_tiles, own_b, other_cols):
            copy.wait()
        for copy in [tiles_copy] + far_copies + handed:
            copy.wait_recv()
    first = (r - 1) * 16

    def product(slot, base):
        def tile_row(t, carry):
            row = base + t
            lhs = jnp.concatenate(
                [v["tiles"][h, row, k] for h in range(2) for k in range(4)], axis=1
            )
            rhs = jnp.concatenate(
                [
                    v["ext"][jnp.clip(v["cols"][h, k, row] - first, 0, 47)]
                    for h in range(2)
                    for k in range(4)
                ],
                axis=0,
            )
            v["part"][slot, t] = jnp.dot(lhs, rhs, preferred_element_type=F32)
            return carry

        lax.fori_loop(0, 2, tile_row, 0)
        return v["part"][slot].reshape(256, 256)

    def coded(i, value, device):
        top = jnp.maximum(jnp.max(jnp.abs(value), axis=1, keepdims=True), 1e-30)
        v["code"][i] = jnp.round(value * (32767.0 / top)).astype(jnp.int32).astype(I16)
        v["unit"][i] = jnp.broadcast_to(top * (1 / 32767.0), (256, 128)).T[0:8]
        return (
            remote(v["code"].at[i], v["code_in"].at[i], device),
            remote(v["unit"].at[i], v["unit_in"].at[i], device),
        )

    def decoded(i, copies):
        for copy in copies:
            copy.wait_recv()
        unit = jnp.broadcast_to(v["unit_in"][i, 0:1], (128, 256)).T
        return v["code_in"][i].astype(jnp.int32).astype(F32) * jnp.concatenate([unit, unit], axis=1)

    with jax.named_scope("product"):
        up_far = coded(0, product(0, 4 * opposite), chip(xr))
        down_far = coded(1, product(1, 4 * opposite + 2), chip(xl))
        down_near = coded(2, product(0, 4 * xr + 2), chip(xr))
        up_near = coded(3, product(1, 4 * xl), chip(xl))
        up_sum = coded(4, product(0, 4 * xr) + decoded(0, up_far), chip(xr))
        down_sum = coded(5, product(1, 4 * xl + 2) + decoded(1, down_far), chip(xl))
        product(0, 4 * x)
        product(1, 4 * x + 2)
        upper_in = decoded(3, up_near) + decoded(4, up_sum)
        lower_in = decoded(2, down_near) + decoded(5, down_sum)
        upper_half = v["part"][0].reshape(256, 256) + upper_in
        lower_half = v["part"][1].reshape(256, 256) + lower_in
        v["swap"][...] = jnp.where(c == 0, lower_half, upper_half)
        swapped = remote(v["swap"], v["samp"].at[c], partner)
        v["samp"][c] = jnp.where(c == 0, upper_half, lower_half)
        swapped.wait_recv()
    def put(slot, value):
        high, low = split(value)
        v["a_h"][slot] = high
        v["a_l"][slot] = low

    def get(slot):
        return v["a_h"][slot], v["a_l"][slot]

    def phi_of(i):
        return v["phi_h"][i], v["phi_l"][i]

    def transposed():
        return v["t_h"][...], v["t_l"][...]

    core_rows = pl.ds(pl.multiple_of(c * 128, 128), 128)
    other_rows = pl.ds(pl.multiple_of((1 - c) * 128, 128), 128)

    def sum_core(m):
        return [remote(v["mine"].at[m, other_rows], v["in_core"].at[m], partner)]

    def crossed(ref, into, m, one, two):
        return [
            remote(v[ref].at[m, 0:64], v[into].at[m, 0:64], chip(one)),
            remote(v[ref].at[m, 64:128], v[into].at[m, 64:128], chip(two)),
        ]

    def arrived(copies):
        for copy in copies:
            copy.wait_recv()

    def sum_first(m, copies):
        arrived(copies)
        v["chip"][m] = v["mine"][m, core_rows] + v["in_core"][m]
        return crossed("chip", "in_chip", m, first_dim, second_dim)

    def sum_second(m, copies):
        arrived(copies)
        v["two"][m] = v["chip"][m] + v["in_chip"][m]
        return crossed("two", "in_two", m, second_dim, first_dim)

    def sum_last(m, copies):
        arrived(copies)
        v["full"][m, core_rows] = v["two"][m] + v["in_two"][m]
        return [remote(v["full"].at[m, core_rows], v["full"].at[m, core_rows], partner)]

    with jax.named_scope("sums"):
        for half in range(2):
            put(half, v["samp"][half])
        sample = (
            jnp.concatenate([v["a_h"][0], v["a_h"][1]], axis=1),
            jnp.concatenate([v["a_l"][0], v["a_l"][1]], axis=1),
        )
        z = dot3(sample, phi_of(0))
        z_high, z_low = split(z)
        v["z_own"][0] = z_high
        v["z_own"][1] = z_low
        t_high, t_low = split(z.T)
        v["t_h"][...] = t_high
        v["t_l"][...] = t_low
        v["mine"][0] = dot3(transposed(), (v["z_own"][0], v["z_own"][1]))
        sum_g = sum_core(0)
        z_local = local(v["z_own"], z_hbm.at[s])
        for half in range(2):
            w = dot3(transposed(), get(half))
            put(3 + half, w)
            for q in range(4):
                v["wpart"][q // 2, 2 * half + q % 2] = w[
                    128 * (q // 2) : 128 * (q // 2) + 128, 128 * (q % 2) : 128 * (q % 2) + 128
                ]
        sum_g = sum_first(0, sum_g)
        w_all = (
            jnp.concatenate([v["a_h"][3], v["a_h"][4]], axis=1),
            jnp.concatenate([v["a_l"][3], v["a_l"][4]], axis=1),
        )
        v["mine"][1] = dot3(w_all, phi_of(1))
        sum_n = sum_core(1)
        v["mine"][2] = dot3(w_all, phi_of(2))
        sum_o = sum_core(2)
        w_core = remote(v["wpart"].at[1 - c], v["w_core"], partner)
        sum_n = sum_first(1, sum_n)
        sum_g = sum_second(0, sum_g)
        sum_o = sum_first(2, sum_o)
        sum_n = sum_second(1, sum_n)
        sum_g = sum_last(0, sum_g)
        w_core.wait_recv()
        v["w_chip"][...] = v["wpart"][c] + v["w_core"][...]
        w_copies = [
            remote(v["w_chip"].at[d], v["w_in"].at[o], chip(d))
            for o, d in enumerate((xr, opposite, xl))
        ]
        z_right = remote(v["z_own"], z_hbm.at[s], chip(xr))
        z_left = remote(v["z_own"], z_hbm.at[s], chip(xl))
        z_partner = remote(v["z_own"], z_hbm.at[s], partner)
        sum_o = sum_second(2, sum_o)
        arrived(sum_g)
    eye = jnp.where(
        lax.broadcasted_iota(jnp.int32, (RANK, RANK), 0)
        == lax.broadcasted_iota(jnp.int32, (RANK, RANK), 1),
        F32(1.5),
        F32(0),
    )

    def inverse_root(level, gram):
        norm = (
            jnp.sqrt(
                jnp.sum(jnp.sum(gram * gram, axis=1, keepdims=True), axis=0, keepdims=True)
            )
            + 1e-06
        )
        y0 = gram / norm
        factor = split(eye - 0.5 * y0)
        new_high, new_low = split(dot3(split(y0), factor))
        v["yx_h"][0:256] = new_high
        v["yx_l"][0:256] = new_low
        v["yx_h"][256:512] = factor[0]
        v["yx_l"][256:512] = factor[1]

        def make_factor():
            both = dot3(
                (v["yx_h"][256:512], v["yx_l"][256:512]), (v["yx_h"][0:256], v["yx_l"][0:256])
            )
            high, low = split(eye - 0.5 * both)
            v["f_h"][...] = high
            v["f_l"][...] = low

        def step(_, carry):
            make_factor()
            high, low = split(
                dot3((v["yx_h"][...], v["yx_l"][...]), (v["f_h"][...], v["f_l"][...]))
            )
            v["yx_h"][...] = high
            v["yx_l"][...] = low
            return carry

        lax.fori_loop(0, NS_ITERS - 2, step, 0)
        make_factor()
        result = dot3((v["yx_h"][256:512], v["yx_l"][256:512]), (v["f_h"][...], v["f_l"][...]))
        high, low = split(result)
        v["x_h"][level] = high
        v["x_l"][level] = low
        return 1.0 / jnp.sqrt(norm), result

    def root(level):
        return v["x_h"][level], v["x_l"][level]

    def exchange(i, device):
        return remote(v["swapped_pair"].at[i, core_rows], v["swapped_in"].at[i], device)

    def exchange_core(i, copy):
        copy.wait_recv()
        v["swapped_sum"][i, core_rows] = v["swapped_pair"][i, core_rows] + v["swapped_in"][i]
        return remote(v["swapped_sum"].at[i, core_rows], v["swapped_sum"].at[i, core_rows], partner)

    with jax.named_scope("leaf"):
        scale_leaf, x_leaf = inverse_root(0, v["full"][0])
        sum_n = sum_last(1, sum_n)
        sum_o = sum_last(2, sum_o)
        root_high, root_low = split(x_leaf * scale_leaf)
        v["root_v"][0] = root_high
        v["root_v"][1] = root_low
        root_copy = local(v["root_v"], root_hbm)
        arrived(sum_n)
        zp = dot3(root(0), split(v["full"][1])) * scale_leaf
        put(0, zp)
        t_high, t_low = split(zp.T)
        v["t_h"][...] = t_high
        v["t_l"][...] = t_low
        v["swapped_pair"][0] = dot3(transposed(), get(0))
        gram_copy = exchange(0, sibling)
        arrived(sum_o)
        put(5, dot3(root(0), split(v["full"][2])) * scale_leaf)
        v["swapped_pair"][1] = dot3(transposed(), get(5))
        cross_copy = exchange(1, sibling)
        arrived(w_copies)
        v["wcol"][c] = v["w_chip"][x] + v["w_in"][0] + v["w_in"][1] + v["w_in"][2]
        wcol_copy = remote(v["wcol"].at[c], v["wcol"].at[c], partner)
        gram_copy = exchange_core(0, gram_copy)
        wcol_copy.wait_recv()
        coarse = dot3(root(0), split(v["wcol"][...].reshape(256, 128))) * scale_leaf
        v["wc"][0] = dot3(transposed(), split(coarse))
        wc_copy = remote(v["wc"].at[0], v["wc_in"].at[0], sibling)
        gram_copy.wait_recv()
    with jax.named_scope("pair"):
        scale_pair, _ = inverse_root(1, v["swapped_sum"][0])
        cross_copy = exchange_core(1, cross_copy)
        put(2, dot3(get(0), root(1)) * scale_pair)
        cross_copy.wait_recv()
        zq = dot3(root(1), split(v["swapped_sum"][1])) * scale_pair
        put(1, zq)
        t_high, t_low = split(zq.T)
        v["t_h"][...] = t_high
        v["t_l"][...] = t_low
        v["swapped_pair"][2] = dot3(transposed(), get(1))
        gram_copy = exchange(2, cousin)
        put(4, dot3(get(2), get(1)))
        wc_copy.wait_recv()
        middle = dot3(root(1), split(v["wc"][0] + v["wc_in"][0])) * scale_pair
        v["wc"][1] = dot3(transposed(), split(middle))
        wc_copy = remote(v["wc"].at[1], v["wc_in"].at[1], cousin)
        z_right.wait_recv()
        from_left = 2 * xl + c
        round_right = remote(
            z_hbm.at[from_left, :, 0:128], z_hbm.at[from_left, :, 0:128], chip(xr)
        )
        z_left.wait_recv()
        from_right = 2 * xr + c
        round_left = remote(
            z_hbm.at[from_right, :, 128:256], z_hbm.at[from_right, :, 128:256], chip(xl)
        )
        handed_z = [
            remote(z_hbm.at[from_left], z_hbm.at[from_left], partner),
            remote(z_hbm.at[from_right], z_hbm.at[from_right], partner),
        ]
        gram_copy = exchange_core(2, gram_copy)
        arrived([round_right, round_left])
        from_far = 2 * opposite + c
        handed_z.append(remote(z_hbm.at[from_far], z_hbm.at[from_far], partner))
        gram_copy.wait_recv()
    with jax.named_scope("quad"):
        scale_quad, _ = inverse_root(2, v["swapped_sum"][2])
        nested = dot3(get(4), root(2)) * scale_quad
        v["nested_v"][...] = nested
        nested_copy = local(v["nested_v"], nested_hbm)
        wc_copy.wait_recv()
        summary = dot3(root(2), split(v["wc"][1] + v["wc_in"][1])) * scale_quad
        inner = dot3(split(nested), split(summary))
        v["inner_t"][...] = inner.T
        v["inner_v"][...] = v["inner_t"][pl.ds(pl.multiple_of(c * 64, 64), 64)]
        inner_copy = local(v["inner_v"], inner_hbm)
        arrived([z_partner] + handed_z)
        for copy in (z_local, root_copy, nested_copy, inner_copy):
            copy.wait()
        assert len(sent) <= N_COPIES and len(locals_) <= 12
        for copy in sent:
            copy.wait_send()


def outputs(z_ref, root_ref, nested_ref, inner_ref, basis_out, nested_out, approx_out):
    basis = dot3((z_ref[0, 0], z_ref[0, 1]), (root_ref[0], root_ref[1]))
    basis_out[...] = basis
    approx_out[...] = dot3_nt(split(inner_ref[...]), split(basis))
    nested_out[...] = nested_ref[...]


def on_device(n_rows, coupling_tiles, tile_columns, sample_matrix, phi_leaf, phi_pair, phi_quad):
    rows = sample_matrix.shape[0]
    share = sample_matrix.shape[1] // SAMP
    any_ = pl.BlockSpec(memory_space=pl.ANY)
    z, root, nested, inner = pl.pallas_call(
        functools.partial(kernel, n_rows),
        out_shape=(
            jax.ShapeDtypeStruct((SAMP, 2, RANK, RANK), BF16),
            jax.ShapeDtypeStruct((2, RANK, RANK), BF16),
            jax.ShapeDtypeStruct((RANK, RANK), F32),
            jax.ShapeDtypeStruct((share, RANK), F32),
        ),
        in_specs=[any_] * 6,
        out_specs=(any_,) * 4,
        scratch_shapes=list(SCRATCH.values()),
        compiler_params=pltpu.CompilerParams(
            collective_id=0, has_side_effects=True, vmem_limit_bytes=48 * 2**20
        ),
        name="hss",
    )(
        coupling_tiles,
        tile_columns.T,
        sample_matrix.reshape(16, 128, 512),
        phi_leaf,
        phi_pair,
        phi_quad,
    )
    basis, nested, approx_t = pl.pallas_call(
        outputs,
        grid=(SAMP,),
        out_shape=(
            jax.ShapeDtypeStruct((rows, RANK), F32),
            jax.ShapeDtypeStruct((RANK, RANK), F32),
            jax.ShapeDtypeStruct((share, rows), F32),
        ),
        in_specs=[
            pl.BlockSpec((1, 2, RANK, RANK), lambda i: (i, 0, 0, 0)),
            pl.BlockSpec((2, RANK, RANK), lambda i: (0, 0, 0)),
            pl.BlockSpec((RANK, RANK), lambda i: (0, 0)),
            pl.BlockSpec((share, RANK), lambda i: (0, 0)),
        ],
        out_specs=(
            pl.BlockSpec((RANK, RANK), lambda i: (i, 0)),
            pl.BlockSpec((RANK, RANK), lambda i: (0, 0)),
            pl.BlockSpec((share, RANK), lambda i: (0, i)),
        ),
        compiler_params=pltpu.CompilerParams(vmem_limit_bytes=16 * 2**20),
        name="expand",
    )(z, root, nested, inner)
    return basis, nested, approx_t.T


def solution(mesh):
    return jax.shard_map(
        functools.partial(on_device, mesh.shape["rows"]),
        mesh=mesh,
        in_specs=(P("rows", "samp", None, None), P("rows", "samp"), P("rows", None), P(), P(), P()),
        out_specs=(P("rows", None), P("rows", None), P("rows", "samp")),
        check_vma=False,
    )
```

```python
import functools

import jax
import jax.numpy as jnp
from jax import lax
from jax.experimental import pallas as pl
from jax.experimental.pallas import tpu as pltpu
from jax.sharding import PartitionSpec as P

NS_ITERS = 5
MESH = pl.DeviceIdType.MESH
F32 = jnp.float32
BF16 = jnp.bfloat16
NT, NN = ((1,), (1,)), ((1,), (0,))

N_COPIES = 96
SAMP = 8
CHIPS = 4
RANK = 256

I16 = jnp.int16

SCRATCH = dict(
    ext=pltpu.VMEM((48, 128, 256), BF16),
    tiles=pltpu.VMEM((2, 16, 4, 128, 128), BF16),
    cols_in=pltpu.VMEM((4, 16), jnp.int32),
    cols=pltpu.SMEM((2, 4, 16), jnp.int32),
    phi=pltpu.VMEM((3, 512, 256), F32),
    phi_h=pltpu.VMEM((3, 512, 256), BF16),
    phi_l=pltpu.VMEM((3, 512, 256), BF16),
    part=pltpu.VMEM((2, 2, 128, 256), F32),
    code=pltpu.VMEM((6, 256, 256), I16),
    code_in=pltpu.VMEM((6, 256, 256), I16),
    unit=pltpu.VMEM((6, 8, 256), F32),
    unit_in=pltpu.VMEM((6, 8, 256), F32),
    swap=pltpu.VMEM((256, 256), F32),
    samp=pltpu.VMEM((2, 256, 256), F32),
    mine=pltpu.VMEM((3, 256, 256), F32),
    in_core=pltpu.VMEM((3, 128, 256), F32),
    chip=pltpu.VMEM((3, 128, 256), F32),
    in_chip=pltpu.VMEM((3, 128, 256), F32),
    two=pltpu.VMEM((3, 128, 256), F32),
    in_two=pltpu.VMEM((3, 128, 256), F32),
    full=pltpu.VMEM((3, 256, 256), F32),
    wpart=pltpu.VMEM((2, 4, 128, 128), F32),
    w_core=pltpu.VMEM((4, 128, 128), F32),
    w_chip=pltpu.VMEM((4, 128, 128), F32),
    w_in=pltpu.VMEM((3, 128, 128), F32),
    wcol=pltpu.VMEM((2, 128, 128), F32),
    z_own=pltpu.VMEM((2, 256, 256), BF16),
    yx_h=pltpu.VMEM((512, 256), BF16),
    yx_l=pltpu.VMEM((512, 256), BF16),
    f_h=pltpu.VMEM((256, 256), BF16),
    f_l=pltpu.VMEM((256, 256), BF16),
    x_h=pltpu.VMEM((3, 256, 256), BF16),
    x_l=pltpu.VMEM((3, 256, 256), BF16),
    a_h=pltpu.VMEM((6, 256, 256), BF16),
    a_l=pltpu.VMEM((6, 256, 256), BF16),
    t_h=pltpu.VMEM((256, 256), BF16),
    t_l=pltpu.VMEM((256, 256), BF16),
    swapped_pair=pltpu.VMEM((3, 256, 256), F32),
    swapped_in=pltpu.VMEM((3, 128, 256), F32),
    swapped_sum=pltpu.VMEM((3, 256, 256), F32),
    wc=pltpu.VMEM((2, 256, 128), F32),
    wc_in=pltpu.VMEM((2, 256, 128), F32),
    root_v=pltpu.VMEM((2, 256, 256), BF16),
    xi_v=pltpu.VMEM((2, 256, 128), BF16),
    nested_v=pltpu.VMEM((256, 256), F32),
    local=pltpu.SemaphoreType.DMA((12,)),
    send=pltpu.SemaphoreType.DMA((N_COPIES,)),
    recv=pltpu.SemaphoreType.DMA((N_COPIES,)),
)


def split(value):
    high = value.astype(BF16)
    return high, (value - high.astype(F32)).astype(BF16)


def dot3(a, b):
    left = jnp.concatenate([a[0], a[0], a[1]], axis=1)
    right = jnp.concatenate([b[0], b[1], b[0]], axis=0)
    return lax.dot_general(left, right, (NN, ((), ())), preferred_element_type=F32)


def dot3_nt(a, b):
    left = jnp.concatenate([a[0], a[0], a[1]], axis=1)
    right = jnp.concatenate([b[0], b[1], b[0]], axis=1)
    return lax.dot_general(left, right, (NT, ((), ())), preferred_element_type=F32)


def kernel(n_rows, *refs):
    tiles_hbm, cols_hbm, b_hbm, phi0_hbm, phi1_hbm, phi2_hbm = refs[:6]
    z_hbm, root_hbm, nested_hbm, inner_hbm = refs[6:10]
    v = dict(zip(SCRATCH, refs[10:]))

    r = lax.axis_index("rows")
    s = lax.axis_index("samp")
    x = lax.div(s, 2)
    c = lax.rem(s, 2)
    y = lax.rem(r, 4)
    xr, opposite, xl = (lax.rem(x + o, CHIPS) for o in (1, 2, 3))

    def chip(index):
        return (r, 2 * index + c)

    partner = (r, s + 1 - 2 * c)
    left = (lax.rem(r + n_rows - 1, n_rows), s)
    right = (lax.rem(r + 1, n_rows), s)
    sibling = (r + 1 - 2 * lax.rem(r, 2), s)
    cousin = (r + 3 - 2 * y, s)
    first_dim = x + 1 - 2 * lax.rem(x, 2)
    second_dim = 3 - x

    barrier = pltpu.get_barrier_semaphore()
    peers = [partner, chip(xr), chip(opposite), chip(xl), left, right, cousin]
    for peer in peers:
        pl.semaphore_signal(barrier, inc=1, device_id=peer, device_id_type=MESH)

    locals_ = []

    def local(src, dst):
        copy = pltpu.make_async_copy(src, dst, v["local"].at[len(locals_)])
        locals_.append(copy)
        copy.start()
        return copy

    sent = []

    def remote(src, dst, device):
        i = len(sent)
        copy = pltpu.make_async_remote_copy(
            src_ref=src,
            dst_ref=dst,
            send_sem=v["send"].at[i],
            recv_sem=v["recv"].at[i],
            device_id=device,
            device_id_type=MESH,
        )
        sent.append(copy)
        copy.start()
        return copy

    mine_half = pl.ds(pl.multiple_of(c * 256, 256), 256)
    own_cols = local(cols_hbm, v["cols"].at[0])
    pl.semaphore_wait(barrier, len(peers))
    with jax.named_scope("halo"):
        direct = []
        for i in range(4):
            at = 4 * x + i
            piece = b_hbm.at[at, :, mine_half]
            direct.append(
                (
                    remote(piece, v["ext"].at[at], right),
                    remote(piece, v["ext"].at[32 + at], left),
                )
            )
        cols_copy = remote(cols_hbm, v["cols_in"], partner)
        far = pl.ds(4 * opposite, 4)
        far_copies = [
            remote(b_hbm.at[far, :, mine_half], v["ext"].at[far], right),
            remote(b_hbm.at[far, :, mine_half], v["ext"].at[pl.ds(32 + 4 * opposite, 4)], left),
        ]
        tiles_copy = remote(tiles_hbm, v["tiles"].at[1], partner)
        own_tiles = local(tiles_hbm, v["tiles"].at[0])
        own_b = local(b_hbm.at[:, :, mine_half], v["ext"].at[pl.ds(16, 16)])
        phis = [local(p, v["phi"].at[i]) for i, p in enumerate((phi0_hbm, phi1_hbm, phi2_hbm))]
        handed = []
        for i in range(4):
            for side in range(2):
                direct[i][side].wait_recv()
                piece = v["ext"].at[32 * side + 4 * x + i]
                handed.append(remote(piece, piece, chip(xr)))
                handed.append(remote(piece, piece, chip(xl)))
        for i, copy in enumerate(phis):
            copy.wait()
            high, low = split(v["phi"][i])
            v["phi_h"][i] = high
            v["phi_l"][i] = low
        cols_copy.wait_recv()
        other_cols = local(v["cols_in"], v["cols"].at[1])
        for copy in (own_cols, own_tiles, own_b, other_cols):
            copy.wait()
        for copy in [tiles_copy] + far_copies + handed:
            copy.wait_recv()
    first = (r - 1) * 16

    def product(slot, base):
        def tile_row(t, carry):
            row = base + t
            lhs = jnp.concatenate(
                [v["tiles"][h, row, k] for h in range(2) for k in range(4)], axis=1
            )
            rhs = jnp.concatenate(
                [
                    v["ext"][jnp.clip(v["cols"][h, k, row] - first, 0, 47)]
                    for h in range(2)
                    for k in range(4)
                ],
                axis=0,
            )
            v["part"][slot, t] = jnp.dot(lhs, rhs, preferred_element_type=F32)
            return carry

        lax.fori_loop(0, 2, tile_row, 0)
        return v["part"][slot].reshape(256, 256)

    def coded(i, value, device):
        top = jnp.maximum(jnp.max(jnp.abs(value), axis=1, keepdims=True), 1e-30)
        v["code"][i] = jnp.round(value * (32767.0 / top)).astype(jnp.int32).astype(I16)
        v["unit"][i] = jnp.broadcast_to(top * (1 / 32767.0), (256, 128)).T[0:8]
        return (
            remote(v["code"].at[i], v["code_in"].at[i], device),
            remote(v["unit"].at[i], v["unit_in"].at[i], device),
        )

    def decoded(i, copies):
        for copy in copies:
            copy.wait_recv()
        unit = jnp.broadcast_to(v["unit_in"][i, 0:1], (128, 256)).T
        return v["code_in"][i].astype(jnp.int32).astype(F32) * jnp.concatenate([unit, unit], axis=1)

    with jax.named_scope("product"):
        up_far = coded(0, product(0, 4 * opposite), chip(xr))
        down_far = coded(1, product(1, 4 * opposite + 2), chip(xl))
        down_near = coded(2, product(0, 4 * xr + 2), chip(xr))
        up_near = coded(3, product(1, 4 * xl), chip(xl))
        up_sum = coded(4, product(0, 4 * xr) + decoded(0, up_far), chip(xr))
        down_sum = coded(5, product(1, 4 * xl + 2) + decoded(1, down_far), chip(xl))
        product(0, 4 * x)
        product(1, 4 * x + 2)
        upper_in = decoded(3, up_near) + decoded(4, up_sum)
        lower_in = decoded(2, down_near) + decoded(5, down_sum)
        upper_half = v["part"][0].reshape(256, 256) + upper_in
        lower_half = v["part"][1].reshape(256, 256) + lower_in
        v["swap"][...] = jnp.where(c == 0, lower_half, upper_half)
        swapped = remote(v["swap"], v["samp"].at[c], partner)
        v["samp"][c] = jnp.where(c == 0, upper_half, lower_half)
        swapped.wait_recv()
    def put(slot, value):
        high, low = split(value)
        v["a_h"][slot] = high
        v["a_l"][slot] = low

    def get(slot):
        return v["a_h"][slot], v["a_l"][slot]

    def phi_of(i):
        return v["phi_h"][i], v["phi_l"][i]

    def transposed():
        return v["t_h"][...], v["t_l"][...]

    core_rows = pl.ds(pl.multiple_of(c * 128, 128), 128)
    other_rows = pl.ds(pl.multiple_of((1 - c) * 128, 128), 128)

    def sum_core(m):
        return [remote(v["mine"].at[m, other_rows], v["in_core"].at[m], partner)]

    def crossed(ref, into, m, one, two):
        return [
            remote(v[ref].at[m, 0:64], v[into].at[m, 0:64], chip(one)),
            remote(v[ref].at[m, 64:128], v[into].at[m, 64:128], chip(two)),
        ]

    def arrived(copies):
        for copy in copies:
            copy.wait_recv()

    def sum_first(m, copies):
        arrived(copies)
        v["chip"][m] = v["mine"][m, core_rows] + v["in_core"][m]
        return crossed("chip", "in_chip", m, first_dim, second_dim)

    def sum_second(m, copies):
        arrived(copies)
        v["two"][m] = v["chip"][m] + v["in_chip"][m]
        return crossed("two", "in_two", m, second_dim, first_dim)

    def sum_last(m, copies):
        arrived(copies)
        v["full"][m, core_rows] = v["two"][m] + v["in_two"][m]
        return [remote(v["full"].at[m, core_rows], v["full"].at[m, core_rows], partner)]

    with jax.named_scope("sums"):
        for half in range(2):
            put(half, v["samp"][half])
        sample = (
            jnp.concatenate([v["a_h"][0], v["a_h"][1]], axis=1),
            jnp.concatenate([v["a_l"][0], v["a_l"][1]], axis=1),
        )
        z = dot3(sample, phi_of(0))
        z_high, z_low = split(z)
        v["z_own"][0] = z_high
        v["z_own"][1] = z_low
        t_high, t_low = split(z.T)
        v["t_h"][...] = t_high
        v["t_l"][...] = t_low
        v["mine"][0] = dot3(transposed(), (v["z_own"][0], v["z_own"][1]))
        sum_g = sum_core(0)
        z_local = local(v["z_own"], z_hbm.at[s])
        for half in range(2):
            w = dot3(transposed(), get(half))
            put(3 + half, w)
            for q in range(4):
                v["wpart"][q // 2, 2 * half + q % 2] = w[
                    128 * (q // 2) : 128 * (q // 2) + 128, 128 * (q % 2) : 128 * (q % 2) + 128
                ]
        sum_g = sum_first(0, sum_g)
        w_all = (
            jnp.concatenate([v["a_h"][3], v["a_h"][4]], axis=1),
            jnp.concatenate([v["a_l"][3], v["a_l"][4]], axis=1),
        )
        v["mine"][1] = dot3(w_all, phi_of(1))
        sum_n = sum_core(1)
        v["mine"][2] = dot3(w_all, phi_of(2))
        sum_o = sum_core(2)
        w_core = remote(v["wpart"].at[1 - c], v["w_core"], partner)
        sum_n = sum_first(1, sum_n)
        sum_g = sum_second(0, sum_g)
        sum_o = sum_first(2, sum_o)
        sum_n = sum_second(1, sum_n)
        sum_g = sum_last(0, sum_g)
        sum_o = sum_second(2, sum_o)
        arrived(sum_g)
    eye = jnp.where(
        lax.broadcasted_iota(jnp.int32, (RANK, RANK), 0)
        == lax.broadcasted_iota(jnp.int32, (RANK, RANK), 1),
        F32(1.5),
        F32(0),
    )

    def inverse_root(level, gram):
        norm = (
            jnp.sqrt(
                jnp.sum(jnp.sum(gram * gram, axis=1, keepdims=True), axis=0, keepdims=True)
            )
            + 1e-06
        )
        y0 = gram / norm
        factor = split(eye - 0.5 * y0)
        new_high, new_low = split(dot3(split(y0), factor))
        v["yx_h"][0:256] = new_high
        v["yx_l"][0:256] = new_low
        v["yx_h"][256:512] = factor[0]
        v["yx_l"][256:512] = factor[1]

        def make_factor():
            both = dot3(
                (v["yx_h"][256:512], v["yx_l"][256:512]), (v["yx_h"][0:256], v["yx_l"][0:256])
            )
            high, low = split(eye - 0.5 * both)
            v["f_h"][...] = high
            v["f_l"][...] = low

        def step(_, carry):
            make_factor()
            high, low = split(
                dot3((v["yx_h"][...], v["yx_l"][...]), (v["f_h"][...], v["f_l"][...]))
            )
            v["yx_h"][...] = high
            v["yx_l"][...] = low
            return carry

        lax.fori_loop(0, NS_ITERS - 2, step, 0)
        make_factor()
        result = dot3((v["yx_h"][256:512], v["yx_l"][256:512]), (v["f_h"][...], v["f_l"][...]))
        high, low = split(result)
        v["x_h"][level] = high
        v["x_l"][level] = low
        return 1.0 / jnp.sqrt(norm), result

    def root(level):
        return v["x_h"][level], v["x_l"][level]

    def exchange(i, device):
        return remote(v["swapped_pair"].at[i, core_rows], v["swapped_in"].at[i], device)

    def exchange_core(i, copy):
        copy.wait_recv()
        v["swapped_sum"][i, core_rows] = v["swapped_pair"][i, core_rows] + v["swapped_in"][i]
        return remote(v["swapped_sum"].at[i, core_rows], v["swapped_sum"].at[i, core_rows], partner)

    with jax.named_scope("leaf"):
        scale_leaf, x_leaf = inverse_root(0, v["full"][0])
        sum_n = sum_last(1, sum_n)
        sum_o = sum_last(2, sum_o)
        root_high, root_low = split(x_leaf * scale_leaf)
        v["root_v"][0] = root_high
        v["root_v"][1] = root_low
        root_copy = local(v["root_v"], root_hbm)
        w_core.wait_recv()
        v["w_chip"][...] = v["wpart"][c] + v["w_core"][...]
        w_copies = [
            remote(v["w_chip"].at[d], v["w_in"].at[o], chip(d))
            for o, d in enumerate((xr, opposite, xl))
        ]
        arrived(sum_n)
        zp = dot3(root(0), split(v["full"][1])) * scale_leaf
        put(0, zp)
        t_high, t_low = split(zp.T)
        v["t_h"][...] = t_high
        v["t_l"][...] = t_low
        v["swapped_pair"][0] = dot3(transposed(), get(0))
        gram_copy = exchange(0, sibling)
        z_right = remote(v["z_own"], z_hbm.at[s], chip(xr))
        z_left = remote(v["z_own"], z_hbm.at[s], chip(xl))
        z_partner = remote(v["z_own"], z_hbm.at[s], partner)
        arrived(sum_o)
        put(5, dot3(root(0), split(v["full"][2])) * scale_leaf)
        v["swapped_pair"][1] = dot3(transposed(), get(5))
        cross_copy = exchange(1, sibling)
        arrived(w_copies)
        v["wcol"][c] = v["w_chip"][x] + v["w_in"][0] + v["w_in"][1] + v["w_in"][2]
        wcol_copy = remote(v["wcol"].at[c], v["wcol"].at[c], partner)
        gram_copy = exchange_core(0, gram_copy)
        wcol_copy.wait_recv()
        coarse = dot3(root(0), split(v["wcol"][...].reshape(256, 128))) * scale_leaf
        v["wc"][0] = dot3(transposed(), split(coarse))
        wc_copy = remote(v["wc"].at[0], v["wc_in"].at[0], sibling)
        gram_copy.wait_recv()
    with jax.named_scope("pair"):
        scale_pair, _ = inverse_root(1, v["swapped_sum"][0])
        cross_copy = exchange_core(1, cross_copy)
        put(2, dot3(get(0), root(1)) * scale_pair)
        cross_copy.wait_recv()
        zq = dot3(root(1), split(v["swapped_sum"][1])) * scale_pair
        put(1, zq)
        t_high, t_low = split(zq.T)
        v["t_h"][...] = t_high
        v["t_l"][...] = t_low
        v["swapped_pair"][2] = dot3(transposed(), get(1))
        gram_copy = exchange(2, cousin)
        put(4, dot3(get(2), get(1)))
        wc_copy.wait_recv()
        middle = dot3(root(1), split(v["wc"][0] + v["wc_in"][0])) * scale_pair
        v["wc"][1] = dot3(transposed(), split(middle))
        wc_copy = remote(v["wc"].at[1], v["wc_in"].at[1], cousin)
        z_right.wait_recv()
        from_left = 2 * xl + c
        round_right = remote(
            z_hbm.at[from_left, :, 0:128], z_hbm.at[from_left, :, 0:128], chip(xr)
        )
        z_left.wait_recv()
        from_right = 2 * xr + c
        round_left = remote(
            z_hbm.at[from_right, :, 128:256], z_hbm.at[from_right, :, 128:256], chip(xl)
        )
        handed_z = [
            remote(z_hbm.at[from_left], z_hbm.at[from_left], partner),
            remote(z_hbm.at[from_right], z_hbm.at[from_right], partner),
        ]
        gram_copy = exchange_core(2, gram_copy)
        arrived([round_right, round_left])
        from_far = 2 * opposite + c
        handed_z.append(remote(z_hbm.at[from_far], z_hbm.at[from_far], partner))
        gram_copy.wait_recv()
    with jax.named_scope("quad"):
        scale_quad, _ = inverse_root(2, v["swapped_sum"][2])
        nested = dot3(get(4), root(2)) * scale_quad
        v["nested_v"][...] = nested
        nested_copy = local(v["nested_v"], nested_hbm)
        wc_copy.wait_recv()
        summary = dot3(root(2), split(v["wc"][1] + v["wc_in"][1])) * scale_quad
        inner = dot3(split(nested), split(summary))
        inner_high, inner_low = split(
            dot3((v["root_v"][0], v["root_v"][1]), split(inner))
        )
        v["xi_v"][0] = inner_high
        v["xi_v"][1] = inner_low
        inner_copy = local(v["xi_v"], inner_hbm)
        arrived([z_partner] + handed_z)
        for copy in (z_local, root_copy, nested_copy, inner_copy):
            copy.wait()
        assert len(sent) <= N_COPIES and len(locals_) <= 12
        for copy in sent:
            copy.wait_send()


def outputs(z_ref, root_ref, nested_ref, inner_ref, basis_out, nested_out, approx_out, turned):
    core = lax.rem(lax.axis_index("samp"), 2)
    for i in range(2):
        rows = pl.ds(256 * i, 256)
        z = z_ref[i, 0], z_ref[i, 1]
        basis_out[rows] = dot3(z, (root_ref[0], root_ref[1]))
        turned[i] = dot3(z, (inner_ref[0], inner_ref[1])).T
        approx_out[:, rows] = turned[i, pl.ds(pl.multiple_of(core * 64, 64), 64)]
    nested_out[...] = nested_ref[...]


def on_device(n_rows, coupling_tiles, tile_columns, sample_matrix, phi_leaf, phi_pair, phi_quad):
    rows = sample_matrix.shape[0]
    share = sample_matrix.shape[1] // SAMP
    any_ = pl.BlockSpec(memory_space=pl.ANY)
    z, root, nested, inner = pl.pallas_call(
        functools.partial(kernel, n_rows),
        out_shape=(
            jax.ShapeDtypeStruct((SAMP, 2, RANK, RANK), BF16),
            jax.ShapeDtypeStruct((2, RANK, RANK), BF16),
            jax.ShapeDtypeStruct((RANK, RANK), F32),
            jax.ShapeDtypeStruct((2, RANK, 128), BF16),
        ),
        in_specs=[any_] * 6,
        out_specs=(any_,) * 4,
        scratch_shapes=list(SCRATCH.values()),
        compiler_params=pltpu.CompilerParams(
            collective_id=0, has_side_effects=True, vmem_limit_bytes=61 * 2**20
        ),
        name="hss",
    )(
        coupling_tiles,
        tile_columns.T,
        sample_matrix.reshape(16, 128, 512),
        phi_leaf,
        phi_pair,
        phi_quad,
    )
    basis, nested, approx_t = pl.pallas_call(
        outputs,
        grid=(SAMP // 2,),
        out_shape=(
            jax.ShapeDtypeStruct((rows, RANK), F32),
            jax.ShapeDtypeStruct((RANK, RANK), F32),
            jax.ShapeDtypeStruct((share, rows), F32),
        ),
        in_specs=[
            pl.BlockSpec((2, 2, RANK, RANK), lambda i: (i, 0, 0, 0)),
            pl.BlockSpec((2, RANK, RANK), lambda i: (0, 0, 0)),
            pl.BlockSpec((RANK, RANK), lambda i: (0, 0)),
            pl.BlockSpec((2, RANK, 128), lambda i: (0, 0, 0)),
        ],
        out_specs=(
            pl.BlockSpec((2 * RANK, RANK), lambda i: (i, 0)),
            pl.BlockSpec((RANK, RANK), lambda i: (0, 0)),
            pl.BlockSpec((share, 2 * RANK), lambda i: (0, i)),
        ),
        scratch_shapes=[pltpu.VMEM((2, 128, RANK), F32)],
        compiler_params=pltpu.CompilerParams(vmem_limit_bytes=61 * 2**20),
        name="expand",
    )(z, root, nested, inner)
    return basis, nested, approx_t.T


def solution(mesh):
    return jax.shard_map(
        functools.partial(on_device, mesh.shape["rows"]),
        mesh=mesh,
        in_specs=(P("rows", "samp", None, None), P("rows", "samp"), P("rows", None), P(), P(), P()),
        out_specs=(P("rows", None), P("rows", None), P("rows", "samp")),
        check_vma=False,
    )
```

```python
import functools

import jax
import jax.numpy as jnp
from jax import lax
from jax.experimental import pallas as pl
from jax.experimental.pallas import tpu as pltpu
from jax.sharding import PartitionSpec as P

NS_ITERS = 5
MESH = pl.DeviceIdType.MESH
F32 = jnp.float32
BF16 = jnp.bfloat16
NT, NN = ((1,), (1,)), ((1,), (0,))

N_COPIES = 96
SAMP = 8
CHIPS = 4
RANK = 256

I16 = jnp.int16

SCRATCH = dict(
    ext=pltpu.VMEM((48, 128, 256), BF16),
    tiles=pltpu.VMEM((2, 16, 4, 128, 128), BF16),
    cols_in=pltpu.VMEM((4, 16), jnp.int32),
    cols=pltpu.SMEM((2, 4, 16), jnp.int32),
    phi=pltpu.VMEM((3, 512, 256), F32),
    phi_h=pltpu.VMEM((3, 512, 256), BF16),
    phi_l=pltpu.VMEM((3, 512, 256), BF16),
    part=pltpu.VMEM((2, 2, 128, 256), F32),
    code=pltpu.VMEM((6, 256, 256), I16),
    code_in=pltpu.VMEM((6, 256, 256), I16),
    unit=pltpu.VMEM((6, 8, 256), F32),
    unit_in=pltpu.VMEM((6, 8, 256), F32),
    swap=pltpu.VMEM((256, 256), F32),
    samp=pltpu.VMEM((2, 256, 256), F32),
    mine=pltpu.VMEM((3, 256, 256), F32),
    in_core=pltpu.VMEM((3, 128, 256), F32),
    chip=pltpu.VMEM((3, 128, 256), F32),
    in_chip=pltpu.VMEM((3, 128, 256), F32),
    two=pltpu.VMEM((3, 128, 256), F32),
    in_two=pltpu.VMEM((3, 128, 256), F32),
    full=pltpu.VMEM((3, 256, 256), F32),
    wpart=pltpu.VMEM((2, 4, 128, 128), F32),
    w_core=pltpu.VMEM((4, 128, 128), F32),
    w_chip=pltpu.VMEM((4, 128, 128), F32),
    w_in=pltpu.VMEM((3, 128, 128), F32),
    wcol=pltpu.VMEM((2, 128, 128), F32),
    z_own=pltpu.VMEM((2, 256, 256), BF16),
    yx_h=pltpu.VMEM((512, 256), BF16),
    yx_l=pltpu.VMEM((512, 256), BF16),
    f_h=pltpu.VMEM((256, 256), BF16),
    f_l=pltpu.VMEM((256, 256), BF16),
    x_h=pltpu.VMEM((3, 256, 256), BF16),
    x_l=pltpu.VMEM((3, 256, 256), BF16),
    a_h=pltpu.VMEM((6, 256, 256), BF16),
    a_l=pltpu.VMEM((6, 256, 256), BF16),
    t_h=pltpu.VMEM((256, 256), BF16),
    t_l=pltpu.VMEM((256, 256), BF16),
    swapped_pair=pltpu.VMEM((3, 256, 256), F32),
    swapped_in=pltpu.VMEM((3, 128, 256), F32),
    swapped_sum=pltpu.VMEM((3, 256, 256), F32),
    wc=pltpu.VMEM((2, 256, 128), F32),
    wc_in=pltpu.VMEM((2, 256, 128), F32),
    root_v=pltpu.VMEM((2, 256, 256), BF16),
    xi_v=pltpu.VMEM((2, 256, 128), BF16),
    nested_v=pltpu.VMEM((256, 256), F32),
    local=pltpu.SemaphoreType.DMA((12,)),
    send=pltpu.SemaphoreType.DMA((N_COPIES,)),
    recv=pltpu.SemaphoreType.DMA((N_COPIES,)),
)


def split(value):
    high = value.astype(BF16)
    return high, (value - high.astype(F32)).astype(BF16)


def dot3(a, b):
    left = jnp.concatenate([a[0], a[0], a[1]], axis=1)
    right = jnp.concatenate([b[0], b[1], b[0]], axis=0)
    return lax.dot_general(left, right, (NN, ((), ())), preferred_element_type=F32)


def dot3_nt(a, b):
    left = jnp.concatenate([a[0], a[0], a[1]], axis=1)
    right = jnp.concatenate([b[0], b[1], b[0]], axis=1)
    return lax.dot_general(left, right, (NT, ((), ())), preferred_element_type=F32)


def kernel(n_rows, *refs):
    tiles_hbm, cols_hbm, b_hbm, phi0_hbm, phi1_hbm, phi2_hbm = refs[:6]
    z_hbm, root_hbm, nested_hbm, inner_hbm = refs[6:10]
    v = dict(zip(SCRATCH, refs[10:]))

    r = lax.axis_index("rows")
    s = lax.axis_index("samp")
    x = lax.div(s, 2)
    c = lax.rem(s, 2)
    y = lax.rem(r, 4)
    xr, opposite, xl = (lax.rem(x + o, CHIPS) for o in (1, 2, 3))

    def chip(index):
        return (r, 2 * index + c)

    partner = (r, s + 1 - 2 * c)
    left = (lax.rem(r + n_rows - 1, n_rows), s)
    right = (lax.rem(r + 1, n_rows), s)
    sibling = (r + 1 - 2 * lax.rem(r, 2), s)
    cousin = (r + 3 - 2 * y, s)
    first_dim = x + 1 - 2 * lax.rem(x, 2)
    second_dim = 3 - x

    barrier = pltpu.get_barrier_semaphore()
    peers = [partner, chip(xr), chip(opposite), chip(xl), left, right, cousin]
    for peer in peers:
        pl.semaphore_signal(barrier, inc=1, device_id=peer, device_id_type=MESH)

    locals_ = []

    def local(src, dst):
        copy = pltpu.make_async_copy(src, dst, v["local"].at[len(locals_)])
        locals_.append(copy)
        copy.start()
        return copy

    sent = []

    def remote(src, dst, device):
        i = len(sent)
        copy = pltpu.make_async_remote_copy(
            src_ref=src,
            dst_ref=dst,
            send_sem=v["send"].at[i],
            recv_sem=v["recv"].at[i],
            device_id=device,
            device_id_type=MESH,
        )
        sent.append(copy)
        copy.start()
        return copy

    mine_half = pl.ds(pl.multiple_of(c * 256, 256), 256)
    own_cols = local(cols_hbm, v["cols"].at[0])
    pl.semaphore_wait(barrier, len(peers))
    with jax.named_scope("halo"):
        direct = []
        for i in range(4):
            at = 4 * x + i
            piece = b_hbm.at[at, :, mine_half]
            direct.append(
                (
                    remote(piece, v["ext"].at[at], right),
                    remote(piece, v["ext"].at[32 + at], left),
                )
            )
        cols_copy = remote(cols_hbm, v["cols_in"], partner)
        far = pl.ds(4 * opposite, 4)
        far_copies = [
            remote(b_hbm.at[far, :, mine_half], v["ext"].at[far], right),
            remote(b_hbm.at[far, :, mine_half], v["ext"].at[pl.ds(32 + 4 * opposite, 4)], left),
        ]
        tiles_copy = remote(tiles_hbm, v["tiles"].at[1], partner)
        own_tiles = local(tiles_hbm, v["tiles"].at[0])
        own_b = local(b_hbm.at[:, :, mine_half], v["ext"].at[pl.ds(16, 16)])
        phis = [local(p, v["phi"].at[i]) for i, p in enumerate((phi0_hbm, phi1_hbm, phi2_hbm))]
        handed = []
        for i in range(4):
            for side in range(2):
                direct[i][side].wait_recv()
                piece = v["ext"].at[32 * side + 4 * x + i]
                handed.append(remote(piece, piece, chip(xr)))
                handed.append(remote(piece, piece, chip(xl)))
        for i, copy in enumerate(phis):
            copy.wait()
            high, low = split(v["phi"][i])
            v["phi_h"][i] = high
            v["phi_l"][i] = low
        cols_copy.wait_recv()
        other_cols = local(v["cols_in"], v["cols"].at[1])
        for copy in (own_cols, own_tiles, own_b, other_cols):
            copy.wait()
        for copy in [tiles_copy] + far_copies + handed:
            copy.wait_recv()
    first = (r - 1) * 16

    def product(slot, base):
        def tile_row(t, carry):
            row = base + t
            lhs = jnp.concatenate(
                [v["tiles"][h, row, k] for h in range(2) for k in range(4)], axis=1
            )
            rhs = jnp.concatenate(
                [
                    v["ext"][jnp.clip(v["cols"][h, k, row] - first, 0, 47)]
                    for h in range(2)
                    for k in range(4)
                ],
                axis=0,
            )
            v["part"][slot, t] = jnp.dot(lhs, rhs, preferred_element_type=F32)
            return carry

        lax.fori_loop(0, 2, tile_row, 0)
        return v["part"][slot].reshape(256, 256)

    def coded(i, value, device):
        top = jnp.maximum(jnp.max(jnp.abs(value), axis=1, keepdims=True), 1e-30)
        v["code"][i] = jnp.round(value * (32767.0 / top)).astype(jnp.int32).astype(I16)
        v["unit"][i] = jnp.broadcast_to(top * (1 / 32767.0), (256, 128)).T[0:8]
        return (
            remote(v["code"].at[i], v["code_in"].at[i], device),
            remote(v["unit"].at[i], v["unit_in"].at[i], device),
        )

    def decoded(i, copies):
        for copy in copies:
            copy.wait_recv()
        unit = jnp.broadcast_to(v["unit_in"][i, 0:1], (128, 256)).T
        return v["code_in"][i].astype(jnp.int32).astype(F32) * jnp.concatenate([unit, unit], axis=1)

    with jax.named_scope("product"):
        up_far = coded(0, product(0, 4 * opposite), chip(xr))
        down_far = coded(1, product(1, 4 * opposite + 2), chip(xl))
        down_near = coded(2, product(0, 4 * xr + 2), chip(xr))
        up_near = coded(3, product(1, 4 * xl), chip(xl))
        up_sum = coded(4, product(0, 4 * xr) + decoded(0, up_far), chip(xr))
        down_sum = coded(5, product(1, 4 * xl + 2) + decoded(1, down_far), chip(xl))
        product(0, 4 * x)
        product(1, 4 * x + 2)
        upper_in = decoded(3, up_near) + decoded(4, up_sum)
        lower_in = decoded(2, down_near) + decoded(5, down_sum)
        upper_half = v["part"][0].reshape(256, 256) + upper_in
        lower_half = v["part"][1].reshape(256, 256) + lower_in
        v["swap"][...] = jnp.where(c == 0, lower_half, upper_half)
        swapped = remote(v["swap"], v["samp"].at[c], partner)
        v["samp"][c] = jnp.where(c == 0, upper_half, lower_half)
        swapped.wait_recv()
    def put(slot, value):
        high, low = split(value)
        v["a_h"][slot] = high
        v["a_l"][slot] = low

    def get(slot):
        return v["a_h"][slot], v["a_l"][slot]

    def phi_of(i):
        return v["phi_h"][i], v["phi_l"][i]

    def transposed():
        return v["t_h"][...], v["t_l"][...]

    core_rows = pl.ds(pl.multiple_of(c * 128, 128), 128)
    other_rows = pl.ds(pl.multiple_of((1 - c) * 128, 128), 128)

    def sum_core(m):
        return [remote(v["mine"].at[m, other_rows], v["in_core"].at[m], partner)]

    def crossed(ref, into, m, one, two):
        return [
            remote(v[ref].at[m, 0:64], v[into].at[m, 0:64], chip(one)),
            remote(v[ref].at[m, 64:128], v[into].at[m, 64:128], chip(two)),
        ]

    def arrived(copies):
        for copy in copies:
            copy.wait_recv()

    def sum_first(m, copies):
        arrived(copies)
        v["chip"][m] = v["mine"][m, core_rows] + v["in_core"][m]
        return crossed("chip", "in_chip", m, first_dim, second_dim)

    def sum_second(m, copies):
        arrived(copies)
        v["two"][m] = v["chip"][m] + v["in_chip"][m]
        return crossed("two", "in_two", m, second_dim, first_dim)

    def sum_last(m, copies):
        arrived(copies)
        v["full"][m, core_rows] = v["two"][m] + v["in_two"][m]
        return [remote(v["full"].at[m, core_rows], v["full"].at[m, core_rows], partner)]

    with jax.named_scope("sums"):
        for half in range(2):
            put(half, v["samp"][half])
        sample = (
            jnp.concatenate([v["a_h"][0], v["a_h"][1]], axis=1),
            jnp.concatenate([v["a_l"][0], v["a_l"][1]], axis=1),
        )
        z = dot3(sample, phi_of(0))
        z_high, z_low = split(z)
        v["z_own"][0] = z_high
        v["z_own"][1] = z_low
        t_high, t_low = split(z.T)
        v["t_h"][...] = t_high
        v["t_l"][...] = t_low
        v["mine"][0] = dot3(transposed(), (v["z_own"][0], v["z_own"][1]))
        sum_g = sum_core(0)
        z_local = local(v["z_own"], z_hbm.at[s])
        for half in range(2):
            w = dot3(transposed(), get(half))
            put(3 + half, w)
            for q in range(4):
                v["wpart"][q // 2, 2 * half + q % 2] = w[
                    128 * (q // 2) : 128 * (q // 2) + 128, 128 * (q % 2) : 128 * (q % 2) + 128
                ]
        sum_g = sum_first(0, sum_g)
        w_all = (
            jnp.concatenate([v["a_h"][3], v["a_h"][4]], axis=1),
            jnp.concatenate([v["a_l"][3], v["a_l"][4]], axis=1),
        )
        v["mine"][1] = dot3(w_all, phi_of(1))
        sum_n = sum_core(1)
        v["mine"][2] = dot3(w_all, phi_of(2))
        sum_o = sum_core(2)
        w_core = remote(v["wpart"].at[1 - c], v["w_core"], partner)
        sum_n = sum_first(1, sum_n)
        sum_g = sum_second(0, sum_g)
        sum_o = sum_first(2, sum_o)
        sum_n = sum_second(1, sum_n)
        sum_o = sum_second(2, sum_o)
        sum_g = sum_last(0, sum_g)
        w_core.wait_recv()
        v["w_chip"][...] = v["wpart"][c] + v["w_core"][...]
        w_copies = [
            remote(v["w_chip"].at[d], v["w_in"].at[o], chip(d))
            for o, d in enumerate((xr, opposite, xl))
        ]
        arrived(sum_g)
    eye = jnp.where(
        lax.broadcasted_iota(jnp.int32, (RANK, RANK), 0)
        == lax.broadcasted_iota(jnp.int32, (RANK, RANK), 1),
        F32(1.5),
        F32(0),
    )

    def inverse_root(level, gram, meanwhile):
        norm = (
            jnp.sqrt(
                jnp.sum(jnp.sum(gram * gram, axis=1, keepdims=True), axis=0, keepdims=True)
            )
            + 1e-06
        )
        y0 = gram / norm
        factor = split(eye - 0.5 * y0)
        new_high, new_low = split(dot3(split(y0), factor))
        v["yx_h"][0:256] = new_high
        v["yx_l"][0:256] = new_low
        v["yx_h"][256:512] = factor[0]
        v["yx_l"][256:512] = factor[1]

        def make_factor():
            both = dot3(
                (v["yx_h"][256:512], v["yx_l"][256:512]), (v["yx_h"][0:256], v["yx_l"][0:256])
            )
            high, low = split(eye - 0.5 * both)
            v["f_h"][...] = high
            v["f_l"][...] = low

        def step(_, carry):
            make_factor()
            high, low = split(
                dot3((v["yx_h"][...], v["yx_l"][...]), (v["f_h"][...], v["f_l"][...]))
            )
            v["yx_h"][...] = high
            v["yx_l"][...] = low
            return carry

        step(0, 0)
        passed_on = meanwhile()
        lax.fori_loop(0, NS_ITERS - 3, step, 0)
        make_factor()
        result = dot3((v["yx_h"][256:512], v["yx_l"][256:512]), (v["f_h"][...], v["f_l"][...]))
        high, low = split(result)
        v["x_h"][level] = high
        v["x_l"][level] = low
        return 1.0 / jnp.sqrt(norm), result, passed_on

    def root(level):
        return v["x_h"][level], v["x_l"][level]

    def exchange(i, device):
        return remote(v["swapped_pair"].at[i, core_rows], v["swapped_in"].at[i], device)

    def exchange_core(i, copy):
        copy.wait_recv()
        v["swapped_sum"][i, core_rows] = v["swapped_pair"][i, core_rows] + v["swapped_in"][i]
        return remote(v["swapped_sum"].at[i, core_rows], v["swapped_sum"].at[i, core_rows], partner)

    with jax.named_scope("leaf"):
        scale_leaf, x_leaf, (sum_n, sum_o) = inverse_root(
            0, v["full"][0], lambda: (sum_last(1, sum_n), sum_last(2, sum_o))
        )
        arrived(sum_n)
        zp = dot3(root(0), split(v["full"][1])) * scale_leaf
        put(0, zp)
        t_high, t_low = split(zp.T)
        v["t_h"][...] = t_high
        v["t_l"][...] = t_low
        v["swapped_pair"][0] = dot3(transposed(), get(0))
        gram_copy = exchange(0, sibling)
        arrived(sum_o)
        put(5, dot3(root(0), split(v["full"][2])) * scale_leaf)
        v["swapped_pair"][1] = dot3(transposed(), get(5))
        cross_copy = exchange(1, sibling)
        z_right = remote(v["z_own"], z_hbm.at[s], chip(xr))
        z_left = remote(v["z_own"], z_hbm.at[s], chip(xl))
        z_partner = remote(v["z_own"], z_hbm.at[s], partner)
        root_high, root_low = split(x_leaf * scale_leaf)
        v["root_v"][0] = root_high
        v["root_v"][1] = root_low
        root_copy = local(v["root_v"], root_hbm)
        gram_copy = exchange_core(0, gram_copy)
        arrived(w_copies)
        v["wcol"][c] = v["w_chip"][x] + v["w_in"][0] + v["w_in"][1] + v["w_in"][2]
        wcol_copy = remote(v["wcol"].at[c], v["wcol"].at[c], partner)
        wcol_copy.wait_recv()
        coarse = dot3(root(0), split(v["wcol"][...].reshape(256, 128))) * scale_leaf
        v["wc"][0] = dot3(transposed(), split(coarse))
        wc_copy = remote(v["wc"].at[0], v["wc_in"].at[0], sibling)
        gram_copy.wait_recv()
    with jax.named_scope("pair"):
        scale_pair, _, cross_copy = inverse_root(
            1, v["swapped_sum"][0], lambda: exchange_core(1, cross_copy)
        )
        put(2, dot3(get(0), root(1)) * scale_pair)
        cross_copy.wait_recv()
        zq = dot3(root(1), split(v["swapped_sum"][1])) * scale_pair
        put(1, zq)
        t_high, t_low = split(zq.T)
        v["t_h"][...] = t_high
        v["t_l"][...] = t_low
        v["swapped_pair"][2] = dot3(transposed(), get(1))
        gram_copy = exchange(2, cousin)
        put(4, dot3(get(2), get(1)))
        wc_copy.wait_recv()
        middle = dot3(root(1), split(v["wc"][0] + v["wc_in"][0])) * scale_pair
        v["wc"][1] = dot3(transposed(), split(middle))
        wc_copy = remote(v["wc"].at[1], v["wc_in"].at[1], cousin)
        z_right.wait_recv()
        from_left = 2 * xl + c
        round_right = remote(
            z_hbm.at[from_left, :, 0:128], z_hbm.at[from_left, :, 0:128], chip(xr)
        )
        z_left.wait_recv()
        from_right = 2 * xr + c
        round_left = remote(
            z_hbm.at[from_right, :, 128:256], z_hbm.at[from_right, :, 128:256], chip(xl)
        )
        handed_z = [
            remote(z_hbm.at[from_left], z_hbm.at[from_left], partner),
            remote(z_hbm.at[from_right], z_hbm.at[from_right], partner),
        ]
        gram_copy = exchange_core(2, gram_copy)
        gram_copy.wait_recv()
    with jax.named_scope("quad"):
        def far_z():
            arrived([round_right, round_left])
            from_far = 2 * opposite + c
            return remote(z_hbm.at[from_far], z_hbm.at[from_far], partner)

        scale_quad, _, far_copy = inverse_root(2, v["swapped_sum"][2], far_z)
        handed_z.append(far_copy)
        nested = dot3(get(4), root(2)) * scale_quad
        v["nested_v"][...] = nested
        nested_copy = local(v["nested_v"], nested_hbm)
        wc_copy.wait_recv()
        summary = dot3(root(2), split(v["wc"][1] + v["wc_in"][1])) * scale_quad
        inner = dot3(split(nested), split(summary))
        inner_high, inner_low = split(
            dot3((v["root_v"][0], v["root_v"][1]), split(inner))
        )
        v["xi_v"][0] = inner_high
        v["xi_v"][1] = inner_low
        inner_copy = local(v["xi_v"], inner_hbm)
        arrived([z_partner] + handed_z)
        for copy in (z_local, root_copy, nested_copy, inner_copy):
            copy.wait()
        assert len(sent) <= N_COPIES and len(locals_) <= 12
        for copy in sent:
            copy.wait_send()


def outputs(z_ref, root_ref, nested_ref, inner_ref, basis_out, nested_out, approx_out, turned):
    core = lax.rem(lax.axis_index("samp"), 2)
    for i in range(2):
        rows = pl.ds(256 * i, 256)
        z = z_ref[i, 0], z_ref[i, 1]
        basis_out[rows] = dot3(z, (root_ref[0], root_ref[1]))
        turned[i] = dot3(z, (inner_ref[0], inner_ref[1])).T
        approx_out[:, rows] = turned[i, pl.ds(pl.multiple_of(core * 64, 64), 64)]
    nested_out[...] = nested_ref[...]


def on_device(n_rows, coupling_tiles, tile_columns, sample_matrix, phi_leaf, phi_pair, phi_quad):
    rows = sample_matrix.shape[0]
    share = sample_matrix.shape[1] // SAMP
    any_ = pl.BlockSpec(memory_space=pl.ANY)
    z, root, nested, inner = pl.pallas_call(
        functools.partial(kernel, n_rows),
        out_shape=(
            jax.ShapeDtypeStruct((SAMP, 2, RANK, RANK), BF16),
            jax.ShapeDtypeStruct((2, RANK, RANK), BF16),
            jax.ShapeDtypeStruct((RANK, RANK), F32),
            jax.ShapeDtypeStruct((2, RANK, 128), BF16),
        ),
        in_specs=[any_] * 6,
        out_specs=(any_,) * 4,
        scratch_shapes=list(SCRATCH.values()),
        compiler_params=pltpu.CompilerParams(
            collective_id=0, has_side_effects=True, vmem_limit_bytes=61 * 2**20
        ),
        name="hss",
    )(
        coupling_tiles,
        tile_columns.T,
        sample_matrix.reshape(16, 128, 512),
        phi_leaf,
        phi_pair,
        phi_quad,
    )
    basis, nested, approx_t = pl.pallas_call(
        outputs,
        grid=(SAMP // 2,),
        out_shape=(
            jax.ShapeDtypeStruct((rows, RANK), F32),
            jax.ShapeDtypeStruct((RANK, RANK), F32),
            jax.ShapeDtypeStruct((share, rows), F32),
        ),
        in_specs=[
            pl.BlockSpec((2, 2, RANK, RANK), lambda i: (i, 0, 0, 0)),
            pl.BlockSpec((2, RANK, RANK), lambda i: (0, 0, 0)),
            pl.BlockSpec((RANK, RANK), lambda i: (0, 0)),
            pl.BlockSpec((2, RANK, 128), lambda i: (0, 0, 0)),
        ],
        out_specs=(
            pl.BlockSpec((2 * RANK, RANK), lambda i: (i, 0)),
            pl.BlockSpec((RANK, RANK), lambda i: (0, 0)),
            pl.BlockSpec((share, 2 * RANK), lambda i: (0, i)),
        ),
        scratch_shapes=[pltpu.VMEM((2, 128, RANK), F32)],
        compiler_params=pltpu.CompilerParams(vmem_limit_bytes=61 * 2**20),
        name="expand",
    )(z, root, nested, inner)
    return basis, nested, approx_t.T


def solution(mesh):
    return jax.shard_map(
        functools.partial(on_device, mesh.shape["rows"]),
        mesh=mesh,
        in_specs=(P("rows", "samp", None, None), P("rows", "samp"), P("rows", None), P(), P(), P()),
        out_specs=(P("rows", None), P("rows", None), P("rows", "samp")),
        check_vma=False,
    )
```

```python
import functools

import jax
import jax.numpy as jnp
from jax import lax
from jax.experimental import pallas as pl
from jax.experimental.pallas import tpu as pltpu
from jax.sharding import PartitionSpec as P

NS_ITERS = 5
MESH = pl.DeviceIdType.MESH
F32 = jnp.float32
BF16 = jnp.bfloat16
NT, NN = ((1,), (1,)), ((1,), (0,))

N_COPIES = 96
SAMP = 8
CHIPS = 4
RANK = 256

I16 = jnp.int16

SCRATCH = dict(
    ext=pltpu.VMEM((48, 128, 256), BF16),
    tiles=pltpu.VMEM((2, 16, 4, 128, 128), BF16),
    cols_in=pltpu.VMEM((4, 16), jnp.int32),
    cols=pltpu.SMEM((2, 4, 16), jnp.int32),
    phi=pltpu.VMEM((3, 512, 256), F32),
    phi_h=pltpu.VMEM((3, 512, 256), BF16),
    phi_l=pltpu.VMEM((3, 512, 256), BF16),
    part=pltpu.VMEM((2, 2, 128, 256), F32),
    code=pltpu.VMEM((6, 256, 256), I16),
    code_in=pltpu.VMEM((6, 256, 256), I16),
    unit=pltpu.VMEM((6, 8, 256), F32),
    unit_in=pltpu.VMEM((6, 8, 256), F32),
    swap=pltpu.VMEM((256, 256), F32),
    samp=pltpu.VMEM((2, 256, 256), F32),
    mine=pltpu.VMEM((3, 256, 256), F32),
    in_core=pltpu.VMEM((3, 128, 256), F32),
    chip=pltpu.VMEM((3, 128, 256), F32),
    in_chip=pltpu.VMEM((3, 128, 256), F32),
    two=pltpu.VMEM((3, 128, 256), F32),
    in_two=pltpu.VMEM((3, 128, 256), F32),
    full=pltpu.VMEM((3, 256, 256), F32),
    wpart=pltpu.VMEM((2, 4, 128, 128), F32),
    w_core=pltpu.VMEM((4, 128, 128), F32),
    w_chip=pltpu.VMEM((4, 128, 128), F32),
    w_in=pltpu.VMEM((3, 128, 128), F32),
    wcol=pltpu.VMEM((2, 128, 128), F32),
    z_own=pltpu.VMEM((2, 256, 256), BF16),
    yx_h=pltpu.VMEM((512, 256), BF16),
    yx_l=pltpu.VMEM((512, 256), BF16),
    f_h=pltpu.VMEM((256, 256), BF16),
    f_l=pltpu.VMEM((256, 256), BF16),
    x_h=pltpu.VMEM((3, 256, 256), BF16),
    x_l=pltpu.VMEM((3, 256, 256), BF16),
    a_h=pltpu.VMEM((6, 256, 256), BF16),
    a_l=pltpu.VMEM((6, 256, 256), BF16),
    t_h=pltpu.VMEM((256, 256), BF16),
    t_l=pltpu.VMEM((256, 256), BF16),
    swapped_pair=pltpu.VMEM((3, 256, 256), F32),
    swapped_in=pltpu.VMEM((3, 128, 256), F32),
    swapped_sum=pltpu.VMEM((3, 256, 256), F32),
    wc=pltpu.VMEM((2, 256, 128), F32),
    wc_in=pltpu.VMEM((2, 256, 128), F32),
    root_v=pltpu.VMEM((2, 256, 256), BF16),
    xi_v=pltpu.VMEM((2, 256, 128), BF16),
    nested_v=pltpu.VMEM((256, 256), F32),
    local=pltpu.SemaphoreType.DMA((12,)),
    send=pltpu.SemaphoreType.DMA((N_COPIES,)),
    recv=pltpu.SemaphoreType.DMA((N_COPIES,)),
)


def split(value):
    high = value.astype(BF16)
    return high, (value - high.astype(F32)).astype(BF16)


def dot3(a, b):
    left = jnp.concatenate([a[0], a[0], a[1]], axis=1)
    right = jnp.concatenate([b[0], b[1], b[0]], axis=0)
    return lax.dot_general(left, right, (NN, ((), ())), preferred_element_type=F32)


def dot3_nt(a, b):
    left = jnp.concatenate([a[0], a[0], a[1]], axis=1)
    right = jnp.concatenate([b[0], b[1], b[0]], axis=1)
    return lax.dot_general(left, right, (NT, ((), ())), preferred_element_type=F32)


def kernel(n_rows, *refs):
    tiles_hbm, cols_hbm, b_hbm, phi0_hbm, phi1_hbm, phi2_hbm = refs[:6]
    z_hbm, root_hbm, nested_hbm, inner_hbm = refs[6:10]
    v = dict(zip(SCRATCH, refs[10:]))

    r = lax.axis_index("rows")
    s = lax.axis_index("samp")
    x = lax.div(s, 2)
    c = lax.rem(s, 2)
    y = lax.rem(r, 4)
    xr, opposite, xl = (lax.rem(x + o, CHIPS) for o in (1, 2, 3))

    def chip(index):
        return (r, 2 * index + c)

    partner = (r, s + 1 - 2 * c)
    left = (lax.rem(r + n_rows - 1, n_rows), s)
    right = (lax.rem(r + 1, n_rows), s)
    sibling = (r + 1 - 2 * lax.rem(r, 2), s)
    cousin = (r + 3 - 2 * y, s)
    first_dim = x + 1 - 2 * lax.rem(x, 2)
    second_dim = 3 - x

    barrier = pltpu.get_barrier_semaphore()
    peers = [partner, chip(xr), chip(opposite), chip(xl), left, right, cousin]
    for peer in peers:
        pl.semaphore_signal(barrier, inc=1, device_id=peer, device_id_type=MESH)

    locals_ = []

    def local(src, dst):
        copy = pltpu.make_async_copy(src, dst, v["local"].at[len(locals_)])
        locals_.append(copy)
        copy.start()
        return copy

    sent = []

    def remote(src, dst, device):
        i = len(sent)
        copy = pltpu.make_async_remote_copy(
            src_ref=src,
            dst_ref=dst,
            send_sem=v["send"].at[i],
            recv_sem=v["recv"].at[i],
            device_id=device,
            device_id_type=MESH,
        )
        sent.append(copy)
        copy.start()
        return copy

    mine_half = pl.ds(pl.multiple_of(c * 256, 256), 256)
    own_cols = local(cols_hbm, v["cols"].at[0])
    pl.semaphore_wait(barrier, len(peers))
    with jax.named_scope("halo"):
        direct = []
        for i in range(4):
            at = 4 * x + i
            piece = b_hbm.at[at, :, mine_half]
            direct.append(
                (
                    remote(piece, v["ext"].at[at], right),
                    remote(piece, v["ext"].at[32 + at], left),
                )
            )
        cols_copy = remote(cols_hbm, v["cols_in"], partner)
        far = pl.ds(4 * opposite, 4)
        far_copies = [
            remote(b_hbm.at[far, :, mine_half], v["ext"].at[far], right),
            remote(b_hbm.at[far, :, mine_half], v["ext"].at[pl.ds(32 + 4 * opposite, 4)], left),
        ]
        tiles_copy = remote(tiles_hbm, v["tiles"].at[1], partner)
        own_tiles = local(tiles_hbm, v["tiles"].at[0])
        own_b = local(b_hbm.at[:, :, mine_half], v["ext"].at[pl.ds(16, 16)])
        phis = [local(p, v["phi"].at[i]) for i, p in enumerate((phi0_hbm, phi1_hbm, phi2_hbm))]
        handed = []
        for i in range(4):
            for side in range(2):
                direct[i][side].wait_recv()
                piece = v["ext"].at[32 * side + 4 * x + i]
                handed.append(remote(piece, piece, chip(xr)))
                handed.append(remote(piece, piece, chip(xl)))
        for i, copy in enumerate(phis):
            copy.wait()
            high, low = split(v["phi"][i])
            v["phi_h"][i] = high
            v["phi_l"][i] = low
        cols_copy.wait_recv()
        other_cols = local(v["cols_in"], v["cols"].at[1])
        for copy in (own_cols, own_tiles, own_b, other_cols):
            copy.wait()
        for copy in [tiles_copy] + far_copies + handed:
            copy.wait_recv()
    first = (r - 1) * 16

    def product(slot, base):
        def tile_row(t, carry):
            row = base + t
            lhs = jnp.concatenate(
                [v["tiles"][h, row, k] for h in range(2) for k in range(4)], axis=1
            )
            rhs = jnp.concatenate(
                [
                    v["ext"][jnp.clip(v["cols"][h, k, row] - first, 0, 47)]
                    for h in range(2)
                    for k in range(4)
                ],
                axis=0,
            )
            v["part"][slot, t] = jnp.dot(lhs, rhs, preferred_element_type=F32)
            return carry

        lax.fori_loop(0, 2, tile_row, 0)
        return v["part"][slot].reshape(256, 256)

    def coded(i, value, device):
        top = jnp.maximum(jnp.max(jnp.abs(value), axis=1, keepdims=True), 1e-30)
        v["code"][i] = jnp.round(value * (32767.0 / top)).astype(jnp.int32).astype(I16)
        v["unit"][i] = jnp.broadcast_to(top * (1 / 32767.0), (256, 128)).T[0:8]
        return (
            remote(v["code"].at[i], v["code_in"].at[i], device),
            remote(v["unit"].at[i], v["unit_in"].at[i], device),
        )

    def decoded(i, copies):
        for copy in copies:
            copy.wait_recv()
        unit = jnp.broadcast_to(v["unit_in"][i, 0:1], (128, 256)).T
        return v["code_in"][i].astype(jnp.int32).astype(F32) * jnp.concatenate([unit, unit], axis=1)

    with jax.named_scope("product"):
        up_far = coded(0, product(0, 4 * opposite), chip(xr))
        down_far = coded(1, product(1, 4 * opposite + 2), chip(xl))
        down_near = coded(2, product(0, 4 * xr + 2), chip(xr))
        up_near = coded(3, product(1, 4 * xl), chip(xl))
        up_sum = coded(4, product(0, 4 * xr) + decoded(0, up_far), chip(xr))
        down_sum = coded(5, product(1, 4 * xl + 2) + decoded(1, down_far), chip(xl))
        product(0, 4 * x)
        product(1, 4 * x + 2)
        upper_in = decoded(3, up_near) + decoded(4, up_sum)
        lower_in = decoded(2, down_near) + decoded(5, down_sum)
        upper_half = v["part"][0].reshape(256, 256) + upper_in
        lower_half = v["part"][1].reshape(256, 256) + lower_in
        v["swap"][...] = jnp.where(c == 0, lower_half, upper_half)
        swapped = remote(v["swap"], v["samp"].at[c], partner)
        v["samp"][c] = jnp.where(c == 0, upper_half, lower_half)
        swapped.wait_recv()
    def put(slot, value):
        high, low = split(value)
        v["a_h"][slot] = high
        v["a_l"][slot] = low

    def get(slot):
        return v["a_h"][slot], v["a_l"][slot]

    def phi_of(i):
        return v["phi_h"][i], v["phi_l"][i]

    def transposed():
        return v["t_h"][...], v["t_l"][...]

    core_rows = pl.ds(pl.multiple_of(c * 128, 128), 128)
    other_rows = pl.ds(pl.multiple_of((1 - c) * 128, 128), 128)

    def sum_core(m):
        return [remote(v["mine"].at[m, other_rows], v["in_core"].at[m], partner)]

    def crossed(ref, into, m, one, two):
        return [
            remote(v[ref].at[m, 0:64], v[into].at[m, 0:64], chip(one)),
            remote(v[ref].at[m, 64:128], v[into].at[m, 64:128], chip(two)),
        ]

    def arrived(copies):
        for copy in copies:
            copy.wait_recv()

    def sum_first(m, copies):
        arrived(copies)
        v["chip"][m] = v["mine"][m, core_rows] + v["in_core"][m]
        return crossed("chip", "in_chip", m, first_dim, second_dim)

    def sum_second(m, copies):
        arrived(copies)
        v["two"][m] = v["chip"][m] + v["in_chip"][m]
        return crossed("two", "in_two", m, second_dim, first_dim)

    def sum_last(m, copies):
        arrived(copies)
        v["full"][m, core_rows] = v["two"][m] + v["in_two"][m]
        return [remote(v["full"].at[m, core_rows], v["full"].at[m, core_rows], partner)]

    with jax.named_scope("sums"):
        for half in range(2):
            put(half, v["samp"][half])
        sample = (
            jnp.concatenate([v["a_h"][0], v["a_h"][1]], axis=1),
            jnp.concatenate([v["a_l"][0], v["a_l"][1]], axis=1),
        )
        z = dot3(sample, phi_of(0))
        z_high, z_low = split(z)
        v["z_own"][0] = z_high
        v["z_own"][1] = z_low
        t_high, t_low = split(z.T)
        v["t_h"][...] = t_high
        v["t_l"][...] = t_low
        v["mine"][0] = dot3(transposed(), (v["z_own"][0], v["z_own"][1]))
        sum_g = sum_core(0)
        z_local = local(v["z_own"], z_hbm.at[s])
        for half in range(2):
            w = dot3(transposed(), get(half))
            put(3 + half, w)
            for q in range(4):
                v["wpart"][q // 2, 2 * half + q % 2] = w[
                    128 * (q // 2) : 128 * (q // 2) + 128, 128 * (q % 2) : 128 * (q % 2) + 128
                ]
        sum_g = sum_first(0, sum_g)
        w_all = (
            jnp.concatenate([v["a_h"][3], v["a_h"][4]], axis=1),
            jnp.concatenate([v["a_l"][3], v["a_l"][4]], axis=1),
        )
        v["mine"][1] = dot3(w_all, phi_of(1))
        sum_n = sum_core(1)
        v["mine"][2] = dot3(w_all, phi_of(2))
        sum_o = sum_core(2)
        w_core = remote(v["wpart"].at[1 - c], v["w_core"], partner)
        sum_n = sum_first(1, sum_n)
        sum_g = sum_second(0, sum_g)
        sum_o = sum_first(2, sum_o)
        sum_n = sum_second(1, sum_n)
        sum_o = sum_second(2, sum_o)
        sum_g = sum_last(0, sum_g)
        w_core.wait_recv()
        v["w_chip"][...] = v["wpart"][c] + v["w_core"][...]
        arrived(sum_g)
    eye = jnp.where(
        lax.broadcasted_iota(jnp.int32, (RANK, RANK), 0)
        == lax.broadcasted_iota(jnp.int32, (RANK, RANK), 1),
        F32(1.5),
        F32(0),
    )

    def inverse_root(level, gram, meanwhile):
        norm = (
            jnp.sqrt(
                jnp.sum(jnp.sum(gram * gram, axis=1, keepdims=True), axis=0, keepdims=True)
            )
            + 1e-06
        )
        y0 = gram / norm
        factor = split(eye - 0.5 * y0)
        new_high, new_low = split(dot3(split(y0), factor))
        v["yx_h"][0:256] = new_high
        v["yx_l"][0:256] = new_low
        v["yx_h"][256:512] = factor[0]
        v["yx_l"][256:512] = factor[1]

        def make_factor():
            both = dot3(
                (v["yx_h"][256:512], v["yx_l"][256:512]), (v["yx_h"][0:256], v["yx_l"][0:256])
            )
            high, low = split(eye - 0.5 * both)
            v["f_h"][...] = high
            v["f_l"][...] = low

        def step(_, carry):
            make_factor()
            high, low = split(
                dot3((v["yx_h"][...], v["yx_l"][...]), (v["f_h"][...], v["f_l"][...]))
            )
            v["yx_h"][...] = high
            v["yx_l"][...] = low
            return carry

        step(0, 0)
        passed_on = meanwhile()
        lax.fori_loop(0, NS_ITERS - 3, step, 0)
        make_factor()
        result = dot3((v["yx_h"][256:512], v["yx_l"][256:512]), (v["f_h"][...], v["f_l"][...]))
        high, low = split(result)
        v["x_h"][level] = high
        v["x_l"][level] = low
        return 1.0 / jnp.sqrt(norm), result, passed_on

    def root(level):
        return v["x_h"][level], v["x_l"][level]

    def exchange(i, device):
        return remote(v["swapped_pair"].at[i, core_rows], v["swapped_in"].at[i], device)

    def exchange_core(i, copy):
        copy.wait_recv()
        v["swapped_sum"][i, core_rows] = v["swapped_pair"][i, core_rows] + v["swapped_in"][i]
        return remote(v["swapped_sum"].at[i, core_rows], v["swapped_sum"].at[i, core_rows], partner)

    with jax.named_scope("leaf"):

        def last_sums():
            last_n, last_o = sum_last(1, sum_n), sum_last(2, sum_o)
            columns = [
                remote(v["w_chip"].at[d], v["w_in"].at[o], chip(d))
                for o, d in enumerate((xr, opposite, xl))
            ]
            return last_n, last_o, columns

        scale_leaf, x_leaf, (sum_n, sum_o, w_copies) = inverse_root(0, v["full"][0], last_sums)
        arrived(sum_n)
        zp = dot3(root(0), split(v["full"][1])) * scale_leaf
        put(0, zp)
        t_high, t_low = split(zp.T)
        v["t_h"][...] = t_high
        v["t_l"][...] = t_low
        v["swapped_pair"][0] = dot3(transposed(), get(0))
        gram_copy = exchange(0, sibling)
        z_right = remote(v["z_own"], z_hbm.at[s], chip(xr))
        z_left = remote(v["z_own"], z_hbm.at[s], chip(xl))
        z_partner = remote(v["z_own"], z_hbm.at[s], partner)
        arrived(sum_o)
        put(5, dot3(root(0), split(v["full"][2])) * scale_leaf)
        v["swapped_pair"][1] = dot3(transposed(), get(5))
        cross_copy = exchange(1, sibling)
        root_high, root_low = split(x_leaf * scale_leaf)
        v["root_v"][0] = root_high
        v["root_v"][1] = root_low
        root_copy = local(v["root_v"], root_hbm)
        gram_copy = exchange_core(0, gram_copy)
        arrived(w_copies)
        v["wcol"][c] = v["w_chip"][x] + v["w_in"][0] + v["w_in"][1] + v["w_in"][2]
        wcol_copy = remote(v["wcol"].at[c], v["wcol"].at[c], partner)
        wcol_copy.wait_recv()
        coarse = dot3(root(0), split(v["wcol"][...].reshape(256, 128))) * scale_leaf
        v["wc"][0] = dot3(transposed(), split(coarse))
        wc_copy = remote(v["wc"].at[0], v["wc_in"].at[0], sibling)
        gram_copy.wait_recv()
    with jax.named_scope("pair"):
        scale_pair, _, cross_copy = inverse_root(
            1, v["swapped_sum"][0], lambda: exchange_core(1, cross_copy)
        )
        put(2, dot3(get(0), root(1)) * scale_pair)
        cross_copy.wait_recv()
        zq = dot3(root(1), split(v["swapped_sum"][1])) * scale_pair
        put(1, zq)
        t_high, t_low = split(zq.T)
        v["t_h"][...] = t_high
        v["t_l"][...] = t_low
        v["swapped_pair"][2] = dot3(transposed(), get(1))
        gram_copy = exchange(2, cousin)
        put(4, dot3(get(2), get(1)))
        wc_copy.wait_recv()
        middle = dot3(root(1), split(v["wc"][0] + v["wc_in"][0])) * scale_pair
        v["wc"][1] = dot3(transposed(), split(middle))
        wc_copy = remote(v["wc"].at[1], v["wc_in"].at[1], cousin)
        z_right.wait_recv()
        from_left = 2 * xl + c
        round_right = remote(
            z_hbm.at[from_left, :, 0:128], z_hbm.at[from_left, :, 0:128], chip(xr)
        )
        z_left.wait_recv()
        from_right = 2 * xr + c
        round_left = remote(
            z_hbm.at[from_right, :, 128:256], z_hbm.at[from_right, :, 128:256], chip(xl)
        )
        handed_z = [
            remote(z_hbm.at[from_left], z_hbm.at[from_left], partner),
            remote(z_hbm.at[from_right], z_hbm.at[from_right], partner),
        ]
        gram_copy = exchange_core(2, gram_copy)
        gram_copy.wait_recv()
    with jax.named_scope("quad"):
        scale_quad, _, _ = inverse_root(2, v["swapped_sum"][2], lambda: None)
        arrived([round_right, round_left])
        from_far = 2 * opposite + c
        handed_z.append(remote(z_hbm.at[from_far], z_hbm.at[from_far], partner))
        nested = dot3(get(4), root(2)) * scale_quad
        v["nested_v"][...] = nested
        nested_copy = local(v["nested_v"], nested_hbm)
        wc_copy.wait_recv()
        summary = dot3(root(2), split(v["wc"][1] + v["wc_in"][1])) * scale_quad
        inner = dot3(split(nested), split(summary))
        inner_high, inner_low = split(
            dot3((v["root_v"][0], v["root_v"][1]), split(inner))
        )
        v["xi_v"][0] = inner_high
        v["xi_v"][1] = inner_low
        inner_copy = local(v["xi_v"], inner_hbm)
        arrived([z_partner] + handed_z)
        for copy in (z_local, root_copy, nested_copy, inner_copy):
            copy.wait()
        assert len(sent) <= N_COPIES and len(locals_) <= 12
        for copy in sent:
            copy.wait_send()


def outputs(z_ref, root_ref, nested_ref, inner_ref, basis_out, nested_out, approx_out, turned):
    core = lax.rem(lax.axis_index("samp"), 2)
    for i in range(2):
        rows = pl.ds(256 * i, 256)
        z = z_ref[i, 0], z_ref[i, 1]
        basis_out[rows] = dot3(z, (root_ref[0], root_ref[1]))
        turned[i] = dot3(z, (inner_ref[0], inner_ref[1])).T
        approx_out[:, rows] = turned[i, pl.ds(pl.multiple_of(core * 64, 64), 64)]
    nested_out[...] = nested_ref[...]


def on_device(n_rows, coupling_tiles, tile_columns, sample_matrix, phi_leaf, phi_pair, phi_quad):
    rows = sample_matrix.shape[0]
    share = sample_matrix.shape[1] // SAMP
    any_ = pl.BlockSpec(memory_space=pl.ANY)
    z, root, nested, inner = pl.pallas_call(
        functools.partial(kernel, n_rows),
        out_shape=(
            jax.ShapeDtypeStruct((SAMP, 2, RANK, RANK), BF16),
            jax.ShapeDtypeStruct((2, RANK, RANK), BF16),
            jax.ShapeDtypeStruct((RANK, RANK), F32),
            jax.ShapeDtypeStruct((2, RANK, 128), BF16),
        ),
        in_specs=[any_] * 6,
        out_specs=(any_,) * 4,
        scratch_shapes=list(SCRATCH.values()),
        compiler_params=pltpu.CompilerParams(
            collective_id=0, has_side_effects=True, vmem_limit_bytes=61 * 2**20
        ),
        name="hss",
    )(
        coupling_tiles,
        tile_columns.T,
        sample_matrix.reshape(16, 128, 512),
        phi_leaf,
        phi_pair,
        phi_quad,
    )
    basis, nested, approx_t = pl.pallas_call(
        outputs,
        grid=(SAMP // 2,),
        out_shape=(
            jax.ShapeDtypeStruct((rows, RANK), F32),
            jax.ShapeDtypeStruct((RANK, RANK), F32),
            jax.ShapeDtypeStruct((share, rows), F32),
        ),
        in_specs=[
            pl.BlockSpec((2, 2, RANK, RANK), lambda i: (i, 0, 0, 0)),
            pl.BlockSpec((2, RANK, RANK), lambda i: (0, 0, 0)),
            pl.BlockSpec((RANK, RANK), lambda i: (0, 0)),
            pl.BlockSpec((2, RANK, 128), lambda i: (0, 0, 0)),
        ],
        out_specs=(
            pl.BlockSpec((2 * RANK, RANK), lambda i: (i, 0)),
            pl.BlockSpec((RANK, RANK), lambda i: (0, 0)),
            pl.BlockSpec((share, 2 * RANK), lambda i: (0, i)),
        ),
        scratch_shapes=[pltpu.VMEM((2, 128, RANK), F32)],
        compiler_params=pltpu.CompilerParams(vmem_limit_bytes=61 * 2**20),
        name="expand",
    )(z, root, nested, inner)
    return basis, nested, approx_t.T


def solution(mesh):
    return jax.shard_map(
        functools.partial(on_device, mesh.shape["rows"]),
        mesh=mesh,
        in_specs=(P("rows", "samp", None, None), P("rows", "samp"), P("rows", None), P(), P(), P()),
        out_specs=(P("rows", None), P("rows", None), P("rows", "samp")),
        check_vma=False,
    )
```

```python
import functools

import jax
import jax.numpy as jnp
from jax import lax
from jax.experimental import pallas as pl
from jax.experimental.pallas import tpu as pltpu
from jax.sharding import PartitionSpec as P

NS_ITERS = 5
MESH = pl.DeviceIdType.MESH
F32 = jnp.float32
BF16 = jnp.bfloat16
NT, NN = ((1,), (1,)), ((1,), (0,))

N_COPIES = 96
SAMP = 8
CHIPS = 4
RANK = 256

I16 = jnp.int16

SCRATCH = dict(
    ext=pltpu.VMEM((48, 128, 256), BF16),
    tiles=pltpu.VMEM((2, 16, 4, 128, 128), BF16),
    cols_in=pltpu.VMEM((4, 16), jnp.int32),
    cols=pltpu.SMEM((2, 4, 16), jnp.int32),
    phi=pltpu.VMEM((3, 512, 256), F32),
    phi_h=pltpu.VMEM((3, 512, 256), BF16),
    phi_l=pltpu.VMEM((3, 512, 256), BF16),
    part=pltpu.VMEM((2, 2, 128, 256), F32),
    code=pltpu.VMEM((6, 256, 256), I16),
    code_in=pltpu.VMEM((6, 256, 256), I16),
    unit=pltpu.VMEM((6, 8, 256), F32),
    unit_in=pltpu.VMEM((6, 8, 256), F32),
    swap=pltpu.VMEM((256, 256), F32),
    samp=pltpu.VMEM((2, 256, 256), F32),
    mine=pltpu.VMEM((3, 256, 256), F32),
    in_core=pltpu.VMEM((3, 128, 256), F32),
    chip=pltpu.VMEM((3, 128, 256), F32),
    in_chip=pltpu.VMEM((3, 128, 256), F32),
    two=pltpu.VMEM((3, 128, 256), F32),
    in_two=pltpu.VMEM((3, 128, 256), F32),
    full=pltpu.VMEM((3, 256, 256), F32),
    wpart=pltpu.VMEM((2, 4, 128, 128), F32),
    w_core=pltpu.VMEM((4, 128, 128), F32),
    w_chip=pltpu.VMEM((4, 128, 128), F32),
    w_in=pltpu.VMEM((3, 128, 128), F32),
    wcol=pltpu.VMEM((2, 128, 128), F32),
    z_own=pltpu.VMEM((2, 256, 256), BF16),
    yx_h=pltpu.VMEM((512, 256), BF16),
    yx_l=pltpu.VMEM((512, 256), BF16),
    f_h=pltpu.VMEM((256, 256), BF16),
    f_l=pltpu.VMEM((256, 256), BF16),
    x_h=pltpu.VMEM((3, 256, 256), BF16),
    x_l=pltpu.VMEM((3, 256, 256), BF16),
    a_h=pltpu.VMEM((6, 256, 256), BF16),
    a_l=pltpu.VMEM((6, 256, 256), BF16),
    t_h=pltpu.VMEM((256, 256), BF16),
    t_l=pltpu.VMEM((256, 256), BF16),
    swapped_pair=pltpu.VMEM((3, 256, 256), F32),
    swapped_in=pltpu.VMEM((3, 128, 256), F32),
    swapped_sum=pltpu.VMEM((3, 256, 256), F32),
    wc=pltpu.VMEM((2, 256, 128), F32),
    wc_in=pltpu.VMEM((2, 256, 128), F32),
    root_v=pltpu.VMEM((2, 256, 256), BF16),
    xi_v=pltpu.VMEM((2, 256, 128), BF16),
    nested_v=pltpu.VMEM((256, 256), F32),
    local=pltpu.SemaphoreType.DMA((12,)),
    send=pltpu.SemaphoreType.DMA((N_COPIES,)),
    recv=pltpu.SemaphoreType.DMA((N_COPIES,)),
)


def split(value):
    high = value.astype(BF16)
    return high, (value - high.astype(F32)).astype(BF16)


def dot3(a, b):
    left = jnp.concatenate([a[0], a[0], a[1]], axis=1)
    right = jnp.concatenate([b[0], b[1], b[0]], axis=0)
    return lax.dot_general(left, right, (NN, ((), ())), preferred_element_type=F32)


def dot3_nt(a, b):
    left = jnp.concatenate([a[0], a[0], a[1]], axis=1)
    right = jnp.concatenate([b[0], b[1], b[0]], axis=1)
    return lax.dot_general(left, right, (NT, ((), ())), preferred_element_type=F32)


def kernel(n_rows, *refs):
    tiles_hbm, cols_hbm, b_hbm, phi0_hbm, phi1_hbm, phi2_hbm = refs[:6]
    z_hbm, root_hbm, nested_hbm, inner_hbm = refs[6:10]
    v = dict(zip(SCRATCH, refs[10:]))

    r = lax.axis_index("rows")
    s = lax.axis_index("samp")
    x = lax.div(s, 2)
    c = lax.rem(s, 2)
    y = lax.rem(r, 4)
    xr, opposite, xl = (lax.rem(x + o, CHIPS) for o in (1, 2, 3))

    def chip(index):
        return (r, 2 * index + c)

    partner = (r, s + 1 - 2 * c)
    left = (lax.rem(r + n_rows - 1, n_rows), s)
    right = (lax.rem(r + 1, n_rows), s)
    sibling = (r + 1 - 2 * lax.rem(r, 2), s)
    cousin = (r + 3 - 2 * y, s)
    first_dim = x + 1 - 2 * lax.rem(x, 2)
    second_dim = 3 - x

    barrier = pltpu.get_barrier_semaphore()
    peers = [partner, chip(xr), chip(opposite), chip(xl), left, right, cousin]
    for peer in peers:
        pl.semaphore_signal(barrier, inc=1, device_id=peer, device_id_type=MESH)

    locals_ = []

    def local(src, dst):
        copy = pltpu.make_async_copy(src, dst, v["local"].at[len(locals_)])
        locals_.append(copy)
        copy.start()
        return copy

    sent = []

    def remote(src, dst, device):
        i = len(sent)
        copy = pltpu.make_async_remote_copy(
            src_ref=src,
            dst_ref=dst,
            send_sem=v["send"].at[i],
            recv_sem=v["recv"].at[i],
            device_id=device,
            device_id_type=MESH,
        )
        sent.append(copy)
        copy.start()
        return copy

    mine_half = pl.ds(pl.multiple_of(c * 256, 256), 256)
    own_cols = local(cols_hbm, v["cols"].at[0])
    pl.semaphore_wait(barrier, len(peers))
    with jax.named_scope("halo"):
        direct = []
        for i in range(4):
            at = 4 * x + i
            piece = b_hbm.at[at, :, mine_half]
            direct.append(
                (
                    remote(piece, v["ext"].at[at], right),
                    remote(piece, v["ext"].at[32 + at], left),
                )
            )
        cols_copy = remote(cols_hbm, v["cols_in"], partner)
        far = pl.ds(4 * opposite, 4)
        far_copies = [
            remote(b_hbm.at[far, :, mine_half], v["ext"].at[far], right),
            remote(b_hbm.at[far, :, mine_half], v["ext"].at[pl.ds(32 + 4 * opposite, 4)], left),
        ]
        tiles_copy = remote(tiles_hbm, v["tiles"].at[1], partner)
        own_tiles = local(tiles_hbm, v["tiles"].at[0])
        own_b = local(b_hbm.at[:, :, mine_half], v["ext"].at[pl.ds(16, 16)])
        phis = [local(p, v["phi"].at[i]) for i, p in enumerate((phi0_hbm, phi1_hbm, phi2_hbm))]
        handed = []
        for i in range(4):
            for side in range(2):
                direct[i][side].wait_recv()
                piece = v["ext"].at[32 * side + 4 * x + i]
                handed.append(remote(piece, piece, chip(xr)))
                handed.append(remote(piece, piece, chip(xl)))
        for i, copy in enumerate(phis):
            copy.wait()
            high, low = split(v["phi"][i])
            v["phi_h"][i] = high
            v["phi_l"][i] = low
        cols_copy.wait_recv()
        other_cols = local(v["cols_in"], v["cols"].at[1])
        for copy in (own_cols, own_tiles, own_b, other_cols):
            copy.wait()
        for copy in [tiles_copy] + far_copies + handed:
            copy.wait_recv()
    first = (r - 1) * 16

    def product(slot, base):
        def tile_row(t, carry):
            row = base + t
            lhs = jnp.concatenate(
                [v["tiles"][h, row, k] for h in range(2) for k in range(4)], axis=1
            )
            rhs = jnp.concatenate(
                [
                    v["ext"][jnp.clip(v["cols"][h, k, row] - first, 0, 47)]
                    for h in range(2)
                    for k in range(4)
                ],
                axis=0,
            )
            v["part"][slot, t] = jnp.dot(lhs, rhs, preferred_element_type=F32)
            return carry

        lax.fori_loop(0, 2, tile_row, 0)
        return v["part"][slot].reshape(256, 256)

    def coded(i, value, device):
        top = jnp.maximum(jnp.max(jnp.abs(value), axis=1, keepdims=True), 1e-30)
        v["code"][i] = jnp.round(value * (32767.0 / top)).astype(jnp.int32).astype(I16)
        v["unit"][i] = jnp.broadcast_to(top * (1 / 32767.0), (256, 128)).T[0:8]
        return (
            remote(v["code"].at[i], v["code_in"].at[i], device),
            remote(v["unit"].at[i], v["unit_in"].at[i], device),
        )

    def decoded(i, copies):
        for copy in copies:
            copy.wait_recv()
        unit = jnp.broadcast_to(v["unit_in"][i, 0:1], (128, 256)).T
        return v["code_in"][i].astype(jnp.int32).astype(F32) * jnp.concatenate([unit, unit], axis=1)

    with jax.named_scope("product"):
        up_far = coded(0, product(0, 4 * opposite), chip(xr))
        down_far = coded(1, product(1, 4 * opposite + 2), chip(xl))
        down_near = coded(2, product(0, 4 * xr + 2), chip(xr))
        up_near = coded(3, product(1, 4 * xl), chip(xl))
        up_sum = coded(4, product(0, 4 * xr) + decoded(0, up_far), chip(xr))
        down_sum = coded(5, product(1, 4 * xl + 2) + decoded(1, down_far), chip(xl))
        product(0, 4 * x)
        product(1, 4 * x + 2)
        upper_in = decoded(3, up_near) + decoded(4, up_sum)
        lower_in = decoded(2, down_near) + decoded(5, down_sum)
        upper_half = v["part"][0].reshape(256, 256) + upper_in
        lower_half = v["part"][1].reshape(256, 256) + lower_in
        v["swap"][...] = jnp.where(c == 0, lower_half, upper_half)
        swapped = remote(v["swap"], v["samp"].at[c], partner)
        v["samp"][c] = jnp.where(c == 0, upper_half, lower_half)
        swapped.wait_recv()
    def put(slot, value):
        high, low = split(value)
        v["a_h"][slot] = high
        v["a_l"][slot] = low

    def get(slot):
        return v["a_h"][slot], v["a_l"][slot]

    def phi_of(i):
        return v["phi_h"][i], v["phi_l"][i]

    def transposed():
        return v["t_h"][...], v["t_l"][...]

    def packed(gram):
        corner = jnp.concatenate([gram[128:192, 128:256], gram[192:256, 128:256]], axis=1)
        return jnp.concatenate([gram[0:128], corner], axis=0)

    def unpacked(rows):
        corner = jnp.concatenate([rows[128:192, 0:128], rows[128:192, 128:256]], axis=0)
        low = jnp.concatenate([rows[0:128, 128:256].T, corner], axis=1)
        return jnp.concatenate([rows[0:128], low], axis=0)

    def core_rows(size, core):
        return pl.ds(pl.multiple_of(core * size, size), size)

    def half_of(m):
        return 96 if m == 0 else 128

    def sum_core(m):
        size = half_of(m)
        rows = core_rows(size, 1 - c)
        return [remote(v["mine"].at[m, rows], v["in_core"].at[m, 0:size], partner)]

    def crossed(ref, into, m, one, two):
        size, cut = half_of(m), half_of(m) // 2
        return [
            remote(v[ref].at[m, 0:cut], v[into].at[m, 0:cut], chip(one)),
            remote(v[ref].at[m, cut:size], v[into].at[m, cut:size], chip(two)),
        ]

    def arrived(copies):
        for copy in copies:
            copy.wait_recv()

    def sum_first(m, copies):
        arrived(copies)
        size = half_of(m)
        v["chip"][m, 0:size] = v["mine"][m, core_rows(size, c)] + v["in_core"][m, 0:size]
        return crossed("chip", "in_chip", m, first_dim, second_dim)

    def sum_second(m, copies):
        arrived(copies)
        size = half_of(m)
        v["two"][m, 0:size] = v["chip"][m, 0:size] + v["in_chip"][m, 0:size]
        return crossed("two", "in_two", m, second_dim, first_dim)

    def sum_last(m, copies):
        arrived(copies)
        size = half_of(m)
        rows = core_rows(size, c)
        v["full"][m, rows] = v["two"][m, 0:size] + v["in_two"][m, 0:size]
        return [remote(v["full"].at[m, rows], v["full"].at[m, rows], partner)]

    with jax.named_scope("sums"):
        for half in range(2):
            put(half, v["samp"][half])
        sample = (
            jnp.concatenate([v["a_h"][0], v["a_h"][1]], axis=1),
            jnp.concatenate([v["a_l"][0], v["a_l"][1]], axis=1),
        )
        z = dot3(sample, phi_of(0))
        z_high, z_low = split(z)
        v["z_own"][0] = z_high
        v["z_own"][1] = z_low
        t_high, t_low = split(z.T)
        v["t_h"][...] = t_high
        v["t_l"][...] = t_low
        v["mine"][0, 0:192] = packed(dot3(transposed(), (v["z_own"][0], v["z_own"][1])))
        sum_g = sum_core(0)
        z_local = local(v["z_own"], z_hbm.at[s])
        for half in range(2):
            w = dot3(transposed(), get(half))
            put(3 + half, w)
            for q in range(4):
                v["wpart"][q // 2, 2 * half + q % 2] = w[
                    128 * (q // 2) : 128 * (q // 2) + 128, 128 * (q % 2) : 128 * (q % 2) + 128
                ]
        sum_g = sum_first(0, sum_g)
        w_all = (
            jnp.concatenate([v["a_h"][3], v["a_h"][4]], axis=1),
            jnp.concatenate([v["a_l"][3], v["a_l"][4]], axis=1),
        )
        v["mine"][1] = dot3(w_all, phi_of(1))
        sum_n = sum_core(1)
        v["mine"][2] = dot3(w_all, phi_of(2))
        sum_o = sum_core(2)
        w_core = remote(v["wpart"].at[1 - c], v["w_core"], partner)
        sum_n = sum_first(1, sum_n)
        sum_g = sum_second(0, sum_g)
        sum_o = sum_first(2, sum_o)
        sum_n = sum_second(1, sum_n)
        sum_o = sum_second(2, sum_o)
        sum_g = sum_last(0, sum_g)
        w_core.wait_recv()
        v["w_chip"][...] = v["wpart"][c] + v["w_core"][...]
        arrived(sum_g)
    eye = jnp.where(
        lax.broadcasted_iota(jnp.int32, (RANK, RANK), 0)
        == lax.broadcasted_iota(jnp.int32, (RANK, RANK), 1),
        F32(1.5),
        F32(0),
    )

    def inverse_root(level, gram, meanwhile):
        norm = (
            jnp.sqrt(
                jnp.sum(jnp.sum(gram * gram, axis=1, keepdims=True), axis=0, keepdims=True)
            )
            + 1e-06
        )
        y0 = gram / norm
        factor = split(eye - 0.5 * y0)
        new_high, new_low = split(dot3(split(y0), factor))
        v["yx_h"][0:256] = new_high
        v["yx_l"][0:256] = new_low
        v["yx_h"][256:512] = factor[0]
        v["yx_l"][256:512] = factor[1]

        def make_factor():
            both = dot3(
                (v["yx_h"][256:512], v["yx_l"][256:512]), (v["yx_h"][0:256], v["yx_l"][0:256])
            )
            high, low = split(eye - 0.5 * both)
            v["f_h"][...] = high
            v["f_l"][...] = low

        def step(_, carry):
            make_factor()
            high, low = split(
                dot3((v["yx_h"][...], v["yx_l"][...]), (v["f_h"][...], v["f_l"][...]))
            )
            v["yx_h"][...] = high
            v["yx_l"][...] = low
            return carry

        step(0, 0)
        passed_on = meanwhile()
        lax.fori_loop(0, NS_ITERS - 3, step, 0)
        make_factor()
        result = dot3((v["yx_h"][256:512], v["yx_l"][256:512]), (v["f_h"][...], v["f_l"][...]))
        high, low = split(result)
        v["x_h"][level] = high
        v["x_l"][level] = low
        return 1.0 / jnp.sqrt(norm), result, passed_on

    def root(level):
        return v["x_h"][level], v["x_l"][level]

    def exchange(i, device):
        size = 128 if i == 1 else 96
        rows = core_rows(size, c)
        return remote(v["swapped_pair"].at[i, rows], v["swapped_in"].at[i, 0:size], device)

    def exchange_core(i, copy):
        copy.wait_recv()
        size = 128 if i == 1 else 96
        rows = core_rows(size, c)
        v["swapped_sum"][i, rows] = v["swapped_pair"][i, rows] + v["swapped_in"][i, 0:size]
        return remote(v["swapped_sum"].at[i, rows], v["swapped_sum"].at[i, rows], partner)

    with jax.named_scope("leaf"):

        def last_sums():
            last_n, last_o = sum_last(1, sum_n), sum_last(2, sum_o)
            columns = [
                remote(v["w_chip"].at[d], v["w_in"].at[o], chip(d))
                for o, d in enumerate((xr, opposite, xl))
            ]
            return last_n, last_o, columns

        scale_leaf, x_leaf, (sum_n, sum_o, w_copies) = inverse_root(0, unpacked(v["full"][0, 0:192]), last_sums)
        arrived(sum_n)
        zp = dot3(root(0), split(v["full"][1])) * scale_leaf
        put(0, zp)
        t_high, t_low = split(zp.T)
        v["t_h"][...] = t_high
        v["t_l"][...] = t_low
        v["swapped_pair"][0, 0:192] = packed(dot3(transposed(), get(0)))
        gram_copy = exchange(0, sibling)
        z_right = remote(v["z_own"], z_hbm.at[s], chip(xr))
        z_left = remote(v["z_own"], z_hbm.at[s], chip(xl))
        z_partner = remote(v["z_own"], z_hbm.at[s], partner)
        arrived(sum_o)
        put(5, dot3(root(0), split(v["full"][2])) * scale_leaf)
        v["swapped_pair"][1] = dot3(transposed(), get(5))
        cross_copy = exchange(1, sibling)
        root_high, root_low = split(x_leaf * scale_leaf)
        v["root_v"][0] = root_high
        v["root_v"][1] = root_low
        root_copy = local(v["root_v"], root_hbm)
        gram_copy = exchange_core(0, gram_copy)
        arrived(w_copies)
        v["wcol"][c] = v["w_chip"][x] + v["w_in"][0] + v["w_in"][1] + v["w_in"][2]
        wcol_copy = remote(v["wcol"].at[c], v["wcol"].at[c], partner)
        wcol_copy.wait_recv()
        coarse = dot3(root(0), split(v["wcol"][...].reshape(256, 128))) * scale_leaf
        v["wc"][0] = dot3(transposed(), split(coarse))
        wc_copy = remote(v["wc"].at[0], v["wc_in"].at[0], sibling)
        gram_copy.wait_recv()
    with jax.named_scope("pair"):
        scale_pair, _, cross_copy = inverse_root(
            1, unpacked(v["swapped_sum"][0, 0:192]), lambda: exchange_core(1, cross_copy)
        )
        put(2, dot3(get(0), root(1)) * scale_pair)
        cross_copy.wait_recv()
        zq = dot3(root(1), split(v["swapped_sum"][1])) * scale_pair
        put(1, zq)
        t_high, t_low = split(zq.T)
        v["t_h"][...] = t_high
        v["t_l"][...] = t_low
        v["swapped_pair"][2, 0:192] = packed(dot3(transposed(), get(1)))
        gram_copy = exchange(2, cousin)
        put(4, dot3(get(2), get(1)))
        wc_copy.wait_recv()
        middle = dot3(root(1), split(v["wc"][0] + v["wc_in"][0])) * scale_pair
        v["wc"][1] = dot3(transposed(), split(middle))
        wc_copy = remote(v["wc"].at[1], v["wc_in"].at[1], cousin)
        z_right.wait_recv()
        from_left = 2 * xl + c
        round_right = remote(
            z_hbm.at[from_left, :, 0:128], z_hbm.at[from_left, :, 0:128], chip(xr)
        )
        z_left.wait_recv()
        from_right = 2 * xr + c
        round_left = remote(
            z_hbm.at[from_right, :, 128:256], z_hbm.at[from_right, :, 128:256], chip(xl)
        )
        handed_z = [
            remote(z_hbm.at[from_left], z_hbm.at[from_left], partner),
            remote(z_hbm.at[from_right], z_hbm.at[from_right], partner),
        ]
        gram_copy = exchange_core(2, gram_copy)
        gram_copy.wait_recv()
    with jax.named_scope("quad"):
        scale_quad, _, _ = inverse_root(2, unpacked(v["swapped_sum"][2, 0:192]), lambda: None)
        arrived([round_right, round_left])
        from_far = 2 * opposite + c
        handed_z.append(remote(z_hbm.at[from_far], z_hbm.at[from_far], partner))
        nested = dot3(get(4), root(2)) * scale_quad
        v["nested_v"][...] = nested
        nested_copy = local(v["nested_v"], nested_hbm)
        wc_copy.wait_recv()
        summary = dot3(root(2), split(v["wc"][1] + v["wc_in"][1])) * scale_quad
        inner = dot3(split(nested), split(summary))
        inner_high, inner_low = split(
            dot3((v["root_v"][0], v["root_v"][1]), split(inner))
        )
        v["xi_v"][0] = inner_high
        v["xi_v"][1] = inner_low
        inner_copy = local(v["xi_v"], inner_hbm)
        arrived([z_partner] + handed_z)
        for copy in (z_local, root_copy, nested_copy, inner_copy):
            copy.wait()
        assert len(sent) <= N_COPIES and len(locals_) <= 12
        for copy in sent:
            copy.wait_send()


def outputs(z_ref, root_ref, nested_ref, inner_ref, basis_out, nested_out, approx_out, turned):
    core = lax.rem(lax.axis_index("samp"), 2)
    for i in range(2):
        rows = pl.ds(256 * i, 256)
        z = z_ref[i, 0], z_ref[i, 1]
        basis_out[rows] = dot3(z, (root_ref[0], root_ref[1]))
        turned[i] = dot3(z, (inner_ref[0], inner_ref[1])).T
        approx_out[:, rows] = turned[i, pl.ds(pl.multiple_of(core * 64, 64), 64)]
    nested_out[...] = nested_ref[...]


def on_device(n_rows, coupling_tiles, tile_columns, sample_matrix, phi_leaf, phi_pair, phi_quad):
    rows = sample_matrix.shape[0]
    share = sample_matrix.shape[1] // SAMP
    any_ = pl.BlockSpec(memory_space=pl.ANY)
    z, root, nested, inner = pl.pallas_call(
        functools.partial(kernel, n_rows),
        out_shape=(
            jax.ShapeDtypeStruct((SAMP, 2, RANK, RANK), BF16),
            jax.ShapeDtypeStruct((2, RANK, RANK), BF16),
            jax.ShapeDtypeStruct((RANK, RANK), F32),
            jax.ShapeDtypeStruct((2, RANK, 128), BF16),
        ),
        in_specs=[any_] * 6,
        out_specs=(any_,) * 4,
        scratch_shapes=list(SCRATCH.values()),
        compiler_params=pltpu.CompilerParams(
            collective_id=0, has_side_effects=True, vmem_limit_bytes=56 * 2**20
        ),
        name="hss",
    )(
        coupling_tiles,
        tile_columns.T,
        sample_matrix.reshape(16, 128, 512),
        phi_leaf,
        phi_pair,
        phi_quad,
    )
    basis, nested, approx_t = pl.pallas_call(
        outputs,
        grid=(SAMP // 2,),
        out_shape=(
            jax.ShapeDtypeStruct((rows, RANK), F32),
            jax.ShapeDtypeStruct((RANK, RANK), F32),
            jax.ShapeDtypeStruct((share, rows), F32),
        ),
        in_specs=[
            pl.BlockSpec((2, 2, RANK, RANK), lambda i: (i, 0, 0, 0)),
            pl.BlockSpec((2, RANK, RANK), lambda i: (0, 0, 0)),
            pl.BlockSpec((RANK, RANK), lambda i: (0, 0)),
            pl.BlockSpec((2, RANK, 128), lambda i: (0, 0, 0)),
        ],
        out_specs=(
            pl.BlockSpec((2 * RANK, RANK), lambda i: (i, 0)),
            pl.BlockSpec((RANK, RANK), lambda i: (0, 0)),
            pl.BlockSpec((share, 2 * RANK), lambda i: (0, i)),
        ),
        scratch_shapes=[pltpu.VMEM((2, 128, RANK), F32)],
        compiler_params=pltpu.CompilerParams(vmem_limit_bytes=56 * 2**20),
        name="expand",
    )(z, root, nested, inner)
    return basis, nested, approx_t.T


def solution(mesh):
    return jax.shard_map(
        functools.partial(on_device, mesh.shape["rows"]),
        mesh=mesh,
        in_specs=(P("rows", "samp", None, None), P("rows", "samp"), P("rows", None), P(), P(), P()),
        out_specs=(P("rows", None), P("rows", None), P("rows", "samp")),
        check_vma=False,
    )
```

```python
import functools

import jax
import jax.numpy as jnp
from jax import lax
from jax.experimental import pallas as pl
from jax.experimental.pallas import tpu as pltpu
from jax.sharding import PartitionSpec as P

NS_ITERS = 5
MESH = pl.DeviceIdType.MESH
F32 = jnp.float32
BF16 = jnp.bfloat16
NT, NN = ((1,), (1,)), ((1,), (0,))

N_COPIES = 96
SAMP = 8
CHIPS = 4
RANK = 256

I16 = jnp.int16

SCRATCH = dict(
    ext=pltpu.VMEM((48, 128, 256), BF16),
    tiles=pltpu.VMEM((2, 16, 4, 128, 128), BF16),
    cols_in=pltpu.VMEM((4, 16), jnp.int32),
    cols=pltpu.SMEM((2, 4, 16), jnp.int32),
    phi=pltpu.VMEM((3, 512, 256), F32),
    phi_h=pltpu.VMEM((3, 512, 256), BF16),
    phi_l=pltpu.VMEM((3, 512, 256), BF16),
    part=pltpu.VMEM((2, 2, 128, 256), F32),
    code=pltpu.VMEM((6, 256, 256), I16),
    code_in=pltpu.VMEM((6, 256, 256), I16),
    unit=pltpu.VMEM((6, 8, 256), F32),
    unit_in=pltpu.VMEM((6, 8, 256), F32),
    swap=pltpu.VMEM((256, 256), F32),
    samp=pltpu.VMEM((2, 256, 256), F32),
    mine=pltpu.VMEM((3, 256, 256), F32),
    in_core=pltpu.VMEM((3, 128, 256), F32),
    chip=pltpu.VMEM((3, 128, 256), F32),
    in_chip=pltpu.VMEM((3, 128, 256), F32),
    two=pltpu.VMEM((3, 128, 256), F32),
    in_two=pltpu.VMEM((3, 128, 256), F32),
    full=pltpu.VMEM((3, 256, 256), F32),
    wpart=pltpu.VMEM((2, 4, 128, 128), F32),
    w_core=pltpu.VMEM((4, 128, 128), F32),
    w_chip=pltpu.VMEM((4, 128, 128), F32),
    w_in=pltpu.VMEM((3, 128, 128), F32),
    wcol=pltpu.VMEM((2, 128, 128), F32),
    z_own=pltpu.VMEM((2, 256, 256), BF16),
    yx_h=pltpu.VMEM((512, 256), BF16),
    yx_l=pltpu.VMEM((512, 256), BF16),
    f_h=pltpu.VMEM((256, 256), BF16),
    f_l=pltpu.VMEM((256, 256), BF16),
    x_h=pltpu.VMEM((3, 256, 256), BF16),
    x_l=pltpu.VMEM((3, 256, 256), BF16),
    a_h=pltpu.VMEM((6, 256, 256), BF16),
    a_l=pltpu.VMEM((6, 256, 256), BF16),
    t_h=pltpu.VMEM((256, 256), BF16),
    t_l=pltpu.VMEM((256, 256), BF16),
    swapped_pair=pltpu.VMEM((3, 256, 256), F32),
    swapped_in=pltpu.VMEM((3, 128, 256), F32),
    swapped_sum=pltpu.VMEM((3, 256, 256), F32),
    wc=pltpu.VMEM((2, 256, 128), F32),
    wc_in=pltpu.VMEM((2, 256, 128), F32),
    root_v=pltpu.VMEM((2, 256, 256), BF16),
    xi_v=pltpu.VMEM((2, 256, 128), BF16),
    nested_v=pltpu.VMEM((256, 256), F32),
    local=pltpu.SemaphoreType.DMA((12,)),
    send=pltpu.SemaphoreType.DMA((N_COPIES,)),
    recv=pltpu.SemaphoreType.DMA((N_COPIES,)),
)


def split(value):
    high = value.astype(BF16)
    return high, (value - high.astype(F32)).astype(BF16)


def dot3(a, b):
    left = jnp.concatenate([a[0], a[0], a[1]], axis=1)
    right = jnp.concatenate([b[0], b[1], b[0]], axis=0)
    return lax.dot_general(left, right, (NN, ((), ())), preferred_element_type=F32)


def dot3_nt(a, b):
    left = jnp.concatenate([a[0], a[0], a[1]], axis=1)
    right = jnp.concatenate([b[0], b[1], b[0]], axis=1)
    return lax.dot_general(left, right, (NT, ((), ())), preferred_element_type=F32)


def kernel(n_rows, *refs):
    tiles_hbm, cols_hbm, b_hbm, phi0_hbm, phi1_hbm, phi2_hbm = refs[:6]
    z_hbm, root_hbm, nested_hbm, inner_hbm = refs[6:10]
    v = dict(zip(SCRATCH, refs[10:]))

    r = lax.axis_index("rows")
    s = lax.axis_index("samp")
    x = lax.div(s, 2)
    c = lax.rem(s, 2)
    y = lax.rem(r, 4)
    xr, opposite, xl = (lax.rem(x + o, CHIPS) for o in (1, 2, 3))

    def chip(index):
        return (r, 2 * index + c)

    partner = (r, s + 1 - 2 * c)
    left = (lax.rem(r + n_rows - 1, n_rows), s)
    right = (lax.rem(r + 1, n_rows), s)
    sibling = (r + 1 - 2 * lax.rem(r, 2), s)
    cousin = (r + 3 - 2 * y, s)
    first_dim = x + 1 - 2 * lax.rem(x, 2)
    second_dim = 3 - x

    barrier = pltpu.get_barrier_semaphore()
    peers = [partner, chip(xr), chip(opposite), chip(xl), left, right, cousin]
    for peer in peers:
        pl.semaphore_signal(barrier, inc=1, device_id=peer, device_id_type=MESH)

    locals_ = []

    def local(src, dst):
        copy = pltpu.make_async_copy(src, dst, v["local"].at[len(locals_)])
        locals_.append(copy)
        copy.start()
        return copy

    sent = []

    def remote(src, dst, device):
        i = len(sent)
        copy = pltpu.make_async_remote_copy(
            src_ref=src,
            dst_ref=dst,
            send_sem=v["send"].at[i],
            recv_sem=v["recv"].at[i],
            device_id=device,
            device_id_type=MESH,
        )
        sent.append(copy)
        copy.start()
        return copy

    mine_half = pl.ds(pl.multiple_of(c * 256, 256), 256)
    own_cols = local(cols_hbm, v["cols"].at[0])
    pl.semaphore_wait(barrier, len(peers))
    with jax.named_scope("halo"):
        direct = []
        for i in range(4):
            at = 4 * x + i
            piece = b_hbm.at[at, :, mine_half]
            direct.append(
                (
                    remote(piece, v["ext"].at[at], right),
                    remote(piece, v["ext"].at[32 + at], left),
                )
            )
        cols_copy = remote(cols_hbm, v["cols_in"], partner)
        far = pl.ds(4 * opposite, 4)
        far_copies = [
            remote(b_hbm.at[far, :, mine_half], v["ext"].at[far], right),
            remote(b_hbm.at[far, :, mine_half], v["ext"].at[pl.ds(32 + 4 * opposite, 4)], left),
        ]
        tiles_copy = remote(tiles_hbm, v["tiles"].at[1], partner)
        own_tiles = local(tiles_hbm, v["tiles"].at[0])
        own_b = local(b_hbm.at[:, :, mine_half], v["ext"].at[pl.ds(16, 16)])
        phis = [local(p, v["phi"].at[i]) for i, p in enumerate((phi0_hbm, phi1_hbm, phi2_hbm))]
        handed = []
        for i in range(4):
            for side in range(2):
                direct[i][side].wait_recv()
                piece = v["ext"].at[32 * side + 4 * x + i]
                handed.append(remote(piece, piece, chip(xr)))
                handed.append(remote(piece, piece, chip(xl)))
        for i, copy in enumerate(phis):
            copy.wait()
            high, low = split(v["phi"][i])
            v["phi_h"][i] = high
            v["phi_l"][i] = low
        cols_copy.wait_recv()
        other_cols = local(v["cols_in"], v["cols"].at[1])
        for copy in (own_cols, own_tiles, own_b, other_cols):
            copy.wait()
        for copy in [tiles_copy] + far_copies + handed:
            copy.wait_recv()
    first = (r - 1) * 16

    def product(slot, base):
        def tile_row(t, carry):
            row = base + t
            lhs = jnp.concatenate(
                [v["tiles"][h, row, k] for h in range(2) for k in range(4)], axis=1
            )
            rhs = jnp.concatenate(
                [
                    v["ext"][jnp.clip(v["cols"][h, k, row] - first, 0, 47)]
                    for h in range(2)
                    for k in range(4)
                ],
                axis=0,
            )
            v["part"][slot, t] = jnp.dot(lhs, rhs, preferred_element_type=F32)
            return carry

        lax.fori_loop(0, 2, tile_row, 0)
        return v["part"][slot].reshape(256, 256)

    def coded(i, value, device):
        top = jnp.maximum(jnp.max(jnp.abs(value), axis=1, keepdims=True), 1e-30)
        v["code"][i] = jnp.round(value * (32767.0 / top)).astype(jnp.int32).astype(I16)
        v["unit"][i] = jnp.broadcast_to(top * (1 / 32767.0), (256, 128)).T[0:8]
        return (
            remote(v["code"].at[i], v["code_in"].at[i], device),
            remote(v["unit"].at[i], v["unit_in"].at[i], device),
        )

    def decoded(i, copies):
        for copy in copies:
            copy.wait_recv()
        unit = jnp.broadcast_to(v["unit_in"][i, 0:1], (128, 256)).T
        return v["code_in"][i].astype(jnp.int32).astype(F32) * jnp.concatenate([unit, unit], axis=1)

    with jax.named_scope("product"):
        up_far = coded(0, product(0, 4 * opposite), chip(xr))
        down_far = coded(1, product(1, 4 * opposite + 2), chip(xl))
        down_near = coded(2, product(0, 4 * xr + 2), chip(xr))
        up_near = coded(3, product(1, 4 * xl), chip(xl))
        up_sum = coded(4, product(0, 4 * xr) + decoded(0, up_far), chip(xr))
        down_sum = coded(5, product(1, 4 * xl + 2) + decoded(1, down_far), chip(xl))
        product(0, 4 * x)
        product(1, 4 * x + 2)
        upper_in = decoded(3, up_near) + decoded(4, up_sum)
        lower_in = decoded(2, down_near) + decoded(5, down_sum)
        upper_half = v["part"][0].reshape(256, 256) + upper_in
        lower_half = v["part"][1].reshape(256, 256) + lower_in
        v["swap"][...] = jnp.where(c == 0, lower_half, upper_half)
        swapped = remote(v["swap"], v["samp"].at[c], partner)
        v["samp"][c] = jnp.where(c == 0, upper_half, lower_half)
        swapped.wait_recv()
    def put(slot, value):
        high, low = split(value)
        v["a_h"][slot] = high
        v["a_l"][slot] = low

    def get(slot):
        return v["a_h"][slot], v["a_l"][slot]

    def phi_of(i):
        return v["phi_h"][i], v["phi_l"][i]

    def transposed():
        return v["t_h"][...], v["t_l"][...]

    def packed(gram):
        corner = jnp.concatenate([gram[128:192, 128:256], gram[192:256, 128:256]], axis=1)
        return jnp.concatenate([gram[0:128], corner], axis=0)

    def unpacked(rows):
        corner = jnp.concatenate([rows[128:192, 0:128], rows[128:192, 128:256]], axis=0)
        low = jnp.concatenate([rows[0:128, 128:256].T, corner], axis=1)
        return jnp.concatenate([rows[0:128], low], axis=0)

    def core_rows(size, core):
        return pl.ds(pl.multiple_of(core * size, size), size)

    def half_of(m):
        return 96 if m == 0 else 128

    def sum_core(m):
        size = half_of(m)
        rows = core_rows(size, 1 - c)
        return [remote(v["mine"].at[m, rows], v["in_core"].at[m, 0:size], partner)]

    def crossed(ref, into, m, one, two):
        size, cut = half_of(m), half_of(m) // 2
        return [
            remote(v[ref].at[m, 0:cut], v[into].at[m, 0:cut], chip(one)),
            remote(v[ref].at[m, cut:size], v[into].at[m, cut:size], chip(two)),
        ]

    def arrived(copies):
        for copy in copies:
            copy.wait_recv()

    def sum_first(m, copies):
        arrived(copies)
        size = half_of(m)
        v["chip"][m, 0:size] = v["mine"][m, core_rows(size, c)] + v["in_core"][m, 0:size]
        return crossed("chip", "in_chip", m, first_dim, second_dim)

    def sum_second(m, copies):
        arrived(copies)
        size = half_of(m)
        v["two"][m, 0:size] = v["chip"][m, 0:size] + v["in_chip"][m, 0:size]
        return crossed("two", "in_two", m, second_dim, first_dim)

    def sum_last(m, copies):
        arrived(copies)
        size = half_of(m)
        rows = core_rows(size, c)
        v["full"][m, rows] = v["two"][m, 0:size] + v["in_two"][m, 0:size]
        return [remote(v["full"].at[m, rows], v["full"].at[m, rows], partner)]

    with jax.named_scope("sums"):
        for half in range(2):
            put(half, v["samp"][half])
        sample = (
            jnp.concatenate([v["a_h"][0], v["a_h"][1]], axis=1),
            jnp.concatenate([v["a_l"][0], v["a_l"][1]], axis=1),
        )
        z = dot3(sample, phi_of(0))
        z_high, z_low = split(z)
        v["z_own"][0] = z_high
        v["z_own"][1] = z_low
        t_high, t_low = split(z.T)
        v["t_h"][...] = t_high
        v["t_l"][...] = t_low
        v["mine"][0, 0:192] = packed(dot3(transposed(), (v["z_own"][0], v["z_own"][1])))
        sum_g = sum_core(0)
        z_local = local(v["z_own"], z_hbm.at[s])
        for half in range(2):
            w = dot3(transposed(), get(half))
            put(3 + half, w)
            for q in range(4):
                v["wpart"][q // 2, 2 * half + q % 2] = w[
                    128 * (q // 2) : 128 * (q // 2) + 128, 128 * (q % 2) : 128 * (q % 2) + 128
                ]
        sum_g = sum_first(0, sum_g)
        w_all = (
            jnp.concatenate([v["a_h"][3], v["a_h"][4]], axis=1),
            jnp.concatenate([v["a_l"][3], v["a_l"][4]], axis=1),
        )
        v["mine"][1] = dot3(w_all, phi_of(1))
        sum_n = sum_core(1)
        v["mine"][2] = dot3(w_all, phi_of(2))
        sum_o = sum_core(2)
        w_core = remote(v["wpart"].at[1 - c], v["w_core"], partner)
        sum_n = sum_first(1, sum_n)
        sum_g = sum_second(0, sum_g)
        sum_o = sum_first(2, sum_o)
        sum_n = sum_second(1, sum_n)
        sum_o = sum_second(2, sum_o)
        sum_g = sum_last(0, sum_g)
        w_core.wait_recv()
        v["w_chip"][...] = v["wpart"][c] + v["w_core"][...]
        arrived(sum_g)
    eye = jnp.where(
        lax.broadcasted_iota(jnp.int32, (RANK, RANK), 0)
        == lax.broadcasted_iota(jnp.int32, (RANK, RANK), 1),
        F32(1.5),
        F32(0),
    )

    def inverse_root(level, gram, meanwhile):
        norm = (
            jnp.sqrt(
                jnp.sum(jnp.sum(gram * gram, axis=1, keepdims=True), axis=0, keepdims=True)
            )
            + 1e-06
        )
        y0 = gram / norm
        factor = split(eye - 0.5 * y0)
        new_high, new_low = split(dot3(split(y0), factor))
        v["yx_h"][0:256] = new_high
        v["yx_l"][0:256] = new_low
        v["yx_h"][256:512] = factor[0]
        v["yx_l"][256:512] = factor[1]

        def make_factor():
            both = dot3(
                (v["yx_h"][256:512], v["yx_l"][256:512]), (v["yx_h"][0:256], v["yx_l"][0:256])
            )
            high, low = split(eye - 0.5 * both)
            v["f_h"][...] = high
            v["f_l"][...] = low

        def step(_, carry):
            make_factor()
            high, low = split(
                dot3((v["yx_h"][...], v["yx_l"][...]), (v["f_h"][...], v["f_l"][...]))
            )
            v["yx_h"][...] = high
            v["yx_l"][...] = low
            return carry

        step(0, 0)
        passed_on = meanwhile()
        lax.fori_loop(0, NS_ITERS - 3, step, 0)
        make_factor()
        result = dot3((v["yx_h"][256:512], v["yx_l"][256:512]), (v["f_h"][...], v["f_l"][...]))
        high, low = split(result)
        v["x_h"][level] = high
        v["x_l"][level] = low
        return 1.0 / jnp.sqrt(norm), result, passed_on

    def root(level):
        return v["x_h"][level], v["x_l"][level]

    def exchange(i, device):
        size = 128 if i == 1 else 96
        rows = core_rows(size, c)
        return remote(v["swapped_pair"].at[i, rows], v["swapped_in"].at[i, 0:size], device)

    def exchange_core(i, copy):
        copy.wait_recv()
        size = 128 if i == 1 else 96
        rows = core_rows(size, c)
        v["swapped_sum"][i, rows] = v["swapped_pair"][i, rows] + v["swapped_in"][i, 0:size]
        return remote(v["swapped_sum"].at[i, rows], v["swapped_sum"].at[i, rows], partner)

    with jax.named_scope("leaf"):

        def last_sums():
            last_n, last_o = sum_last(1, sum_n), sum_last(2, sum_o)
            columns = [
                remote(v["w_chip"].at[d], v["w_in"].at[o], chip(d))
                for o, d in enumerate((xr, opposite, xl))
            ]
            return last_n, last_o, columns

        scale_leaf, x_leaf, (sum_n, sum_o, w_copies) = inverse_root(0, unpacked(v["full"][0, 0:192]), last_sums)
        arrived(sum_n)
        zp = dot3(root(0), split(v["full"][1])) * scale_leaf
        put(0, zp)
        t_high, t_low = split(zp.T)
        v["t_h"][...] = t_high
        v["t_l"][...] = t_low
        v["swapped_pair"][0, 0:192] = packed(dot3(transposed(), get(0)))
        gram_copy = exchange(0, sibling)
        z_right = remote(v["z_own"], z_hbm.at[s], chip(xr))
        z_left = remote(v["z_own"], z_hbm.at[s], chip(xl))
        z_partner = remote(v["z_own"], z_hbm.at[s], partner)
        arrived(sum_o)
        put(5, dot3(root(0), split(v["full"][2])) * scale_leaf)
        v["swapped_pair"][1] = dot3(transposed(), get(5))
        cross_copy = exchange(1, sibling)
        root_high, root_low = split(x_leaf * scale_leaf)
        v["root_v"][0] = root_high
        v["root_v"][1] = root_low
        root_copy = local(v["root_v"], root_hbm)
        gram_copy = exchange_core(0, gram_copy)
        arrived(w_copies)
        v["wcol"][c] = v["w_chip"][x] + v["w_in"][0] + v["w_in"][1] + v["w_in"][2]
        wcol_copy = remote(v["wcol"].at[c], v["wcol"].at[c], partner)
        wcol_copy.wait_recv()
        coarse = dot3(root(0), split(v["wcol"][...].reshape(256, 128))) * scale_leaf
        v["wc"][0] = dot3(transposed(), split(coarse))
        wc_copy = remote(v["wc"].at[0], v["wc_in"].at[0], sibling)
        gram_copy.wait_recv()
    with jax.named_scope("pair"):
        scale_pair, _, cross_copy = inverse_root(
            1, unpacked(v["swapped_sum"][0, 0:192]), lambda: exchange_core(1, cross_copy)
        )
        put(2, dot3(get(0), root(1)) * scale_pair)
        cross_copy.wait_recv()
        zq = dot3(root(1), split(v["swapped_sum"][1])) * scale_pair
        put(1, zq)
        t_high, t_low = split(zq.T)
        v["t_h"][...] = t_high
        v["t_l"][...] = t_low
        v["swapped_pair"][2, 0:192] = packed(dot3(transposed(), get(1)))
        gram_copy = exchange(2, cousin)
        put(4, dot3(get(2), get(1)))
        wc_copy.wait_recv()
        middle = dot3(root(1), split(v["wc"][0] + v["wc_in"][0])) * scale_pair
        v["wc"][1] = dot3(transposed(), split(middle))
        wc_copy = remote(v["wc"].at[1], v["wc_in"].at[1], cousin)
        z_right.wait_recv()
        from_left = 2 * xl + c
        round_right = remote(
            z_hbm.at[from_left, :, 0:128], z_hbm.at[from_left, :, 0:128], chip(xr)
        )
        z_left.wait_recv()
        from_right = 2 * xr + c
        round_left = remote(
            z_hbm.at[from_right, :, 128:256], z_hbm.at[from_right, :, 128:256], chip(xl)
        )
        handed_z = [
            remote(z_hbm.at[from_left], z_hbm.at[from_left], partner),
            remote(z_hbm.at[from_right], z_hbm.at[from_right], partner),
        ]
        gram_copy = exchange_core(2, gram_copy)
        gram_copy.wait_recv()
    with jax.named_scope("quad"):
        scale_quad, _, _ = inverse_root(2, unpacked(v["swapped_sum"][2, 0:192]), lambda: None)
        arrived([round_right, round_left])
        from_far = 2 * opposite + c
        handed_z.append(remote(z_hbm.at[from_far], z_hbm.at[from_far], partner))
        nested = dot3(get(4), root(2)) * scale_quad
        v["nested_v"][...] = nested
        nested_copy = local(v["nested_v"], nested_hbm)
        wc_copy.wait_recv()
        summary = dot3(root(2), split(v["wc"][1] + v["wc_in"][1])) * scale_quad
        inner = dot3(split(nested), split(summary))
        inner_high, inner_low = split(
            dot3((v["root_v"][0], v["root_v"][1]), split(inner))
        )
        v["xi_v"][0] = inner_high
        v["xi_v"][1] = inner_low
        inner_copy = local(v["xi_v"], inner_hbm)
        arrived([z_partner] + handed_z)
        for copy in (z_local, root_copy, nested_copy, inner_copy):
            copy.wait()
        assert len(sent) <= N_COPIES and len(locals_) <= 12
        for copy in sent:
            copy.wait_send()


OUT_SCRATCH = dict(
    z=pltpu.VMEM((SAMP, 2, RANK, RANK), BF16),
    root=pltpu.VMEM((2, RANK, RANK), BF16),
    inner=pltpu.VMEM((2, RANK, 128), BF16),
    nested=pltpu.VMEM((RANK, RANK), F32),
    basis=pltpu.VMEM((SAMP, RANK, RANK), F32),
    turned=pltpu.VMEM((2, 128, RANK), F32),
    approx=pltpu.VMEM((64, SAMP * RANK), F32),
    read=pltpu.SemaphoreType.DMA((SAMP + 3,)),
    write=pltpu.SemaphoreType.DMA((SAMP + 2,)),
)


def outputs(*refs):
    z_hbm, root_hbm, nested_hbm, inner_hbm, basis_out, nested_out, approx_out = refs[:7]
    v = dict(zip(OUT_SCRATCH, refs[7:]))
    core = lax.rem(lax.axis_index("samp"), 2)
    reads = [
        pltpu.make_async_copy(root_hbm, v["root"], v["read"].at[SAMP]),
        pltpu.make_async_copy(inner_hbm, v["inner"], v["read"].at[SAMP + 1]),
    ]
    blocks = [
        pltpu.make_async_copy(z_hbm.at[i], v["z"].at[i], v["read"].at[i]) for i in range(SAMP)
    ]
    nested_in = pltpu.make_async_copy(nested_hbm, v["nested"], v["read"].at[SAMP + 2])
    for copy in reads + blocks + [nested_in]:
        copy.start()
    for copy in reads:
        copy.wait()
    writes = []
    for i in range(SAMP):
        blocks[i].wait()
        rows = pl.ds(RANK * i, RANK)
        z = v["z"][i, 0], v["z"][i, 1]
        v["basis"][i] = dot3(z, (v["root"][0], v["root"][1]))
        writes.append(pltpu.make_async_copy(v["basis"].at[i], basis_out.at[rows], v["write"].at[i]))
        writes[-1].start()
        v["turned"][i % 2] = dot3(z, (v["inner"][0], v["inner"][1])).T
        v["approx"][:, rows] = v["turned"][i % 2, pl.ds(pl.multiple_of(core * 64, 64), 64)]
    writes.append(pltpu.make_async_copy(v["approx"], approx_out, v["write"].at[SAMP]))
    writes[-1].start()
    nested_in.wait()
    writes.append(pltpu.make_async_copy(v["nested"], nested_out, v["write"].at[SAMP + 1]))
    writes[-1].start()
    for copy in writes:
        copy.wait()


def on_device(n_rows, coupling_tiles, tile_columns, sample_matrix, phi_leaf, phi_pair, phi_quad):
    rows = sample_matrix.shape[0]
    share = sample_matrix.shape[1] // SAMP
    any_ = pl.BlockSpec(memory_space=pl.ANY)
    z, root, nested, inner = pl.pallas_call(
        functools.partial(kernel, n_rows),
        out_shape=(
            jax.ShapeDtypeStruct((SAMP, 2, RANK, RANK), BF16),
            jax.ShapeDtypeStruct((2, RANK, RANK), BF16),
            jax.ShapeDtypeStruct((RANK, RANK), F32),
            jax.ShapeDtypeStruct((2, RANK, 128), BF16),
        ),
        in_specs=[any_] * 6,
        out_specs=(any_,) * 4,
        scratch_shapes=list(SCRATCH.values()),
        compiler_params=pltpu.CompilerParams(
            collective_id=0, has_side_effects=True, vmem_limit_bytes=56 * 2**20
        ),
        name="hss",
    )(
        coupling_tiles,
        tile_columns.T,
        sample_matrix.reshape(16, 128, 512),
        phi_leaf,
        phi_pair,
        phi_quad,
    )
    basis, nested, approx_t = pl.pallas_call(
        outputs,
        out_shape=(
            jax.ShapeDtypeStruct((rows, RANK), F32),
            jax.ShapeDtypeStruct((RANK, RANK), F32),
            jax.ShapeDtypeStruct((share, rows), F32),
        ),
        in_specs=[any_] * 4,
        out_specs=(any_,) * 3,
        scratch_shapes=list(OUT_SCRATCH.values()),
        compiler_params=pltpu.CompilerParams(vmem_limit_bytes=56 * 2**20),
        name="expand",
    )(z, root, nested, inner)
    return basis, nested, approx_t.T


def solution(mesh):
    return jax.shard_map(
        functools.partial(on_device, mesh.shape["rows"]),
        mesh=mesh,
        in_specs=(P("rows", "samp", None, None), P("rows", "samp"), P("rows", None), P(), P(), P()),
        out_specs=(P("rows", None), P("rows", None), P("rows", "samp")),
        check_vma=False,
    )
```

```python
import functools

import jax
import jax.numpy as jnp
from jax import lax
from jax.experimental import pallas as pl
from jax.experimental.pallas import tpu as pltpu
from jax.sharding import PartitionSpec as P

NS_ITERS = 5
MESH = pl.DeviceIdType.MESH
F32 = jnp.float32
BF16 = jnp.bfloat16
NT, NN = ((1,), (1,)), ((1,), (0,))

N_COPIES = 112
HANDED = 3
SAMP = 8
CHIPS = 4
RANK = 256

I16 = jnp.int16

SCRATCH = dict(
    ext=pltpu.VMEM((48, 128, 256), BF16),
    tiles=pltpu.VMEM((2, 16, 4, 128, 128), BF16),
    cols_in=pltpu.VMEM((4, 16), jnp.int32),
    cols=pltpu.SMEM((2, 4, 16), jnp.int32),
    phi=pltpu.VMEM((3, 512, 256), F32),
    phi_h=pltpu.VMEM((3, 512, 256), BF16),
    phi_l=pltpu.VMEM((3, 512, 256), BF16),
    part=pltpu.VMEM((4, 128, 256), F32),
    code=pltpu.VMEM((12, 128, 256), I16),
    code_in=pltpu.VMEM((12, 128, 256), I16),
    unit=pltpu.VMEM((12, 8, 128), F32),
    unit_in=pltpu.VMEM((12, 8, 128), F32),
    swap=pltpu.VMEM((256, 256), F32),
    samp=pltpu.VMEM((2, 256, 256), F32),
    mine=pltpu.VMEM((3, 256, 256), F32),
    in_core=pltpu.VMEM((3, 128, 256), F32),
    chip=pltpu.VMEM((3, 128, 256), F32),
    in_chip=pltpu.VMEM((3, 128, 256), F32),
    two=pltpu.VMEM((3, 128, 256), F32),
    in_two=pltpu.VMEM((3, 128, 256), F32),
    full=pltpu.VMEM((3, 256, 256), F32),
    wpart=pltpu.VMEM((2, 4, 128, 128), F32),
    w_core=pltpu.VMEM((4, 128, 128), F32),
    w_chip=pltpu.VMEM((4, 128, 128), F32),
    w_in=pltpu.VMEM((3, 128, 128), F32),
    wcol=pltpu.VMEM((2, 128, 128), F32),
    z_own=pltpu.VMEM((2, 256, 256), BF16),
    yx_h=pltpu.VMEM((512, 256), BF16),
    yx_l=pltpu.VMEM((512, 256), BF16),
    f_h=pltpu.VMEM((256, 256), BF16),
    f_l=pltpu.VMEM((256, 256), BF16),
    x_h=pltpu.VMEM((3, 256, 256), BF16),
    x_l=pltpu.VMEM((3, 256, 256), BF16),
    a_h=pltpu.VMEM((6, 256, 256), BF16),
    a_l=pltpu.VMEM((6, 256, 256), BF16),
    t_h=pltpu.VMEM((256, 256), BF16),
    t_l=pltpu.VMEM((256, 256), BF16),
    swapped_pair=pltpu.VMEM((3, 256, 256), F32),
    swapped_in=pltpu.VMEM((3, 128, 256), F32),
    swapped_sum=pltpu.VMEM((3, 256, 256), F32),
    wc=pltpu.VMEM((2, 256, 128), F32),
    wc_in=pltpu.VMEM((2, 256, 128), F32),
    root_v=pltpu.VMEM((2, 256, 256), BF16),
    xi_v=pltpu.VMEM((2, 256, 128), BF16),
    nested_v=pltpu.VMEM((256, 256), F32),
    local=pltpu.SemaphoreType.DMA((12,)),
    send=pltpu.SemaphoreType.DMA((N_COPIES,)),
    recv=pltpu.SemaphoreType.DMA((N_COPIES,)),
)


def split(value):
    high = value.astype(BF16)
    return high, (value - high.astype(F32)).astype(BF16)


def dot3(a, b):
    left = jnp.concatenate([a[0], a[0], a[1]], axis=1)
    right = jnp.concatenate([b[0], b[1], b[0]], axis=0)
    return lax.dot_general(left, right, (NN, ((), ())), preferred_element_type=F32)


def dot3_nt(a, b):
    left = jnp.concatenate([a[0], a[0], a[1]], axis=1)
    right = jnp.concatenate([b[0], b[1], b[0]], axis=1)
    return lax.dot_general(left, right, (NT, ((), ())), preferred_element_type=F32)


def kernel(n_rows, *refs):
    tiles_hbm, cols_hbm, b_hbm, phi0_hbm, phi1_hbm, phi2_hbm = refs[:6]
    z_hbm, root_hbm, nested_hbm, inner_hbm = refs[6:10]
    v = dict(zip(SCRATCH, refs[10:]))

    r = lax.axis_index("rows")
    s = lax.axis_index("samp")
    x = lax.div(s, 2)
    c = lax.rem(s, 2)
    y = lax.rem(r, 4)
    xr, opposite, xl = (lax.rem(x + o, CHIPS) for o in (1, 2, 3))

    def chip(index):
        return (r, 2 * index + c)

    partner = (r, s + 1 - 2 * c)
    left = (lax.rem(r + n_rows - 1, n_rows), s)
    right = (lax.rem(r + 1, n_rows), s)
    sibling = (r + 1 - 2 * lax.rem(r, 2), s)
    cousin = (r + 3 - 2 * y, s)
    first_dim = x + 1 - 2 * lax.rem(x, 2)
    second_dim = 3 - x

    barrier = pltpu.get_barrier_semaphore()
    peers = [partner, chip(xr), chip(opposite), chip(xl), left, right, cousin]
    for peer in peers:
        pl.semaphore_signal(barrier, inc=1, device_id=peer, device_id_type=MESH)

    locals_ = []

    def local(src, dst):
        copy = pltpu.make_async_copy(src, dst, v["local"].at[len(locals_)])
        locals_.append(copy)
        copy.start()
        return copy

    sent = []

    def remote(src, dst, device):
        i = len(sent)
        copy = pltpu.make_async_remote_copy(
            src_ref=src,
            dst_ref=dst,
            send_sem=v["send"].at[i],
            recv_sem=v["recv"].at[i],
            device_id=device,
            device_id_type=MESH,
        )
        sent.append(copy)
        copy.start()
        return copy

    def z_at(origin, start=0, size=256):
        return z_hbm.at[:, pl.ds(pl.multiple_of(256 * origin + start, 128), size)]

    mine_half = pl.ds(pl.multiple_of(c * 256, 256), 256)
    own_cols = local(cols_hbm, v["cols"].at[0])
    pl.semaphore_wait(barrier, len(peers))
    with jax.named_scope("halo"):
        def to_both(at, count):
            piece = b_hbm.at[pl.ds(at, count), :, mine_half]
            return (
                remote(piece, v["ext"].at[pl.ds(at, count)], right),
                remote(piece, v["ext"].at[pl.ds(32 + at, count)], left),
            )

        direct = [to_both(4 * x + i, 1) for i in range(HANDED)]
        cols_copy = remote(cols_hbm, v["cols_in"], partner)
        rest = 4 - HANDED
        far_copies = [
            *to_both(4 * xr + HANDED, rest),
            *to_both(4 * xl + HANDED, rest),
            *to_both(4 * x + HANDED, rest),
            *to_both(4 * opposite, 4),
        ]
        tiles_copy = remote(tiles_hbm, v["tiles"].at[1], partner)
        own_tiles = local(tiles_hbm, v["tiles"].at[0])
        own_b = local(b_hbm.at[:, :, mine_half], v["ext"].at[pl.ds(16, 16)])
        phis = [local(p, v["phi"].at[i]) for i, p in enumerate((phi0_hbm, phi1_hbm, phi2_hbm))]
        handed = []
        for i in range(HANDED):
            for side in range(2):
                direct[i][side].wait_recv()
                piece = v["ext"].at[32 * side + 4 * x + i]
                handed.append(remote(piece, piece, chip(xr)))
                handed.append(remote(piece, piece, chip(xl)))
        for i, copy in enumerate(phis):
            copy.wait()
            high, low = split(v["phi"][i])
            v["phi_h"][i] = high
            v["phi_l"][i] = low
        cols_copy.wait_recv()
        other_cols = local(v["cols_in"], v["cols"].at[1])
        for copy in (own_cols, own_tiles, own_b, other_cols):
            copy.wait()
        for copy in [tiles_copy] + far_copies + handed:
            copy.wait_recv()
    first = (r - 1) * 16

    def product(row):
        lhs = jnp.concatenate(
            [v["tiles"][h, row, k] for h in range(2) for k in range(4)], axis=1
        )
        rhs = jnp.concatenate(
            [
                v["ext"][jnp.clip(v["cols"][h, k, row] - first, 0, 47)]
                for h in range(2)
                for k in range(4)
            ],
            axis=0,
        )
        return jnp.dot(lhs, rhs, preferred_element_type=F32)

    def coded(i, value, device):
        top = jnp.maximum(jnp.max(jnp.abs(value), axis=1, keepdims=True), 1e-30)
        v["code"][i] = jnp.round(value * (32767.0 / top)).astype(jnp.int32).astype(I16)
        v["unit"][i] = jnp.broadcast_to(top * (1 / 32767.0), (128, 128)).T[0:8]
        return (
            remote(v["code"].at[i], v["code_in"].at[i], device),
            remote(v["unit"].at[i], v["unit_in"].at[i], device),
        )

    def decoded(i, copies):
        for copy in copies:
            copy.wait_recv()
        unit = jnp.broadcast_to(v["unit_in"][i, 0:1], (128, 128)).T
        return v["code_in"][i].astype(jnp.int32).astype(F32) * jnp.concatenate([unit, unit], axis=1)

    with jax.named_scope("product"):
        up_far, down_far, up_near, down_near, up_sum, down_sum = ([] for _ in range(6))
        for j in range(2):
            up_far.append(coded(j, product(4 * opposite + j), chip(xr)))
            down_far.append(coded(2 + j, product(4 * opposite + 2 + j), chip(xl)))
        for j in range(2):
            down_near.append(coded(4 + j, product(4 * xr + 2 + j), chip(xr)))
            up_near.append(coded(6 + j, product(4 * xl + j), chip(xl)))
        for j in range(2):
            up_sum.append(coded(8 + j, product(4 * xr + j) + decoded(j, up_far[j]), chip(xr)))
            down_sum.append(
                coded(10 + j, product(4 * xl + 2 + j) + decoded(2 + j, down_far[j]), chip(xl))
            )
        for j in range(4):
            v["part"][j] = product(4 * x + j)
        for j in range(2):
            v["part"][j] = v["part"][j] + decoded(6 + j, up_near[j])
            v["part"][2 + j] = v["part"][2 + j] + decoded(4 + j, down_near[j])
        for j in range(2):
            rows = pl.ds(128 * j, 128)
            upper = v["part"][j] + decoded(8 + j, up_sum[j])
            lower = v["part"][2 + j] + decoded(10 + j, down_sum[j])
            v["swap"][rows] = jnp.where(c == 0, lower, upper)
            v["samp"][c, rows] = jnp.where(c == 0, upper, lower)
        swapped = remote(v["swap"], v["samp"].at[c], partner)
        swapped.wait_recv()
    def put(slot, value):
        high, low = split(value)
        v["a_h"][slot] = high
        v["a_l"][slot] = low

    def get(slot):
        return v["a_h"][slot], v["a_l"][slot]

    def phi_of(i):
        return v["phi_h"][i], v["phi_l"][i]

    def transposed():
        return v["t_h"][...], v["t_l"][...]

    def packed(gram):
        corner = jnp.concatenate([gram[128:192, 128:256], gram[192:256, 128:256]], axis=1)
        return jnp.concatenate([gram[0:128], corner], axis=0)

    def unpacked(rows):
        corner = jnp.concatenate([rows[128:192, 0:128], rows[128:192, 128:256]], axis=0)
        low = jnp.concatenate([rows[0:128, 128:256].T, corner], axis=1)
        return jnp.concatenate([rows[0:128], low], axis=0)

    def core_rows(size, core):
        return pl.ds(pl.multiple_of(core * size, size), size)

    def half_of(m):
        return 96 if m == 0 else 128

    def sum_core(m):
        size = half_of(m)
        rows = core_rows(size, 1 - c)
        return [remote(v["mine"].at[m, rows], v["in_core"].at[m, 0:size], partner)]

    def crossed(ref, into, m, one, two):
        size, cut = half_of(m), half_of(m) // 2
        return [
            remote(v[ref].at[m, 0:cut], v[into].at[m, 0:cut], chip(one)),
            remote(v[ref].at[m, cut:size], v[into].at[m, cut:size], chip(two)),
        ]

    def arrived(copies):
        for copy in copies:
            copy.wait_recv()

    def sum_first(m, copies):
        arrived(copies)
        size = half_of(m)
        v["chip"][m, 0:size] = v["mine"][m, core_rows(size, c)] + v["in_core"][m, 0:size]
        return crossed("chip", "in_chip", m, first_dim, second_dim)

    def sum_second(m, copies):
        arrived(copies)
        size = half_of(m)
        v["two"][m, 0:size] = v["chip"][m, 0:size] + v["in_chip"][m, 0:size]
        return crossed("two", "in_two", m, second_dim, first_dim)

    def sum_last(m, copies):
        arrived(copies)
        size = half_of(m)
        rows = core_rows(size, c)
        v["full"][m, rows] = v["two"][m, 0:size] + v["in_two"][m, 0:size]
        return [remote(v["full"].at[m, rows], v["full"].at[m, rows], partner)]

    with jax.named_scope("sums"):
        for half in range(2):
            put(half, v["samp"][half])
        sample = (
            jnp.concatenate([v["a_h"][0], v["a_h"][1]], axis=1),
            jnp.concatenate([v["a_l"][0], v["a_l"][1]], axis=1),
        )
        z = dot3(sample, phi_of(0))
        z_high, z_low = split(z)
        v["z_own"][0] = z_high
        v["z_own"][1] = z_low
        t_high, t_low = split(z.T)
        v["t_h"][...] = t_high
        v["t_l"][...] = t_low
        v["mine"][0, 0:192] = packed(dot3(transposed(), (v["z_own"][0], v["z_own"][1])))
        sum_g = sum_core(0)
        z_local = local(v["z_own"], z_at(s))
        for half in range(2):
            w = dot3(transposed(), get(half))
            put(3 + half, w)
            for q in range(4):
                v["wpart"][q // 2, 2 * half + q % 2] = w[
                    128 * (q // 2) : 128 * (q // 2) + 128, 128 * (q % 2) : 128 * (q % 2) + 128
                ]
        sum_g = sum_first(0, sum_g)
        w_all = (
            jnp.concatenate([v["a_h"][3], v["a_h"][4]], axis=1),
            jnp.concatenate([v["a_l"][3], v["a_l"][4]], axis=1),
        )
        v["mine"][1] = dot3(w_all, phi_of(1))
        sum_n = sum_core(1)
        v["mine"][2] = dot3(w_all, phi_of(2))
        sum_o = sum_core(2)
        w_core = remote(v["wpart"].at[1 - c], v["w_core"], partner)
        sum_n = sum_first(1, sum_n)
        sum_g = sum_second(0, sum_g)
        sum_o = sum_first(2, sum_o)
        sum_n = sum_second(1, sum_n)
        sum_o = sum_second(2, sum_o)
        sum_g = sum_last(0, sum_g)
        w_core.wait_recv()
        v["w_chip"][...] = v["wpart"][c] + v["w_core"][...]
        arrived(sum_g)
    eye = jnp.where(
        lax.broadcasted_iota(jnp.int32, (RANK, RANK), 0)
        == lax.broadcasted_iota(jnp.int32, (RANK, RANK), 1),
        F32(1.5),
        F32(0),
    )

    def inverse_root(level, gram, meanwhile):
        norm = (
            jnp.sqrt(
                jnp.sum(jnp.sum(gram * gram, axis=1, keepdims=True), axis=0, keepdims=True)
            )
            + 1e-06
        )
        y0 = gram / norm
        factor = split(eye - 0.5 * y0)
        new_high, new_low = split(dot3(split(y0), factor))
        v["yx_h"][0:256] = new_high
        v["yx_l"][0:256] = new_low
        v["yx_h"][256:512] = factor[0]
        v["yx_l"][256:512] = factor[1]

        def make_factor():
            both = dot3(
                (v["yx_h"][256:512], v["yx_l"][256:512]), (v["yx_h"][0:256], v["yx_l"][0:256])
            )
            high, low = split(eye - 0.5 * both)
            v["f_h"][...] = high
            v["f_l"][...] = low

        def step(_, carry):
            make_factor()
            high, low = split(
                dot3((v["yx_h"][...], v["yx_l"][...]), (v["f_h"][...], v["f_l"][...]))
            )
            v["yx_h"][...] = high
            v["yx_l"][...] = low
            return carry

        step(0, 0)
        passed_on = meanwhile()
        lax.fori_loop(0, NS_ITERS - 3, step, 0)
        make_factor()
        result = dot3((v["yx_h"][256:512], v["yx_l"][256:512]), (v["f_h"][...], v["f_l"][...]))
        high, low = split(result)
        v["x_h"][level] = high
        v["x_l"][level] = low
        return 1.0 / jnp.sqrt(norm), result, passed_on

    def root(level):
        return v["x_h"][level], v["x_l"][level]

    def exchange(i, device):
        size = 128 if i == 1 else 96
        rows = core_rows(size, c)
        return remote(v["swapped_pair"].at[i, rows], v["swapped_in"].at[i, 0:size], device)

    def exchange_core(i, copy):
        copy.wait_recv()
        size = 128 if i == 1 else 96
        rows = core_rows(size, c)
        v["swapped_sum"][i, rows] = v["swapped_pair"][i, rows] + v["swapped_in"][i, 0:size]
        return remote(v["swapped_sum"].at[i, rows], v["swapped_sum"].at[i, rows], partner)

    with jax.named_scope("leaf"):

        def last_sums():
            last_n, last_o = sum_last(1, sum_n), sum_last(2, sum_o)
            columns = [
                remote(v["w_chip"].at[d], v["w_in"].at[o], chip(d))
                for o, d in enumerate((xr, opposite, xl))
            ]
            return last_n, last_o, columns

        scale_leaf, x_leaf, (sum_n, sum_o, w_copies) = inverse_root(0, unpacked(v["full"][0, 0:192]), last_sums)
        arrived(sum_n)
        zp = dot3(root(0), split(v["full"][1])) * scale_leaf
        put(0, zp)
        t_high, t_low = split(zp.T)
        v["t_h"][...] = t_high
        v["t_l"][...] = t_low
        v["swapped_pair"][0, 0:192] = packed(dot3(transposed(), get(0)))
        gram_copy = exchange(0, sibling)
        z_right = remote(v["z_own"], z_at(s), chip(xr))
        z_left = remote(v["z_own"], z_at(s), chip(xl))
        z_partner = remote(v["z_own"], z_at(s), partner)
        arrived(sum_o)
        put(5, dot3(root(0), split(v["full"][2])) * scale_leaf)
        v["swapped_pair"][1] = dot3(transposed(), get(5))
        cross_copy = exchange(1, sibling)
        root_high, root_low = split(x_leaf * scale_leaf)
        v["root_v"][0] = root_high
        v["root_v"][1] = root_low
        root_copy = local(v["root_v"], root_hbm)
        gram_copy = exchange_core(0, gram_copy)
        arrived(w_copies)
        v["wcol"][c] = v["w_chip"][x] + v["w_in"][0] + v["w_in"][1] + v["w_in"][2]
        wcol_copy = remote(v["wcol"].at[c], v["wcol"].at[c], partner)
        wcol_copy.wait_recv()
        coarse = dot3(root(0), split(v["wcol"][...].reshape(256, 128))) * scale_leaf
        v["wc"][0] = dot3(transposed(), split(coarse))
        wc_copy = remote(v["wc"].at[0], v["wc_in"].at[0], sibling)
        gram_copy.wait_recv()
    with jax.named_scope("pair"):
        scale_pair, _, cross_copy = inverse_root(
            1, unpacked(v["swapped_sum"][0, 0:192]), lambda: exchange_core(1, cross_copy)
        )
        put(2, dot3(get(0), root(1)) * scale_pair)
        cross_copy.wait_recv()
        zq = dot3(root(1), split(v["swapped_sum"][1])) * scale_pair
        put(1, zq)
        t_high, t_low = split(zq.T)
        v["t_h"][...] = t_high
        v["t_l"][...] = t_low
        v["swapped_pair"][2, 0:192] = packed(dot3(transposed(), get(1)))
        gram_copy = exchange(2, cousin)
        put(4, dot3(get(2), get(1)))
        wc_copy.wait_recv()
        middle = dot3(root(1), split(v["wc"][0] + v["wc_in"][0])) * scale_pair
        v["wc"][1] = dot3(transposed(), split(middle))
        wc_copy = remote(v["wc"].at[1], v["wc_in"].at[1], cousin)
        z_right.wait_recv()
        from_left = 2 * xl + c
        round_right = remote(
            z_at(from_left, 0, 128), z_at(from_left, 0, 128), chip(xr)
        )
        z_left.wait_recv()
        from_right = 2 * xr + c
        round_left = remote(
            z_at(from_right, 128, 128), z_at(from_right, 128, 128), chip(xl)
        )
        handed_z = [
            remote(z_at(from_left), z_at(from_left), partner),
            remote(z_at(from_right), z_at(from_right), partner),
        ]
        gram_copy = exchange_core(2, gram_copy)
        gram_copy.wait_recv()
    with jax.named_scope("quad"):
        scale_quad, _, _ = inverse_root(2, unpacked(v["swapped_sum"][2, 0:192]), lambda: None)
        arrived([round_right, round_left])
        from_far = 2 * opposite + c
        handed_z.append(remote(z_at(from_far), z_at(from_far), partner))
        nested = dot3(get(4), root(2)) * scale_quad
        v["nested_v"][...] = nested
        nested_copy = local(v["nested_v"], nested_hbm)
        wc_copy.wait_recv()
        summary = dot3(root(2), split(v["wc"][1] + v["wc_in"][1])) * scale_quad
        inner = dot3(split(nested), split(summary))
        inner_high, inner_low = split(
            dot3((v["root_v"][0], v["root_v"][1]), split(inner))
        )
        v["xi_v"][0] = inner_high
        v["xi_v"][1] = inner_low
        inner_copy = local(v["xi_v"], inner_hbm)
        arrived([z_partner] + handed_z)
        for copy in (z_local, root_copy, nested_copy, inner_copy):
            copy.wait()
        assert len(sent) <= N_COPIES and len(locals_) <= 12
        for copy in sent:
            copy.wait_send()


def outputs(z_ref, root_ref, nested_ref, inner_ref, basis_out, nested_out, approx_out, turned):
    core = lax.rem(lax.axis_index("samp"), 2)
    z = z_ref[0], z_ref[1]
    basis_out[...] = dot3(z, (root_ref[0], root_ref[1]))
    turned[...] = dot3(z, (inner_ref[0], inner_ref[1])).T
    approx_out[...] = turned[pl.ds(pl.multiple_of(core * 64, 64), 64)]
    nested_out[...] = nested_ref[...]


def on_device(n_rows, coupling_tiles, tile_columns, sample_matrix, phi_leaf, phi_pair, phi_quad):
    rows = sample_matrix.shape[0]
    share = sample_matrix.shape[1] // SAMP
    any_ = pl.BlockSpec(memory_space=pl.ANY)
    z, root, nested, inner = pl.pallas_call(
        functools.partial(kernel, n_rows),
        out_shape=(
            jax.ShapeDtypeStruct((2, SAMP * RANK, RANK), BF16),
            jax.ShapeDtypeStruct((2, RANK, RANK), BF16),
            jax.ShapeDtypeStruct((RANK, RANK), F32),
            jax.ShapeDtypeStruct((2, RANK, 128), BF16),
        ),
        in_specs=[any_] * 6,
        out_specs=(any_,) * 4,
        scratch_shapes=list(SCRATCH.values()),
        compiler_params=pltpu.CompilerParams(
            collective_id=0, has_side_effects=True, vmem_limit_bytes=56 * 2**20
        ),
        name="hss",
    )(
        coupling_tiles,
        tile_columns.T,
        sample_matrix.reshape(16, 128, 512),
        phi_leaf,
        phi_pair,
        phi_quad,
    )
    basis, nested, approx_t = pl.pallas_call(
        outputs,
        grid=(SAMP // 2,),
        out_shape=(
            jax.ShapeDtypeStruct((rows, RANK), F32),
            jax.ShapeDtypeStruct((RANK, RANK), F32),
            jax.ShapeDtypeStruct((share, rows), F32),
        ),
        in_specs=[
            pl.BlockSpec((2, 2 * RANK, RANK), lambda i: (0, i, 0)),
            pl.BlockSpec((2, RANK, RANK), lambda i: (0, 0, 0)),
            pl.BlockSpec((RANK, RANK), lambda i: (0, 0)),
            pl.BlockSpec((2, RANK, 128), lambda i: (0, 0, 0)),
        ],
        out_specs=(
            pl.BlockSpec((2 * RANK, RANK), lambda i: (i, 0)),
            pl.BlockSpec((RANK, RANK), lambda i: (0, 0)),
            pl.BlockSpec((share, 2 * RANK), lambda i: (0, i)),
        ),
        scratch_shapes=[pltpu.VMEM((128, 2 * RANK), F32)],
        compiler_params=pltpu.CompilerParams(vmem_limit_bytes=56 * 2**20),
        name="expand",
    )(z, root, nested, inner)
    return basis, nested, approx_t.T


def solution(mesh):
    return jax.shard_map(
        functools.partial(on_device, mesh.shape["rows"]),
        mesh=mesh,
        in_specs=(P("rows", "samp", None, None), P("rows", "samp"), P("rows", None), P(), P(), P()),
        out_specs=(P("rows", None), P("rows", None), P("rows", "samp")),
        check_vma=False,
    )
```

```python
import functools

import jax
import jax.numpy as jnp
from jax import lax
from jax.experimental import pallas as pl
from jax.experimental.pallas import tpu as pltpu
from jax.sharding import PartitionSpec as P

NS_ITERS = 5
MESH = pl.DeviceIdType.MESH
F32 = jnp.float32
BF16 = jnp.bfloat16
NT, NN = ((1,), (1,)), ((1,), (0,))

N_COPIES = 112
SAMP = 8
CHIPS = 4
RANK = 256

I16 = jnp.int16

SCRATCH = dict(
    ext=pltpu.VMEM((48, 128, 256), BF16),
    tiles=pltpu.VMEM((2, 16, 4, 128, 128), BF16),
    cols_in=pltpu.VMEM((4, 16), jnp.int32),
    cols=pltpu.SMEM((2, 4, 16), jnp.int32),
    phi=pltpu.VMEM((3, 512, 256), F32),
    phi_h=pltpu.VMEM((3, 512, 256), BF16),
    phi_l=pltpu.VMEM((3, 512, 256), BF16),
    part=pltpu.VMEM((4, 128, 256), F32),
    code=pltpu.VMEM((12, 128, 256), I16),
    code_in=pltpu.VMEM((12, 128, 256), I16),
    unit=pltpu.VMEM((12, 8, 128), F32),
    unit_in=pltpu.VMEM((12, 8, 128), F32),
    swap=pltpu.VMEM((256, 256), F32),
    samp=pltpu.VMEM((2, 256, 256), F32),
    mine=pltpu.VMEM((3, 256, 256), F32),
    in_core=pltpu.VMEM((3, 128, 256), F32),
    chip=pltpu.VMEM((3, 128, 256), F32),
    in_chip=pltpu.VMEM((3, 128, 256), F32),
    two=pltpu.VMEM((3, 128, 256), F32),
    in_two=pltpu.VMEM((3, 128, 256), F32),
    full=pltpu.VMEM((3, 256, 256), F32),
    wpart=pltpu.VMEM((2, 4, 128, 128), F32),
    w_core=pltpu.VMEM((4, 128, 128), F32),
    w_chip=pltpu.VMEM((4, 128, 128), F32),
    w_in=pltpu.VMEM((3, 128, 128), F32),
    wcol=pltpu.VMEM((2, 128, 128), F32),
    z_own=pltpu.VMEM((2, 256, 256), BF16),
    yx_h=pltpu.VMEM((512, 256), BF16),
    yx_l=pltpu.VMEM((512, 256), BF16),
    f_h=pltpu.VMEM((256, 256), BF16),
    f_l=pltpu.VMEM((256, 256), BF16),
    x_h=pltpu.VMEM((3, 256, 256), BF16),
    x_l=pltpu.VMEM((3, 256, 256), BF16),
    a_h=pltpu.VMEM((6, 256, 256), BF16),
    a_l=pltpu.VMEM((6, 256, 256), BF16),
    t_h=pltpu.VMEM((256, 256), BF16),
    t_l=pltpu.VMEM((256, 256), BF16),
    swapped_pair=pltpu.VMEM((3, 256, 256), F32),
    swapped_in=pltpu.VMEM((3, 128, 256), F32),
    swapped_sum=pltpu.VMEM((3, 256, 256), F32),
    wc=pltpu.VMEM((2, 256, 128), F32),
    wc_in=pltpu.VMEM((2, 256, 128), F32),
    root_v=pltpu.VMEM((2, 256, 256), BF16),
    xi_v=pltpu.VMEM((2, 256, 128), BF16),
    nested_v=pltpu.VMEM((256, 256), F32),
    local=pltpu.SemaphoreType.DMA((12,)),
    send=pltpu.SemaphoreType.DMA((N_COPIES,)),
    recv=pltpu.SemaphoreType.DMA((N_COPIES,)),
)


def split(value):
    high = value.astype(BF16)
    return high, (value - high.astype(F32)).astype(BF16)


def dot3(a, b):
    left = jnp.concatenate([a[0], a[0], a[1]], axis=1)
    right = jnp.concatenate([b[0], b[1], b[0]], axis=0)
    return lax.dot_general(left, right, (NN, ((), ())), preferred_element_type=F32)


def dot3_nt(a, b):
    left = jnp.concatenate([a[0], a[0], a[1]], axis=1)
    right = jnp.concatenate([b[0], b[1], b[0]], axis=1)
    return lax.dot_general(left, right, (NT, ((), ())), preferred_element_type=F32)


def kernel(n_rows, *refs):
    tiles_hbm, cols_hbm, b_hbm, phi0_hbm, phi1_hbm, phi2_hbm = refs[:6]
    z_hbm, root_hbm, nested_hbm, inner_hbm = refs[6:10]
    v = dict(zip(SCRATCH, refs[10:]))

    r = lax.axis_index("rows")
    s = lax.axis_index("samp")
    x = lax.div(s, 2)
    c = lax.rem(s, 2)
    y = lax.rem(r, 4)
    xr, opposite, xl = (lax.rem(x + o, CHIPS) for o in (1, 2, 3))

    def chip(index):
        return (r, 2 * index + c)

    partner = (r, s + 1 - 2 * c)
    left = (lax.rem(r + n_rows - 1, n_rows), s)
    right = (lax.rem(r + 1, n_rows), s)
    sibling = (r + 1 - 2 * lax.rem(r, 2), s)
    cousin = (r + 3 - 2 * y, s)
    first_dim = x + 1 - 2 * lax.rem(x, 2)
    second_dim = 3 - x

    barrier = pltpu.get_barrier_semaphore()
    peers = [partner, chip(xr), chip(opposite), chip(xl), left, right, cousin]
    for peer in peers:
        pl.semaphore_signal(barrier, inc=1, device_id=peer, device_id_type=MESH)

    locals_ = []

    def local(src, dst):
        copy = pltpu.make_async_copy(src, dst, v["local"].at[len(locals_)])
        locals_.append(copy)
        copy.start()
        return copy

    sent = []

    def remote(src, dst, device):
        i = len(sent)
        copy = pltpu.make_async_remote_copy(
            src_ref=src,
            dst_ref=dst,
            send_sem=v["send"].at[i],
            recv_sem=v["recv"].at[i],
            device_id=device,
            device_id_type=MESH,
        )
        sent.append(copy)
        copy.start()
        return copy

    def z_at(origin, start=0, size=256):
        return z_hbm.at[:, pl.ds(pl.multiple_of(256 * origin + start, 128), size)]

    mine_half = pl.ds(pl.multiple_of(c * 256, 256), 256)
    own_cols = local(cols_hbm, v["cols"].at[0])
    pl.semaphore_wait(barrier, len(peers))
    with jax.named_scope("halo"):
        def to_both(at, count):
            piece = b_hbm.at[pl.ds(at, count), :, mine_half]
            return (
                remote(piece, v["ext"].at[pl.ds(at, count)], right),
                remote(piece, v["ext"].at[pl.ds(32 + at, count)], left),
            )

        direct = [to_both(4 * x + i, 1) for i in range(4)]
        cols_copy = remote(cols_hbm, v["cols_in"], partner)
        far_copies = to_both(4 * opposite, 4)
        tiles_copy = remote(tiles_hbm, v["tiles"].at[1], partner)
        own_tiles = local(tiles_hbm, v["tiles"].at[0])
        own_b = local(b_hbm.at[:, :, mine_half], v["ext"].at[pl.ds(16, 16)])
        phis = [local(p, v["phi"].at[i]) for i, p in enumerate((phi0_hbm, phi1_hbm, phi2_hbm))]
        handed = []
        for i in range(4):
            for side in range(2):
                direct[i][side].wait_recv()
                piece = v["ext"].at[32 * side + 4 * x + i]
                handed.append(remote(piece, piece, chip(xr)))
                handed.append(remote(piece, piece, chip(xl)))
        for i, copy in enumerate(phis):
            copy.wait()
            high, low = split(v["phi"][i])
            v["phi_h"][i] = high
            v["phi_l"][i] = low
        cols_copy.wait_recv()
        other_cols = local(v["cols_in"], v["cols"].at[1])
        for copy in (own_cols, own_tiles, own_b, other_cols):
            copy.wait()
        for copy in [tiles_copy, *far_copies, *handed]:
            copy.wait_recv()
    first = (r - 1) * 16

    def product(row):
        lhs = jnp.concatenate(
            [v["tiles"][h, row, k] for h in range(2) for k in range(4)], axis=1
        )
        rhs = jnp.concatenate(
            [
                v["ext"][jnp.clip(v["cols"][h, k, row] - first, 0, 47)]
                for h in range(2)
                for k in range(4)
            ],
            axis=0,
        )
        return jnp.dot(lhs, rhs, preferred_element_type=F32)

    def coded(i, value, device):
        top = jnp.maximum(jnp.max(jnp.abs(value), axis=1, keepdims=True), 1e-30)
        v["code"][i] = jnp.round(value * (32767.0 / top)).astype(jnp.int32).astype(I16)
        v["unit"][i] = jnp.broadcast_to(top * (1 / 32767.0), (128, 128)).T[0:8]
        return (
            remote(v["code"].at[i], v["code_in"].at[i], device),
            remote(v["unit"].at[i], v["unit_in"].at[i], device),
        )

    def decoded(i, copies):
        for copy in copies:
            copy.wait_recv()
        unit = jnp.broadcast_to(v["unit_in"][i, 0:1], (128, 128)).T
        return v["code_in"][i].astype(jnp.int32).astype(F32) * jnp.concatenate([unit, unit], axis=1)

    with jax.named_scope("product"):
        up_far, down_far, up_near, down_near, up_sum, down_sum = ([] for _ in range(6))
        for j in range(2):
            up_far.append(coded(j, product(4 * opposite + j), chip(xr)))
            down_far.append(coded(2 + j, product(4 * opposite + 2 + j), chip(xl)))
        for j in range(2):
            down_near.append(coded(4 + j, product(4 * xr + 2 + j), chip(xr)))
            up_near.append(coded(6 + j, product(4 * xl + j), chip(xl)))
        for j in range(2):
            up_sum.append(coded(8 + j, product(4 * xr + j) + decoded(j, up_far[j]), chip(xr)))
            down_sum.append(
                coded(10 + j, product(4 * xl + 2 + j) + decoded(2 + j, down_far[j]), chip(xl))
            )
        for j in range(4):
            v["part"][j] = product(4 * x + j)
        for j in range(2):
            v["part"][j] = v["part"][j] + decoded(6 + j, up_near[j])
            v["part"][2 + j] = v["part"][2 + j] + decoded(4 + j, down_near[j])
        for j in range(2):
            rows = pl.ds(128 * j, 128)
            upper = v["part"][j] + decoded(8 + j, up_sum[j])
            lower = v["part"][2 + j] + decoded(10 + j, down_sum[j])
            v["swap"][rows] = jnp.where(c == 0, lower, upper)
            v["samp"][c, rows] = jnp.where(c == 0, upper, lower)
        swapped = remote(v["swap"], v["samp"].at[c], partner)
        swapped.wait_recv()
    def put(slot, value):
        high, low = split(value)
        v["a_h"][slot] = high
        v["a_l"][slot] = low

    def get(slot):
        return v["a_h"][slot], v["a_l"][slot]

    def phi_of(i):
        return v["phi_h"][i], v["phi_l"][i]

    def transposed():
        return v["t_h"][...], v["t_l"][...]

    def packed(gram):
        corner = jnp.concatenate([gram[128:192, 128:256], gram[192:256, 128:256]], axis=1)
        return jnp.concatenate([gram[0:128], corner], axis=0)

    def unpacked(rows):
        corner = jnp.concatenate([rows[128:192, 0:128], rows[128:192, 128:256]], axis=0)
        low = jnp.concatenate([rows[0:128, 128:256].T, corner], axis=1)
        return jnp.concatenate([rows[0:128], low], axis=0)

    def core_rows(size, core):
        return pl.ds(pl.multiple_of(core * size, size), size)

    def half_of(m):
        return 96 if m == 0 else 128

    def sum_core(m):
        size = half_of(m)
        rows = core_rows(size, 1 - c)
        return [remote(v["mine"].at[m, rows], v["in_core"].at[m, 0:size], partner)]

    def crossed(ref, into, m, one, two):
        size, cut = half_of(m), half_of(m) // 2
        return [
            remote(v[ref].at[m, 0:cut], v[into].at[m, 0:cut], chip(one)),
            remote(v[ref].at[m, cut:size], v[into].at[m, cut:size], chip(two)),
        ]

    def arrived(copies):
        for copy in copies:
            copy.wait_recv()

    def sum_first(m, copies):
        arrived(copies)
        size = half_of(m)
        v["chip"][m, 0:size] = v["mine"][m, core_rows(size, c)] + v["in_core"][m, 0:size]
        return crossed("chip", "in_chip", m, first_dim, second_dim)

    def sum_second(m, copies):
        arrived(copies)
        size = half_of(m)
        v["two"][m, 0:size] = v["chip"][m, 0:size] + v["in_chip"][m, 0:size]
        return crossed("two", "in_two", m, second_dim, first_dim)

    def sum_last(m, copies):
        arrived(copies)
        size = half_of(m)
        rows = core_rows(size, c)
        v["full"][m, rows] = v["two"][m, 0:size] + v["in_two"][m, 0:size]
        return [remote(v["full"].at[m, rows], v["full"].at[m, rows], partner)]

    with jax.named_scope("sums"):
        for half in range(2):
            put(half, v["samp"][half])
        sample = (
            jnp.concatenate([v["a_h"][0], v["a_h"][1]], axis=1),
            jnp.concatenate([v["a_l"][0], v["a_l"][1]], axis=1),
        )
        z = dot3(sample, phi_of(0))
        z_high, z_low = split(z)
        v["z_own"][0] = z_high
        v["z_own"][1] = z_low
        t_high, t_low = split(z.T)
        v["t_h"][...] = t_high
        v["t_l"][...] = t_low
        v["mine"][0, 0:192] = packed(dot3(transposed(), (v["z_own"][0], v["z_own"][1])))
        sum_g = sum_core(0)
        z_local = local(v["z_own"], z_at(s))
        for half in range(2):
            w = dot3(transposed(), get(half))
            put(3 + half, w)
            for q in range(4):
                v["wpart"][q // 2, 2 * half + q % 2] = w[
                    128 * (q // 2) : 128 * (q // 2) + 128, 128 * (q % 2) : 128 * (q % 2) + 128
                ]
        sum_g = sum_first(0, sum_g)
        w_all = (
            jnp.concatenate([v["a_h"][3], v["a_h"][4]], axis=1),
            jnp.concatenate([v["a_l"][3], v["a_l"][4]], axis=1),
        )
        v["mine"][1] = dot3(w_all, phi_of(1))
        sum_n = sum_core(1)
        v["mine"][2] = dot3(w_all, phi_of(2))
        sum_o = sum_core(2)
        w_core = remote(v["wpart"].at[1 - c], v["w_core"], partner)
        sum_n = sum_first(1, sum_n)
        sum_g = sum_second(0, sum_g)
        sum_o = sum_first(2, sum_o)
        sum_n = sum_second(1, sum_n)
        sum_o = sum_second(2, sum_o)
        sum_g = sum_last(0, sum_g)
        w_core.wait_recv()
        v["w_chip"][...] = v["wpart"][c] + v["w_core"][...]
        arrived(sum_g)
    eye = jnp.where(
        lax.broadcasted_iota(jnp.int32, (RANK, RANK), 0)
        == lax.broadcasted_iota(jnp.int32, (RANK, RANK), 1),
        F32(1.5),
        F32(0),
    )

    def inverse_root(level, gram, meanwhile):
        norm = (
            jnp.sqrt(
                jnp.sum(jnp.sum(gram * gram, axis=1, keepdims=True), axis=0, keepdims=True)
            )
            + 1e-06
        )
        y0 = gram / norm
        factor = split(eye - 0.5 * y0)
        new_high, new_low = split(dot3(split(y0), factor))
        v["yx_h"][0:256] = new_high
        v["yx_l"][0:256] = new_low
        v["yx_h"][256:512] = factor[0]
        v["yx_l"][256:512] = factor[1]

        def make_factor():
            both = dot3(
                (v["yx_h"][256:512], v["yx_l"][256:512]), (v["yx_h"][0:256], v["yx_l"][0:256])
            )
            high, low = split(eye - 0.5 * both)
            v["f_h"][...] = high
            v["f_l"][...] = low

        def step(_, carry):
            make_factor()
            high, low = split(
                dot3((v["yx_h"][...], v["yx_l"][...]), (v["f_h"][...], v["f_l"][...]))
            )
            v["yx_h"][...] = high
            v["yx_l"][...] = low
            return carry

        step(0, 0)
        passed_on = meanwhile()
        lax.fori_loop(0, NS_ITERS - 3, step, 0)
        make_factor()
        result = dot3((v["yx_h"][256:512], v["yx_l"][256:512]), (v["f_h"][...], v["f_l"][...]))
        high, low = split(result)
        v["x_h"][level] = high
        v["x_l"][level] = low
        return 1.0 / jnp.sqrt(norm), result, passed_on

    def root(level):
        return v["x_h"][level], v["x_l"][level]

    def exchange(i, device):
        size = 128 if i == 1 else 96
        rows = core_rows(size, c)
        return remote(v["swapped_pair"].at[i, rows], v["swapped_in"].at[i, 0:size], device)

    def exchange_core(i, copy):
        copy.wait_recv()
        size = 128 if i == 1 else 96
        rows = core_rows(size, c)
        v["swapped_sum"][i, rows] = v["swapped_pair"][i, rows] + v["swapped_in"][i, 0:size]
        return remote(v["swapped_sum"].at[i, rows], v["swapped_sum"].at[i, rows], partner)

    with jax.named_scope("leaf"):

        def last_sums():
            last_n, last_o = sum_last(1, sum_n), sum_last(2, sum_o)
            columns = [
                remote(v["w_chip"].at[d], v["w_in"].at[o], chip(d))
                for o, d in enumerate((xr, opposite, xl))
            ]
            return last_n, last_o, columns

        scale_leaf, x_leaf, (sum_n, sum_o, w_copies) = inverse_root(0, unpacked(v["full"][0, 0:192]), last_sums)
        arrived(sum_n)
        zp = dot3(root(0), split(v["full"][1])) * scale_leaf
        put(0, zp)
        t_high, t_low = split(zp.T)
        v["t_h"][...] = t_high
        v["t_l"][...] = t_low
        v["swapped_pair"][0, 0:192] = packed(dot3(transposed(), get(0)))
        gram_copy = exchange(0, sibling)
        z_right = remote(v["z_own"], z_at(s), chip(xr))
        z_left = remote(v["z_own"], z_at(s), chip(xl))
        z_partner = remote(v["z_own"], z_at(s), partner)
        arrived(sum_o)
        put(5, dot3(root(0), split(v["full"][2])) * scale_leaf)
        v["swapped_pair"][1] = dot3(transposed(), get(5))
        cross_copy = exchange(1, sibling)
        root_high, root_low = split(x_leaf * scale_leaf)
        v["root_v"][0] = root_high
        v["root_v"][1] = root_low
        root_copy = local(v["root_v"], root_hbm)
        gram_copy = exchange_core(0, gram_copy)
        arrived(w_copies)
        v["wcol"][c] = v["w_chip"][x] + v["w_in"][0] + v["w_in"][1] + v["w_in"][2]
        wcol_copy = remote(v["wcol"].at[c], v["wcol"].at[c], partner)
        wcol_copy.wait_recv()
        coarse = dot3(root(0), split(v["wcol"][...].reshape(256, 128))) * scale_leaf
        v["wc"][0] = dot3(transposed(), split(coarse))
        wc_copy = remote(v["wc"].at[0], v["wc_in"].at[0], sibling)
        gram_copy.wait_recv()
    with jax.named_scope("pair"):
        scale_pair, _, cross_copy = inverse_root(
            1, unpacked(v["swapped_sum"][0, 0:192]), lambda: exchange_core(1, cross_copy)
        )
        put(2, dot3(get(0), root(1)) * scale_pair)
        cross_copy.wait_recv()
        zq = dot3(root(1), split(v["swapped_sum"][1])) * scale_pair
        put(1, zq)
        t_high, t_low = split(zq.T)
        v["t_h"][...] = t_high
        v["t_l"][...] = t_low
        v["swapped_pair"][2, 0:192] = packed(dot3(transposed(), get(1)))
        gram_copy = exchange(2, cousin)
        put(4, dot3(get(2), get(1)))
        wc_copy.wait_recv()
        middle = dot3(root(1), split(v["wc"][0] + v["wc_in"][0])) * scale_pair
        v["wc"][1] = dot3(transposed(), split(middle))
        wc_copy = remote(v["wc"].at[1], v["wc_in"].at[1], cousin)
        z_right.wait_recv()
        from_left = 2 * xl + c
        round_right = remote(
            z_at(from_left, 0, 128), z_at(from_left, 0, 128), chip(xr)
        )
        z_left.wait_recv()
        from_right = 2 * xr + c
        round_left = remote(
            z_at(from_right, 128, 128), z_at(from_right, 128, 128), chip(xl)
        )
        handed_z = [
            remote(z_at(from_left), z_at(from_left), partner),
            remote(z_at(from_right), z_at(from_right), partner),
        ]
        gram_copy = exchange_core(2, gram_copy)
        gram_copy.wait_recv()
    with jax.named_scope("quad"):
        scale_quad, _, _ = inverse_root(2, unpacked(v["swapped_sum"][2, 0:192]), lambda: None)
        arrived([round_right, round_left])
        from_far = 2 * opposite + c
        handed_z.append(remote(z_at(from_far), z_at(from_far), partner))
        nested = dot3(get(4), root(2)) * scale_quad
        v["nested_v"][...] = nested
        nested_copy = local(v["nested_v"], nested_hbm)
        wc_copy.wait_recv()
        summary = dot3(root(2), split(v["wc"][1] + v["wc_in"][1])) * scale_quad
        inner = dot3(split(nested), split(summary))
        inner_high, inner_low = split(
            dot3((v["root_v"][0], v["root_v"][1]), split(inner))
        )
        v["xi_v"][0] = inner_high
        v["xi_v"][1] = inner_low
        inner_copy = local(v["xi_v"], inner_hbm)
        arrived([z_partner] + handed_z)
        for copy in (z_local, root_copy, nested_copy, inner_copy):
            copy.wait()
        assert len(sent) <= N_COPIES and len(locals_) <= 12
        for copy in sent:
            copy.wait_send()


def outputs(z_ref, root_ref, nested_ref, inner_ref, basis_out, nested_out, approx_out, turned):
    core = lax.rem(lax.axis_index("samp"), 2)
    z = z_ref[0], z_ref[1]
    basis_out[...] = dot3(z, (root_ref[0], root_ref[1]))
    turned[...] = dot3(z, (inner_ref[0], inner_ref[1])).T
    approx_out[...] = turned[pl.ds(pl.multiple_of(core * 64, 64), 64)]
    nested_out[...] = nested_ref[...]


def on_device(n_rows, coupling_tiles, tile_columns, sample_matrix, phi_leaf, phi_pair, phi_quad):
    rows = sample_matrix.shape[0]
    share = sample_matrix.shape[1] // SAMP
    any_ = pl.BlockSpec(memory_space=pl.ANY)
    z, root, nested, inner = pl.pallas_call(
        functools.partial(kernel, n_rows),
        out_shape=(
            jax.ShapeDtypeStruct((2, SAMP * RANK, RANK), BF16),
            jax.ShapeDtypeStruct((2, RANK, RANK), BF16),
            jax.ShapeDtypeStruct((RANK, RANK), F32),
            jax.ShapeDtypeStruct((2, RANK, 128), BF16),
        ),
        in_specs=[any_] * 6,
        out_specs=(any_,) * 4,
        scratch_shapes=list(SCRATCH.values()),
        compiler_params=pltpu.CompilerParams(
            collective_id=0, has_side_effects=True, vmem_limit_bytes=56 * 2**20
        ),
        name="hss",
    )(
        coupling_tiles,
        tile_columns.T,
        sample_matrix.reshape(16, 128, 512),
        phi_leaf,
        phi_pair,
        phi_quad,
    )
    basis, nested, approx_t = pl.pallas_call(
        outputs,
        grid=(SAMP // 4,),
        out_shape=(
            jax.ShapeDtypeStruct((rows, RANK), F32),
            jax.ShapeDtypeStruct((RANK, RANK), F32),
            jax.ShapeDtypeStruct((share, rows), F32),
        ),
        in_specs=[
            pl.BlockSpec((2, 4 * RANK, RANK), lambda i: (0, i, 0)),
            pl.BlockSpec((2, RANK, RANK), lambda i: (0, 0, 0)),
            pl.BlockSpec((RANK, RANK), lambda i: (0, 0)),
            pl.BlockSpec((2, RANK, 128), lambda i: (0, 0, 0)),
        ],
        out_specs=(
            pl.BlockSpec((4 * RANK, RANK), lambda i: (i, 0)),
            pl.BlockSpec((RANK, RANK), lambda i: (0, 0)),
            pl.BlockSpec((share, 4 * RANK), lambda i: (0, i)),
        ),
        scratch_shapes=[pltpu.VMEM((128, 4 * RANK), F32)],
        compiler_params=pltpu.CompilerParams(vmem_limit_bytes=56 * 2**20),
        name="expand",
    )(z, root, nested, inner)
    return basis, nested, approx_t.T


def solution(mesh):
    return jax.shard_map(
        functools.partial(on_device, mesh.shape["rows"]),
        mesh=mesh,
        in_specs=(P("rows", "samp", None, None), P("rows", "samp"), P("rows", None), P(), P(), P()),
        out_specs=(P("rows", None), P("rows", None), P("rows", "samp")),
        check_vma=False,
    )
```

```python
import functools

import jax
import jax.numpy as jnp
from jax import lax
from jax.experimental import pallas as pl
from jax.experimental.pallas import tpu as pltpu
from jax.sharding import PartitionSpec as P

NS_ITERS = 5
MESH = pl.DeviceIdType.MESH
F32 = jnp.float32
BF16 = jnp.bfloat16
NT, NN = ((1,), (1,)), ((1,), (0,))

N_COPIES = 112
SAMP = 8
CHIPS = 4
RANK = 256

I16 = jnp.int16

SCRATCH = dict(
    ext=pltpu.VMEM((48, 128, 256), BF16),
    tiles=pltpu.VMEM((2, 16, 4, 128, 128), BF16),
    cols_in=pltpu.VMEM((4, 16), jnp.int32),
    cols=pltpu.SMEM((2, 4, 16), jnp.int32),
    phi=pltpu.VMEM((3, 512, 256), F32),
    phi_h=pltpu.VMEM((3, 512, 256), BF16),
    phi_l=pltpu.VMEM((3, 512, 256), BF16),
    part=pltpu.VMEM((4, 128, 256), F32),
    code=pltpu.VMEM((12, 128, 256), I16),
    code_in=pltpu.VMEM((12, 128, 256), I16),
    unit=pltpu.VMEM((12, 8, 128), F32),
    unit_in=pltpu.VMEM((12, 8, 128), F32),
    swap=pltpu.VMEM((256, 256), F32),
    samp=pltpu.VMEM((2, 256, 256), F32),
    mine=pltpu.VMEM((3, 256, 256), F32),
    in_core=pltpu.VMEM((3, 128, 256), F32),
    chip=pltpu.VMEM((3, 128, 256), F32),
    in_chip=pltpu.VMEM((3, 128, 256), F32),
    two=pltpu.VMEM((3, 128, 256), F32),
    in_two=pltpu.VMEM((3, 128, 256), F32),
    full=pltpu.VMEM((3, 256, 256), F32),
    wpart=pltpu.VMEM((2, 4, 128, 128), F32),
    w_core=pltpu.VMEM((4, 128, 128), F32),
    w_chip=pltpu.VMEM((4, 128, 128), F32),
    w_in=pltpu.VMEM((3, 128, 128), F32),
    wcol=pltpu.VMEM((2, 128, 128), F32),
    z_own=pltpu.VMEM((2, 256, 256), BF16),
    yx_h=pltpu.VMEM((512, 256), BF16),
    yx_l=pltpu.VMEM((512, 256), BF16),
    f_h=pltpu.VMEM((256, 256), BF16),
    f_l=pltpu.VMEM((256, 256), BF16),
    x_h=pltpu.VMEM((3, 256, 256), BF16),
    x_l=pltpu.VMEM((3, 256, 256), BF16),
    a_h=pltpu.VMEM((6, 256, 256), BF16),
    a_l=pltpu.VMEM((6, 256, 256), BF16),
    t_h=pltpu.VMEM((256, 256), BF16),
    t_l=pltpu.VMEM((256, 256), BF16),
    swapped_pair=pltpu.VMEM((3, 256, 256), F32),
    swapped_in=pltpu.VMEM((3, 128, 256), F32),
    swapped_sum=pltpu.VMEM((3, 256, 256), F32),
    wc=pltpu.VMEM((2, 256, 128), F32),
    wc_in=pltpu.VMEM((2, 256, 128), F32),
    root_v=pltpu.VMEM((2, 256, 256), BF16),
    xi_v=pltpu.VMEM((2, 256, 128), BF16),
    nested_v=pltpu.VMEM((256, 256), F32),
    local=pltpu.SemaphoreType.DMA((12,)),
    send=pltpu.SemaphoreType.DMA((N_COPIES,)),
    recv=pltpu.SemaphoreType.DMA((N_COPIES,)),
)


def split(value):
    high = value.astype(BF16)
    return high, (value - high.astype(F32)).astype(BF16)


def dot3(a, b):
    left = jnp.concatenate([a[0], a[0], a[1]], axis=1)
    right = jnp.concatenate([b[0], b[1], b[0]], axis=0)
    return lax.dot_general(left, right, (NN, ((), ())), preferred_element_type=F32)


def dot3_nt(a, b):
    left = jnp.concatenate([a[0], a[0], a[1]], axis=1)
    right = jnp.concatenate([b[0], b[1], b[0]], axis=1)
    return lax.dot_general(left, right, (NT, ((), ())), preferred_element_type=F32)


def kernel(n_rows, *refs):
    tiles_hbm, cols_hbm, b_hbm, phi0_hbm, phi1_hbm, phi2_hbm = refs[:6]
    z_hbm, root_hbm, nested_hbm, inner_hbm = refs[6:10]
    v = dict(zip(SCRATCH, refs[10:]))

    r = lax.axis_index("rows")
    s = lax.axis_index("samp")
    x = lax.div(s, 2)
    c = lax.rem(s, 2)
    y = lax.rem(r, 4)
    xr, opposite, xl = (lax.rem(x + o, CHIPS) for o in (1, 2, 3))

    def chip(index):
        return (r, 2 * index + c)

    partner = (r, s + 1 - 2 * c)
    left = (lax.rem(r + n_rows - 1, n_rows), s)
    right = (lax.rem(r + 1, n_rows), s)
    sibling = (r + 1 - 2 * lax.rem(r, 2), s)
    cousin = (r + 3 - 2 * y, s)
    first_dim = x + 1 - 2 * lax.rem(x, 2)
    second_dim = 3 - x

    barrier = pltpu.get_barrier_semaphore()
    peers = [partner, chip(xr), chip(opposite), chip(xl), left, right, cousin]
    for peer in peers:
        pl.semaphore_signal(barrier, inc=1, device_id=peer, device_id_type=MESH)

    locals_ = []

    def local(src, dst):
        copy = pltpu.make_async_copy(src, dst, v["local"].at[len(locals_)])
        locals_.append(copy)
        copy.start()
        return copy

    sent = []

    def remote(src, dst, device):
        i = len(sent)
        copy = pltpu.make_async_remote_copy(
            src_ref=src,
            dst_ref=dst,
            send_sem=v["send"].at[i],
            recv_sem=v["recv"].at[i],
            device_id=device,
            device_id_type=MESH,
        )
        sent.append(copy)
        copy.start()
        return copy

    def z_at(origin, start=0, size=256):
        return z_hbm.at[:, pl.ds(pl.multiple_of(256 * origin + start, 128), size)]

    mine_half = pl.ds(pl.multiple_of(c * 256, 256), 256)
    own_cols = local(cols_hbm, v["cols"].at[0])
    pl.semaphore_wait(barrier, len(peers))
    with jax.named_scope("halo"):
        def to_both(at, count):
            piece = b_hbm.at[pl.ds(at, count), :, mine_half]
            return (
                remote(piece, v["ext"].at[pl.ds(at, count)], right),
                remote(piece, v["ext"].at[pl.ds(32 + at, count)], left),
            )

        direct = [to_both(4 * x + i, 1) for i in range(4)]
        cols_copy = remote(cols_hbm, v["cols_in"], partner)
        far_copies = to_both(4 * opposite, 4)
        tiles_copy = remote(tiles_hbm, v["tiles"].at[1], partner)
        own_tiles = local(tiles_hbm, v["tiles"].at[0])
        own_b = local(b_hbm.at[:, :, mine_half], v["ext"].at[pl.ds(16, 16)])
        phis = [local(p, v["phi"].at[i]) for i, p in enumerate((phi0_hbm, phi1_hbm, phi2_hbm))]
        handed = []
        for i in range(4):
            for side in range(2):
                direct[i][side].wait_recv()
                piece = v["ext"].at[32 * side + 4 * x + i]
                handed.append(remote(piece, piece, chip(xr)))
                handed.append(remote(piece, piece, chip(xl)))
        for i, copy in enumerate(phis):
            copy.wait()
            high, low = split(v["phi"][i])
            v["phi_h"][i] = high
            v["phi_l"][i] = low
        cols_copy.wait_recv()
        other_cols = local(v["cols_in"], v["cols"].at[1])
        for copy in (own_cols, own_tiles, own_b, other_cols):
            copy.wait()
        for copy in [tiles_copy, *far_copies, *handed]:
            copy.wait_recv()
    first = (r - 1) * 16

    def product(row):
        lhs = jnp.concatenate(
            [v["tiles"][h, row, k] for h in range(2) for k in range(4)], axis=1
        )
        rhs = jnp.concatenate(
            [
                v["ext"][jnp.clip(v["cols"][h, k, row] - first, 0, 47)]
                for h in range(2)
                for k in range(4)
            ],
            axis=0,
        )
        return jnp.dot(lhs, rhs, preferred_element_type=F32)

    def coded(i, value, device):
        top = jnp.maximum(jnp.max(jnp.abs(value), axis=1, keepdims=True), 1e-30)
        v["code"][i] = jnp.round(value * (32767.0 / top)).astype(jnp.int32).astype(I16)
        v["unit"][i] = jnp.broadcast_to(top * (1 / 32767.0), (128, 128)).T[0:8]
        return (
            remote(v["code"].at[i], v["code_in"].at[i], device),
            remote(v["unit"].at[i], v["unit_in"].at[i], device),
        )

    def decoded(i, copies):
        for copy in copies:
            copy.wait_recv()
        unit = jnp.broadcast_to(v["unit_in"][i, 0:1], (128, 128)).T
        return v["code_in"][i].astype(jnp.int32).astype(F32) * jnp.concatenate([unit, unit], axis=1)

    with jax.named_scope("product"):
        up_far, down_far, up_near, down_near, up_sum, down_sum = ([] for _ in range(6))
        for j in range(2):
            up_far.append(coded(j, product(4 * opposite + j), chip(xr)))
            down_far.append(coded(2 + j, product(4 * opposite + 2 + j), chip(xl)))
        for j in range(2):
            down_near.append(coded(4 + j, product(4 * xr + 2 + j), chip(xr)))
            up_near.append(coded(6 + j, product(4 * xl + j), chip(xl)))
        for j in range(2):
            up_sum.append(coded(8 + j, product(4 * xr + j) + decoded(j, up_far[j]), chip(xr)))
            down_sum.append(
                coded(10 + j, product(4 * xl + 2 + j) + decoded(2 + j, down_far[j]), chip(xl))
            )
        for j in range(4):
            v["part"][j] = product(4 * x + j)
        for j in range(2):
            v["part"][j] = v["part"][j] + decoded(6 + j, up_near[j])
            v["part"][2 + j] = v["part"][2 + j] + decoded(4 + j, down_near[j])
        for j in range(2):
            rows = pl.ds(128 * j, 128)
            upper = v["part"][j] + decoded(8 + j, up_sum[j])
            lower = v["part"][2 + j] + decoded(10 + j, down_sum[j])
            v["swap"][rows] = jnp.where(c == 0, lower, upper)
            v["samp"][c, rows] = jnp.where(c == 0, upper, lower)
        swapped = remote(v["swap"], v["samp"].at[c], partner)
        swapped.wait_recv()
    def put(slot, value):
        high, low = split(value)
        v["a_h"][slot] = high
        v["a_l"][slot] = low

    def get(slot):
        return v["a_h"][slot], v["a_l"][slot]

    def phi_of(i):
        return v["phi_h"][i], v["phi_l"][i]

    def transposed():
        return v["t_h"][...], v["t_l"][...]

    def packed(gram):
        corner = jnp.concatenate([gram[128:192, 128:256], gram[192:256, 128:256]], axis=1)
        return jnp.concatenate([gram[0:128], corner], axis=0)

    def unpacked(rows):
        corner = jnp.concatenate([rows[128:192, 0:128], rows[128:192, 128:256]], axis=0)
        low = jnp.concatenate([rows[0:128, 128:256].T, corner], axis=1)
        return jnp.concatenate([rows[0:128], low], axis=0)

    def core_rows(size, core):
        return pl.ds(pl.multiple_of(core * size, size), size)

    def half_of(m):
        return 96 if m == 0 else 128

    def sum_core(m):
        size = half_of(m)
        rows = core_rows(size, 1 - c)
        return [remote(v["mine"].at[m, rows], v["in_core"].at[m, 0:size], partner)]

    def crossed(ref, into, m, one, two):
        size, cut = half_of(m), half_of(m) // 2
        return [
            remote(v[ref].at[m, 0:cut], v[into].at[m, 0:cut], chip(one)),
            remote(v[ref].at[m, cut:size], v[into].at[m, cut:size], chip(two)),
        ]

    def arrived(copies):
        for copy in copies:
            copy.wait_recv()

    def sum_first(m, copies):
        arrived(copies)
        size = half_of(m)
        v["chip"][m, 0:size] = v["mine"][m, core_rows(size, c)] + v["in_core"][m, 0:size]
        return crossed("chip", "in_chip", m, first_dim, second_dim)

    def sum_second(m, copies):
        arrived(copies)
        size = half_of(m)
        v["two"][m, 0:size] = v["chip"][m, 0:size] + v["in_chip"][m, 0:size]
        return crossed("two", "in_two", m, second_dim, first_dim)

    def sum_last(m, copies):
        arrived(copies)
        size = half_of(m)
        rows = core_rows(size, c)
        v["full"][m, rows] = v["two"][m, 0:size] + v["in_two"][m, 0:size]
        return [remote(v["full"].at[m, rows], v["full"].at[m, rows], partner)]

    with jax.named_scope("sums"):
        for half in range(2):
            put(half, v["samp"][half])
        sample = (
            jnp.concatenate([v["a_h"][0], v["a_h"][1]], axis=1),
            jnp.concatenate([v["a_l"][0], v["a_l"][1]], axis=1),
        )
        z = dot3(sample, phi_of(0))
        z_high, z_low = split(z)
        v["z_own"][0] = z_high
        v["z_own"][1] = z_low
        t_high, t_low = split(z.T)
        v["t_h"][...] = t_high
        v["t_l"][...] = t_low
        v["mine"][0, 0:192] = packed(dot3(transposed(), (v["z_own"][0], v["z_own"][1])))
        sum_g = sum_core(0)
        z_local = local(v["z_own"], z_at(s))
        for half in range(2):
            w = dot3(transposed(), get(half))
            put(3 + half, w)
            for q in range(4):
                v["wpart"][q // 2, 2 * half + q % 2] = w[
                    128 * (q // 2) : 128 * (q // 2) + 128, 128 * (q % 2) : 128 * (q % 2) + 128
                ]
        sum_g = sum_first(0, sum_g)
        w_all = (
            jnp.concatenate([v["a_h"][3], v["a_h"][4]], axis=1),
            jnp.concatenate([v["a_l"][3], v["a_l"][4]], axis=1),
        )
        v["mine"][1] = dot3(w_all, phi_of(1))
        sum_n = sum_core(1)
        v["mine"][2] = dot3(w_all, phi_of(2))
        sum_o = sum_core(2)
        w_core = remote(v["wpart"].at[1 - c], v["w_core"], partner)
        sum_n = sum_first(1, sum_n)
        sum_g = sum_second(0, sum_g)
        sum_o = sum_first(2, sum_o)
        sum_n = sum_second(1, sum_n)
        sum_o = sum_second(2, sum_o)
        sum_g = sum_last(0, sum_g)
        w_core.wait_recv()
        v["w_chip"][...] = v["wpart"][c] + v["w_core"][...]
        arrived(sum_g)
    eye = jnp.where(
        lax.broadcasted_iota(jnp.int32, (RANK, RANK), 0)
        == lax.broadcasted_iota(jnp.int32, (RANK, RANK), 1),
        F32(1.5),
        F32(0),
    )

    def inverse_root(level, gram, meanwhile):
        norm = (
            jnp.sqrt(
                jnp.sum(jnp.sum(gram * gram, axis=1, keepdims=True), axis=0, keepdims=True)
            )
            + 1e-06
        )
        y0 = gram / norm
        factor = split(eye - 0.5 * y0)
        new_high, new_low = split(dot3(split(y0), factor))
        v["yx_h"][0:256] = new_high
        v["yx_l"][0:256] = new_low
        v["yx_h"][256:512] = factor[0]
        v["yx_l"][256:512] = factor[1]

        def make_factor():
            both = dot3(
                (v["yx_h"][256:512], v["yx_l"][256:512]), (v["yx_h"][0:256], v["yx_l"][0:256])
            )
            high, low = split(eye - 0.5 * both)
            v["f_h"][...] = high
            v["f_l"][...] = low

        def step(_, carry):
            make_factor()
            high, low = split(
                dot3((v["yx_h"][...], v["yx_l"][...]), (v["f_h"][...], v["f_l"][...]))
            )
            v["yx_h"][...] = high
            v["yx_l"][...] = low
            return carry

        step(0, 0)
        passed_on = meanwhile()
        lax.fori_loop(0, NS_ITERS - 3, step, 0)
        make_factor()
        result = dot3((v["yx_h"][256:512], v["yx_l"][256:512]), (v["f_h"][...], v["f_l"][...]))
        high, low = split(result)
        v["x_h"][level] = high
        v["x_l"][level] = low
        return 1.0 / jnp.sqrt(norm), result, passed_on

    def root(level):
        return v["x_h"][level], v["x_l"][level]

    def exchange(i, device):
        size = 128 if i == 1 else 96
        rows = core_rows(size, c)
        return remote(v["swapped_pair"].at[i, rows], v["swapped_in"].at[i, 0:size], device)

    def exchange_core(i, copy):
        copy.wait_recv()
        size = 128 if i == 1 else 96
        rows = core_rows(size, c)
        v["swapped_sum"][i, rows] = v["swapped_pair"][i, rows] + v["swapped_in"][i, 0:size]
        return remote(v["swapped_sum"].at[i, rows], v["swapped_sum"].at[i, rows], partner)

    with jax.named_scope("leaf"):

        def last_sums():
            last_n = sum_last(1, sum_n)
            columns = [
                remote(v["w_chip"].at[d], v["w_in"].at[o], chip(d))
                for o, d in enumerate((xr, opposite, xl))
            ]
            return last_n, columns

        scale_leaf, x_leaf, (sum_n, w_copies) = inverse_root(0, unpacked(v["full"][0, 0:192]), last_sums)
        arrived(sum_n)
        zp = dot3(root(0), split(v["full"][1])) * scale_leaf
        put(0, zp)
        t_high, t_low = split(zp.T)
        v["t_h"][...] = t_high
        v["t_l"][...] = t_low
        v["swapped_pair"][0, 0:192] = packed(dot3(transposed(), get(0)))
        gram_copy = exchange(0, sibling)
        sum_o = sum_last(2, sum_o)
        z_right = remote(v["z_own"], z_at(s), chip(xr))
        z_left = remote(v["z_own"], z_at(s), chip(xl))
        z_partner = remote(v["z_own"], z_at(s), partner)
        arrived(sum_o)
        put(5, dot3(root(0), split(v["full"][2])) * scale_leaf)
        v["swapped_pair"][1] = dot3(transposed(), get(5))
        cross_copy = exchange(1, sibling)
        root_high, root_low = split(x_leaf * scale_leaf)
        v["root_v"][0] = root_high
        v["root_v"][1] = root_low
        root_copy = local(v["root_v"], root_hbm)
        gram_copy = exchange_core(0, gram_copy)
        arrived(w_copies)
        v["wcol"][c] = v["w_chip"][x] + v["w_in"][0] + v["w_in"][1] + v["w_in"][2]
        wcol_copy = remote(v["wcol"].at[c], v["wcol"].at[c], partner)
        wcol_copy.wait_recv()
        coarse = dot3(root(0), split(v["wcol"][...].reshape(256, 128))) * scale_leaf
        v["wc"][0] = dot3(transposed(), split(coarse))
        wc_copy = remote(v["wc"].at[0], v["wc_in"].at[0], sibling)
        gram_copy.wait_recv()
    with jax.named_scope("pair"):
        scale_pair, _, cross_copy = inverse_root(
            1, unpacked(v["swapped_sum"][0, 0:192]), lambda: exchange_core(1, cross_copy)
        )
        put(2, dot3(get(0), root(1)) * scale_pair)
        cross_copy.wait_recv()
        zq = dot3(root(1), split(v["swapped_sum"][1])) * scale_pair
        put(1, zq)
        t_high, t_low = split(zq.T)
        v["t_h"][...] = t_high
        v["t_l"][...] = t_low
        v["swapped_pair"][2, 0:192] = packed(dot3(transposed(), get(1)))
        gram_copy = exchange(2, cousin)
        put(4, dot3(get(2), get(1)))
        wc_copy.wait_recv()
        middle = dot3(root(1), split(v["wc"][0] + v["wc_in"][0])) * scale_pair
        v["wc"][1] = dot3(transposed(), split(middle))
        wc_copy = remote(v["wc"].at[1], v["wc_in"].at[1], cousin)
        z_right.wait_recv()
        from_left = 2 * xl + c
        round_right = remote(
            z_at(from_left, 0, 128), z_at(from_left, 0, 128), chip(xr)
        )
        z_left.wait_recv()
        from_right = 2 * xr + c
        round_left = remote(
            z_at(from_right, 128, 128), z_at(from_right, 128, 128), chip(xl)
        )
        handed_z = [
            remote(z_at(from_left), z_at(from_left), partner),
            remote(z_at(from_right), z_at(from_right), partner),
        ]
        gram_copy = exchange_core(2, gram_copy)
        gram_copy.wait_recv()
    with jax.named_scope("quad"):
        scale_quad, _, _ = inverse_root(2, unpacked(v["swapped_sum"][2, 0:192]), lambda: None)
        arrived([round_right, round_left])
        from_far = 2 * opposite + c
        handed_z.append(remote(z_at(from_far), z_at(from_far), partner))
        nested = dot3(get(4), root(2)) * scale_quad
        v["nested_v"][...] = nested
        nested_copy = local(v["nested_v"], nested_hbm)
        wc_copy.wait_recv()
        summary = dot3(root(2), split(v["wc"][1] + v["wc_in"][1])) * scale_quad
        inner = dot3(split(nested), split(summary))
        inner_high, inner_low = split(
            dot3((v["root_v"][0], v["root_v"][1]), split(inner))
        )
        v["xi_v"][0] = inner_high
        v["xi_v"][1] = inner_low
        inner_copy = local(v["xi_v"], inner_hbm)
        arrived([z_partner] + handed_z)
        for copy in (z_local, root_copy, nested_copy, inner_copy):
            copy.wait()
        assert len(sent) <= N_COPIES and len(locals_) <= 12
        for copy in sent:
            copy.wait_send()


def outputs(z_ref, root_ref, nested_ref, inner_ref, basis_out, nested_out, approx_out, turned):
    core = lax.rem(lax.axis_index("samp"), 2)
    z = z_ref[0], z_ref[1]
    basis_out[...] = dot3(z, (root_ref[0], root_ref[1]))
    turned[...] = dot3(z, (inner_ref[0], inner_ref[1])).T
    approx_out[...] = turned[pl.ds(pl.multiple_of(core * 64, 64), 64)]
    nested_out[...] = nested_ref[...]


def on_device(n_rows, coupling_tiles, tile_columns, sample_matrix, phi_leaf, phi_pair, phi_quad):
    rows = sample_matrix.shape[0]
    share = sample_matrix.shape[1] // SAMP
    any_ = pl.BlockSpec(memory_space=pl.ANY)
    z, root, nested, inner = pl.pallas_call(
        functools.partial(kernel, n_rows),
        out_shape=(
            jax.ShapeDtypeStruct((2, SAMP * RANK, RANK), BF16),
            jax.ShapeDtypeStruct((2, RANK, RANK), BF16),
            jax.ShapeDtypeStruct((RANK, RANK), F32),
            jax.ShapeDtypeStruct((2, RANK, 128), BF16),
        ),
        in_specs=[any_] * 6,
        out_specs=(any_,) * 4,
        scratch_shapes=list(SCRATCH.values()),
        compiler_params=pltpu.CompilerParams(
            collective_id=0, has_side_effects=True, vmem_limit_bytes=56 * 2**20
        ),
        name="hss",
    )(
        coupling_tiles,
        tile_columns.T,
        sample_matrix.reshape(16, 128, 512),
        phi_leaf,
        phi_pair,
        phi_quad,
    )
    basis, nested, approx_t = pl.pallas_call(
        outputs,
        grid=(SAMP // 4,),
        out_shape=(
            jax.ShapeDtypeStruct((rows, RANK), F32),
            jax.ShapeDtypeStruct((RANK, RANK), F32),
            jax.ShapeDtypeStruct((share, rows), F32),
        ),
        in_specs=[
            pl.BlockSpec((2, 4 * RANK, RANK), lambda i: (0, i, 0)),
            pl.BlockSpec((2, RANK, RANK), lambda i: (0, 0, 0)),
            pl.BlockSpec((RANK, RANK), lambda i: (0, 0)),
            pl.BlockSpec((2, RANK, 128), lambda i: (0, 0, 0)),
        ],
        out_specs=(
            pl.BlockSpec((4 * RANK, RANK), lambda i: (i, 0)),
            pl.BlockSpec((RANK, RANK), lambda i: (0, 0)),
            pl.BlockSpec((share, 4 * RANK), lambda i: (0, i)),
        ),
        scratch_shapes=[pltpu.VMEM((128, 4 * RANK), F32)],
        compiler_params=pltpu.CompilerParams(vmem_limit_bytes=56 * 2**20),
        name="expand",
    )(z, root, nested, inner)
    return basis, nested, approx_t.T


def solution(mesh):
    return jax.shard_map(
        functools.partial(on_device, mesh.shape["rows"]),
        mesh=mesh,
        in_specs=(P("rows", "samp", None, None), P("rows", "samp"), P("rows", None), P(), P(), P()),
        out_specs=(P("rows", None), P("rows", None), P("rows", "samp")),
        check_vma=False,
    )
```
